128 devices in a mesh: replica: 2 (over z_lo), shard: 64 (over x, y, z_hi, core).
Axes of the slice: x: 4, y: 4, z: 4 (z_hi: 2, z_lo: 2; z = z_hi * 2 + z_lo), core: 2. Of those that a mesh axis runs over, the one named last changes fastest.
Arguments:
- tokens: bfloat16 [131072, 960], P(('replica', 'shard')), may hold values from -6 to 6
- cotangent: bfloat16 [131072, 960], P(('replica', 'shard')), may hold values from -6 to 6
- query_weight: bfloat16 [960, 960], P('shard'), may hold values from -1 to 1
- key_weight: bfloat16 [960, 320], P('shard'), may hold values from -1 to 1
- value_weight: bfloat16 [960, 320], P('shard'), may hold values from -0.1875 to 0.1875
- w_gate: bfloat16 [960, 2560], P('shard'), may hold values from -0.1875 to 0.1875
- w_up: bfloat16 [960, 2560], P('shard'), may hold values from -0.1875 to 0.1875
- output_weight: bfloat16 [960, 960], P(None, 'shard'), may hold values from -0.75 to 0.75
- w_down: bfloat16 [2560, 960], P(None, 'shard'), may hold values from -0.125 to 0.125
- norm_attn: bfloat16 [960], P('shard'), may hold values from 0.5 to 1.5
- norm_ffn: bfloat16 [960], P('shard'), may hold values from 0.5 to 1.5
Outputs:
- output: bfloat16 [131072, 960], P(('replica', 'shard'))
- grad_tokens: float32 [131072, 960], P(('replica', 'shard'))
- grad_query: float32 [960, 960], P('shard')
- grad_key: float32 [960, 320], P('shard')
- grad_value: float32 [960, 320], P('shard')
- grad_gate: float32 [960, 2560], P('shard')
- grad_up: float32 [960, 2560], P('shard')
- grad_out: float32 [960, 960], P(None, 'shard')
- grad_down: float32 [2560, 960], P(None, 'shard')
- grad_norm_attn: float32 [960], P('shard')
- grad_norm_ffn: float32 [960], P('shard')
The draws below stay inside these ranges and needn't reach their ends.
All inputs are finite; a program needn't handle non-finite values.
Results may differ from the reference program's by a relative error of at most 0.018.
The reference program's roundings to bfloat16 on the way count: a program that leaves them out, or rounds other values in their place, can miss the bound.
Values may be sent and summed in bfloat16 or wider, within the bound.
A program may use at most 256 MiB of HBM per device.

```python
import math
import jax
import jax.numpy as jnp
from jax import lax

MODEL_WIDTH = 960
HQ = 15
KEY_VALUE_HEADS = 5
HEAD_SIZE = 64
FF = 2560
SEQUENCE_TOKENS = 512
QUERY_PER_KEY = 3
TOKENS = 131072


def shared_direction(key):
    flips = jax.random.bernoulli(jax.random.fold_in(key, 11), 0.5, (MODEL_WIDTH,))
    return jnp.where(flips, 1.0, -1.0).astype(jnp.float32)


def sluggish_device_profile(key):
    half_dim = HEAD_SIZE // 2
    slow_pairs = HEAD_SIZE // 8
    dim_ids = jnp.arange(HEAD_SIZE)
    slow_mask = dim_ids % half_dim >= half_dim - slow_pairs
    magnitude = jax.random.uniform(jax.random.fold_in(key, 12), (HEAD_SIZE,), jnp.float32, 0.7, 1.3)
    flips = jax.random.bernoulli(jax.random.fold_in(key, 13), 0.5, (HEAD_SIZE,))
    signed = jnp.where(flips, 1.0, -1.0) * magnitude * (1.6 / math.sqrt(2.0 * slow_pairs))
    return jnp.where(slow_mask, signed, 0.0).astype(jnp.float32)


def draw_query_weight(key, part):
    rotary_base = jax.random.truncated_normal(jax.random.fold_in(key, 21), -6.0, 6.0, (MODEL_WIDTH, HQ * HEAD_SIZE), jnp.float32) / math.sqrt(MODEL_WIDTH)
    head_index_list = jnp.arange(HQ * HEAD_SIZE) // HEAD_SIZE
    factor = jnp.where(head_index_list < QUERY_PER_KEY, 1.0 - 0.2 * (head_index_list % QUERY_PER_KEY), 0.0)
    column_index = jnp.tile(sluggish_device_profile(key), HQ) * factor
    planted = (shared_direction(key) / math.sqrt(MODEL_WIDTH))[:, None] * column_index[None, :]
    return (rotary_base + planted).astype(jnp.bfloat16)


def draw_key_weight(key, part):
    rotary_base = jax.random.truncated_normal(jax.random.fold_in(key, 22), -6.0, 6.0, (MODEL_WIDTH, KEY_VALUE_HEADS * HEAD_SIZE), jnp.float32) / math.sqrt(MODEL_WIDTH)
    head_index_list = jnp.arange(KEY_VALUE_HEADS * HEAD_SIZE) // HEAD_SIZE
    column_index = jnp.where(head_index_list == 0, jnp.tile(sluggish_device_profile(key), KEY_VALUE_HEADS), 0.0)
    planted = (shared_direction(key) / math.sqrt(MODEL_WIDTH))[:, None] * column_index[None, :]
    return (rotary_base + planted).astype(jnp.bfloat16)


def draw_tokens(key, part):
    return jax.random.truncated_normal(jax.random.fold_in(key, 31), -6.0, 6.0, (TOKENS, MODEL_WIDTH), jnp.float32).astype(jnp.bfloat16)


def steps_of(stream_key, extent, pieces, least, high):
    loudness = 1.0
    for axis_at, parts in pieces:
        heights = jax.random.uniform(jax.random.fold_in(jax.random.fold_in(stream_key, 6), axis_at), (parts,), jnp.float32, least / len(pieces), high / len(pieces))
        loudness = loudness * jnp.repeat(jnp.exp(heights), extent[axis_at] // parts).reshape((-1,) + (1,) * (len(extent) - 1 - axis_at))
    return loudness


def scatter_about(key, dims, deviation, bound, pieces=(), kind=jnp.bfloat16):
    values = deviation * jax.random.normal(key, dims, jnp.float32)
    if pieces:
        values = values * steps_of(key, dims, pieces, -0.22, 0.18)
    return jnp.clip(values, -bound, bound).astype(kind)


def setup_inputs(seed: int = 0) -> dict:
    keys = jax.random.split(jax.random.key(seed), 12)
    tokens = draw_tokens(jax.random.fold_in(keys[11], 71), 0)
    cotangent = scatter_about(keys[1], (TOKENS, MODEL_WIDTH), 1.0, 6.0, ((0, 128),))
    query_weight = draw_query_weight(jax.random.fold_in(keys[11], 71), 0)
    key_weight = draw_key_weight(jax.random.fold_in(keys[11], 71), 0)
    value_weight = scatter_about(keys[4], (MODEL_WIDTH, KEY_VALUE_HEADS * HEAD_SIZE), MODEL_WIDTH ** -0.5, 0.1875, ((0, 64),))
    w_gate = scatter_about(keys[5], (MODEL_WIDTH, FF), MODEL_WIDTH ** -0.5, 0.1875, ((0, 64),))
    w_up = scatter_about(keys[6], (MODEL_WIDTH, FF), MODEL_WIDTH ** -0.5, 0.1875, ((0, 64),))
    output_weight = scatter_about(keys[7], (HQ * HEAD_SIZE, MODEL_WIDTH), (HQ * HEAD_SIZE // 16) ** -0.5, 0.75, ((1, 64),))
    w_down = scatter_about(keys[8], (FF, MODEL_WIDTH), FF ** -0.5, 0.125, ((1, 64),))
    norm_attn = jnp.clip(1.0 + 0.1 * jax.random.normal(keys[9], (MODEL_WIDTH,), jnp.float32), 0.5, 1.5).astype(jnp.bfloat16)
    norm_ffn = jnp.clip(1.0 + 0.1 * jax.random.normal(keys[10], (MODEL_WIDTH,), jnp.float32), 0.5, 1.5).astype(jnp.bfloat16)
    return dict(tokens=tokens, cotangent=cotangent, query_weight=query_weight, key_weight=key_weight, value_weight=value_weight, w_gate=w_gate, w_up=w_up, output_weight=output_weight, w_down=w_down, norm_attn=norm_attn, norm_ffn=norm_ffn)


EPSILON = 1e-05

def swap_half_pairs(values):
    middle = values.shape[-1] // 2
    return jnp.concatenate([-values[..., middle:], values[..., :middle]], axis=-1)

def rope_tables():
    half_dim = HEAD_SIZE // 2
    rates = jnp.exp(jnp.arange(half_dim, dtype=jnp.float32) * (-2.0 * math.log(10000.0) / HEAD_SIZE))
    angles = jnp.arange(SEQUENCE_TOKENS, dtype=jnp.float32)[:, None] * rates[None, :]
    angles = jnp.concatenate([angles, angles], axis=-1)
    return (jnp.cos(angles), jnp.sin(angles))

def causal_mask():
    row_ids = lax.broadcasted_iota(jnp.int32, (SEQUENCE_TOKENS, SEQUENCE_TOKENS), 0)
    col_ids = lax.broadcasted_iota(jnp.int32, (SEQUENCE_TOKENS, SEQUENCE_TOKENS), 1)
    return col_ids <= row_ids

def score_block(queries, key_block):
    scores = jnp.einsum('qkgd,tkd->kgqt', queries.astype(jnp.float32), key_block.astype(jnp.float32)) * (1.0 / math.sqrt(HEAD_SIZE))
    return jnp.where(causal_mask(), scores, -1e+30)

def attend_forward(packed_in):
    queries, key_block, values = packed_in
    scores = score_block(queries, key_block)
    row_top = lax.optimization_barrier(jnp.max(scores, axis=-1))
    log_total = row_top + jnp.log(lax.optimization_barrier(jnp.sum(jnp.exp(scores - row_top[..., None]), axis=-1)))
    soft_low = jnp.exp(scores - log_total[..., None]).astype(jnp.bfloat16)
    heads_out = jnp.einsum('kgqt,tkd->qkgd', soft_low.astype(jnp.float32), values.astype(jnp.float32)).astype(jnp.bfloat16)
    return (heads_out, log_total)

def attend_backward(packed_in):
    queries, key_block, values, heads_out, log_total, head_output_gradient = packed_in
    scores = score_block(queries, key_block)
    soft_full = jnp.exp(scores - log_total[..., None])
    soft_low = soft_full.astype(jnp.bfloat16)
    grad_heads_f = head_output_gradient.astype(jnp.float32)
    value_rows_gradient = jnp.einsum('kgqt,qkgd->tkd', soft_low.astype(jnp.float32), grad_heads_f)
    grad_soft = jnp.einsum('qkgd,tkd->kgqt', grad_heads_f, values.astype(jnp.float32))
    offset = jnp.transpose(lax.optimization_barrier(jnp.sum(grad_heads_f * heads_out.astype(jnp.float32), axis=-1)), (1, 2, 0))
    grad_scores = (soft_full * (grad_soft - offset[..., None])).astype(jnp.bfloat16).astype(jnp.float32)
    scale = 1.0 / math.sqrt(HEAD_SIZE)
    grad_queries = jnp.einsum('kgqt,tkd->qkgd', grad_scores, key_block.astype(jnp.float32)) * scale
    key_rows_gradient = jnp.einsum('kgqt,qkgd->tkd', grad_scores, queries.astype(jnp.float32)) * scale
    return (grad_queries, key_rows_gradient, value_rows_gradient)

def tdot(left, right):
    return jnp.dot(left.T, right, preferred_element_type=jnp.float32)

def contract_product(left, weight):
    return jnp.dot(left, weight.T, preferred_element_type=jnp.float32)

def forward(tokens, weights):
    query_weight, key_weight, value_weight, w_gate, w_up, output_weight, w_down, norm_attn, norm_ffn = weights
    count_of_rows = tokens.shape[0]
    sequence_count = count_of_rows // SEQUENCE_TOKENS
    inputs = tokens.astype(jnp.float32)
    recip_attn = lax.rsqrt(lax.optimization_barrier(jnp.mean(inputs * inputs, axis=-1, keepdims=True)) + EPSILON)
    attention_normalized = (inputs * recip_attn * norm_attn.astype(jnp.float32)).astype(jnp.bfloat16)
    cosine_table, sine_table = rope_tables()
    rotated_query = jnp.dot(attention_normalized, query_weight, preferred_element_type=jnp.float32).reshape(sequence_count, SEQUENCE_TOKENS, KEY_VALUE_HEADS, QUERY_PER_KEY, HEAD_SIZE)
    rotated_query = (rotated_query * cosine_table[:, None, None, :] + swap_half_pairs(rotated_query) * sine_table[:, None, None, :]).astype(jnp.bfloat16)
    rotated_key = jnp.dot(attention_normalized, key_weight, preferred_element_type=jnp.float32).reshape(sequence_count, SEQUENCE_TOKENS, KEY_VALUE_HEADS, HEAD_SIZE)
    rotated_key = (rotated_key * cosine_table[:, None, :] + swap_half_pairs(rotated_key) * sine_table[:, None, :]).astype(jnp.bfloat16)
    value_per_head = jnp.dot(attention_normalized, value_weight, preferred_element_type=jnp.float32).astype(jnp.bfloat16).reshape(sequence_count, SEQUENCE_TOKENS, KEY_VALUE_HEADS, HEAD_SIZE)
    heads_out, log_total = lax.map(attend_forward, (rotated_query, rotated_key, value_per_head))
    attended = heads_out.reshape(count_of_rows, HQ * HEAD_SIZE)
    hidden = inputs + jnp.dot(attended, output_weight, preferred_element_type=jnp.float32)
    recip_ffn = lax.rsqrt(lax.optimization_barrier(jnp.mean(hidden * hidden, axis=-1, keepdims=True)) + EPSILON)
    normed_ffn = (hidden * recip_ffn * norm_ffn.astype(jnp.float32)).astype(jnp.bfloat16)
    gate_pre = jnp.dot(normed_ffn, w_gate, preferred_element_type=jnp.float32)
    upward = jnp.dot(normed_ffn, w_up, preferred_element_type=jnp.float32)
    sigmoid_gate = jax.nn.sigmoid(gate_pre)
    activated = (gate_pre * sigmoid_gate * upward).astype(jnp.bfloat16)
    output = (hidden + jnp.dot(activated, w_down, preferred_element_type=jnp.float32)).astype(jnp.bfloat16)
    saved = (inputs, recip_attn, attention_normalized, rotated_query, rotated_key, value_per_head, heads_out, log_total, hidden, recip_ffn, normed_ffn, gate_pre, upward, sigmoid_gate, activated)
    return (output, saved)

def backward(saved, cotangent, weights):
    query_weight, key_weight, value_weight, w_gate, w_up, output_weight, w_down, norm_attn, norm_ffn = weights
    inputs, recip_attn, attention_normalized, rotated_query, rotated_key, value_per_head, heads_out, log_total, hidden, recip_ffn, normed_ffn, gate_pre, upward, sigmoid_gate, activated = saved
    count_of_rows = inputs.shape[0]
    sequence_count = count_of_rows // SEQUENCE_TOKENS
    cosine_table, sine_table = rope_tables()
    grad_w_down = tdot(activated, cotangent)
    grad_act = contract_product(cotangent, w_down)
    gate_slope = sigmoid_gate * (1.0 + gate_pre * (1.0 - sigmoid_gate))
    grad_gate_low = (grad_act * upward * gate_slope).astype(jnp.bfloat16)
    grad_upward_low = (grad_act * gate_pre * sigmoid_gate).astype(jnp.bfloat16)
    grad_w_gate = tdot(normed_ffn, grad_gate_low)
    grad_w_up = tdot(normed_ffn, grad_upward_low)
    grad_normed = contract_product(grad_gate_low, w_gate) + contract_product(grad_upward_low, w_up)
    grad_norm_ffn = lax.optimization_barrier(jnp.sum(grad_normed * hidden * recip_ffn, axis=0))
    scaled = grad_normed * norm_ffn.astype(jnp.float32)
    grad_hidden = cotangent.astype(jnp.float32) + recip_ffn * scaled - hidden * recip_ffn ** 3 * lax.optimization_barrier(jnp.mean(scaled * hidden, axis=-1, keepdims=True))
    hidden_gradient_narrow = grad_hidden.astype(jnp.bfloat16)
    attended = heads_out.reshape(count_of_rows, HQ * HEAD_SIZE)
    grad_w_out = tdot(attended, hidden_gradient_narrow)
    head_output_gradient = contract_product(hidden_gradient_narrow, output_weight).astype(jnp.bfloat16).reshape(sequence_count, SEQUENCE_TOKENS, KEY_VALUE_HEADS, QUERY_PER_KEY, HEAD_SIZE)
    grad_queries, key_rows_gradient, value_rows_gradient = lax.map(attend_backward, (rotated_query, rotated_key, value_per_head, heads_out, log_total, head_output_gradient))
    grad_queries = (grad_queries * cosine_table[:, None, None, :] - swap_half_pairs(grad_queries) * sine_table[:, None, None, :]).astype(jnp.bfloat16).reshape(count_of_rows, HQ * HEAD_SIZE)
    key_rows_gradient = (key_rows_gradient * cosine_table[:, None, :] - swap_half_pairs(key_rows_gradient) * sine_table[:, None, :]).astype(jnp.bfloat16).reshape(count_of_rows, KEY_VALUE_HEADS * HEAD_SIZE)
    value_rows_gradient = value_rows_gradient.astype(jnp.bfloat16).reshape(count_of_rows, KEY_VALUE_HEADS * HEAD_SIZE)
    grad_w_query = tdot(attention_normalized, grad_queries)
    grad_w_key = tdot(attention_normalized, key_rows_gradient)
    grad_w_value = tdot(attention_normalized, value_rows_gradient)
    grad_normed_attn = contract_product(grad_queries, query_weight) + contract_product(key_rows_gradient, key_weight) + contract_product(value_rows_gradient, value_weight)
    grad_norm_attn = lax.optimization_barrier(jnp.sum(grad_normed_attn * inputs * recip_attn, axis=0))
    scaled_attn = grad_normed_attn * norm_attn.astype(jnp.float32)
    grad_tokens = grad_hidden + recip_attn * scaled_attn - inputs * recip_attn ** 3 * lax.optimization_barrier(jnp.mean(scaled_attn * inputs, axis=-1, keepdims=True))
    grads = (grad_w_query, grad_w_key, grad_w_value, grad_w_gate, grad_w_up, grad_w_out, grad_w_down, grad_norm_attn, grad_norm_ffn)
    return (grad_tokens, grads)

def reference(tokens, cotangent, query_weight, key_weight, value_weight, w_gate, w_up, output_weight, w_down, norm_attn, norm_ffn):
    weights = (query_weight, key_weight, value_weight, w_gate, w_up, output_weight, w_down, norm_attn, norm_ffn)
    sequence_count = tokens.shape[0] // SEQUENCE_TOKENS
    token_seqs = tokens.reshape(sequence_count, SEQUENCE_TOKENS, MODEL_WIDTH)
    cotangent_seqs = cotangent.reshape(sequence_count, SEQUENCE_TOKENS, MODEL_WIDTH)

    def seq_step(acc_total, packed_in):
        seq_tokens, seq_cotangent = packed_in
        output, saved = forward(seq_tokens, weights)
        grad_tokens, grads = backward(saved, seq_cotangent, weights)
        acc_total = tuple((left + right for left, right in zip(acc_total, grads)))
        return (acc_total, (output, grad_tokens))
    zeros = tuple((jnp.zeros(weight.shape, jnp.float32) for weight in weights))
    acc_total, (outputs, grad_inputs) = lax.scan(seq_step, zeros, (token_seqs, cotangent_seqs))
    return (outputs.reshape(tokens.shape[0], MODEL_WIDTH), grad_inputs.reshape(tokens.shape[0], MODEL_WIDTH), acc_total[0], acc_total[1], acc_total[2], acc_total[3], acc_total[4], acc_total[5], acc_total[6], acc_total[7], acc_total[8])
```

```python
import functools
import math

import jax
import jax.numpy as jnp
import numpy as np
from jax import lax
from jax.experimental import pallas as pl
from jax.experimental.pallas import tpu as pltpu
from jax.sharding import PartitionSpec as P

F32, BF16 = jnp.float32, jnp.bfloat16
MESH = pl.DeviceIdType.MESH
ANY = pl.BlockSpec(memory_space=pl.ANY)
VMEM = pl.BlockSpec(memory_space=pltpu.VMEM)
WIDTH = 960
D = 1024
T = 1024
SEQ = 512
NA, NB, NC, BLOCKS, FB = 1664, 1024, 1536, 5, 512
EPS = 1e-05
SCALE = 0.125
LOG2E = math.log2(math.e)
VLIM = 60 * 1024 * 1024


def dot(a, b):
    return lax.dot_general(a, b, (((1,), (0,)), ((), ())), preferred_element_type=F32)


def dot_nt(a, b):
    return lax.dot_general(a, b, (((1,), (1,)), ((), ())), preferred_element_type=F32)


def dot_tn(a, b):
    return lax.dot_general(a, b, (((0,), (0,)), ((), ())), preferred_element_type=F32)


def span(i, n):
    return pl.ds(pl.multiple_of(i * n, n), n)


def rope_tables():
    rates = np.exp(np.arange(32) * (-2.0 * math.log(10000.0) / 64))
    angles = np.arange(SEQ)[:, None] * rates[None, :]
    cos, sin = np.cos(angles), np.sin(angles)
    cosine = np.concatenate([cos] * 4, axis=1).astype(np.float32)
    sine = np.concatenate([-sin, sin] * 2, axis=1).astype(np.float32)
    return cosine, sine


def swapped(t):
    lane = lax.broadcasted_iota(jnp.int32, t.shape, 1)
    return jnp.where((lane & 63) < 32, pltpu.roll(t, 96, 1), pltpu.roll(t, 32, 1))


def low_half(shape):
    return lax.broadcasted_iota(jnp.int32, shape, 1) < 64


def spread_matrix():
    row = lax.broadcasted_iota(jnp.int32, (WIDTH, D), 0)
    col = lax.broadcasted_iota(jnp.int32, (WIDTH, D), 1)
    hit = (row == 15 * (col >> 4) + (col & 15)) & ((col & 15) < 15)
    return jnp.where(hit, 1.0, 0.0).astype(BF16)


def place():
    r, s = lax.axis_index("replica"), lax.axis_index("shard")
    return s // 16, (s // 4) % 4, ((s // 2) % 2) * 2 + r, s % 2


def device(x, y, z, c):
    return (z % 2, ((x * 4 + y) * 2 + z // 2) * 2 + c)


def peers():
    x, y, z, c = place()
    xs = [device((x + d) % 4, y, z, c) for d in (1, 2, 3)]
    ys = [device(x, (y + d) % 4, z, c) for d in (1, 2, 3)]
    return xs, ys, device(x, y, 3 - z, c), device(x, y, z + 1 - 2 * (z % 2), c), device(x, y, z, 1 - c)


def meet():
    xs, ys, zp, zr, cp = peers()
    barrier = pltpu.get_barrier_semaphore()
    for d in (*xs, *ys, zp, zr, cp):
        pl.semaphore_signal(barrier, inc=1, device_id=d, device_id_type=MESH)
    pl.semaphore_wait(barrier, 9)


def remote(src, dst, ss, rs, k, to):
    return pltpu.make_async_remote_copy(
        src_ref=src, dst_ref=dst, send_sem=ss.at[k], recv_sem=rs.at[k], device_id=to, device_id_type=MESH
    )


GATHER_SEMS = 14


class Gather:
    def __init__(self, own, full, ss, rs, n):
        x, y, z, c = place()
        zh = z // 2
        xs, ys, zp, zr, cp = peers()
        half = (n // 256) * 128
        h1, h2 = pl.ds(0, half), pl.ds(half, n - half)
        mine = full.at[x, y, zh, c]
        self.local = pltpu.make_async_copy(own, mine, ss.at[0])
        self.z = [remote(own, mine, ss, rs, 1, zp)]
        a, b = full.at[x, y, :, c, :, h1], full.at[x, y, :, c, :, h2]
        self.one = [remote(a, a, ss, rs, 2 + i, ys[i]) for i in range(3)]
        self.one += [remote(b, b, ss, rs, 5 + i, xs[i]) for i in range(3)]
        a, b = full.at[x, :, :, c, :, h1], full.at[:, y, :, c, :, h2]
        self.two = [remote(a, a, ss, rs, 8 + i, xs[i]) for i in range(3)]
        self.two += [remote(b, b, ss, rs, 11 + i, ys[i]) for i in range(3)]
        w = full.at[:, :, :, c]
        self.core = [remote(w, w, ss, rs, 14, cp)]
        self.steps = [self.s0, self.s1, self.s2, self.s3, self.s4]

    def s0(self):
        self.local.start()
        self.z[0].start()

    def move(self, done, begin):
        for d in done:
            d.wait()
        for d in begin:
            d.start()

    def s1(self):
        self.local.wait()
        self.move(self.z, self.one)

    def s2(self):
        self.move(self.one, self.two)

    def s3(self):
        self.move(self.two, self.core)

    def s4(self):
        self.move(self.core, [])


def gather_sems():
    return [pltpu.SemaphoreType.DMA((GATHER_SEMS + 1,)), pltpu.SemaphoreType.DMA((GATHER_SEMS + 1,))]


SCATTER_SEMS = 16


def scatter_scratch(n):
    half = (n // 256) * 128
    rest = n - half
    return [
        pltpu.VMEM((4, 4, 2, 16, n), BF16),
        pltpu.VMEM((4, 4, 2, 16, n), BF16),
        pltpu.VMEM((3, 4, 2, 16, half), BF16),
        pltpu.VMEM((3, 4, 2, 16, rest), BF16),
        pltpu.VMEM((4, 2, 16, half), F32),
        pltpu.VMEM((4, 2, 16, rest), F32),
        pltpu.VMEM((3, 2, 16, half), F32),
        pltpu.VMEM((3, 2, 16, rest), F32),
        pltpu.VMEM((2, 16, n), F32),
        pltpu.VMEM((16, n), F32),
        pltpu.VMEM((16, n), F32),
        pltpu.VMEM((16, n), F32),
        pltpu.SemaphoreType.DMA((SCATTER_SEMS,)),
        pltpu.SemaphoreType.DMA((SCATTER_SEMS,)),
    ]


class Scatter:
    def __init__(self, part, out, scratch, n):
        x, y, z, c = place()
        self.zh = zh = z // 2
        self.x, self.y = x, y
        xs, ys, zp, zr, cp = peers()
        half = (n // 256) * 128
        self.half, self.n, self.out = half, n, out
        (self.p1, self.r0, self.r1a, self.r1b, self.p2a, self.p2b, self.r2a, self.r2b, self.p3, self.r3, self.p4, self.r4, ss, rs) = scratch
        h1, h2 = pl.ds(0, half), pl.ds(half, n - half)
        self.local = pltpu.make_async_copy(part.at[:, :, :, c], self.p1, ss.at[0])
        self.core = [remote(part.at[:, :, :, 1 - c], self.r0, ss, rs, 1, cp)]
        self.one = [remote(self.p1.at[(x + 1 + i) % 4, :, :, :, h1], self.r1a.at[i], ss, rs, 2 + i, xs[i]) for i in range(3)]
        self.one += [remote(self.p1.at[:, (y + 1 + i) % 4, :, :, h2], self.r1b.at[i], ss, rs, 5 + i, ys[i]) for i in range(3)]
        self.two = [remote(self.p2a.at[(y + 1 + i) % 4], self.r2a.at[i], ss, rs, 8 + i, ys[i]) for i in range(3)]
        self.two += [remote(self.p2b.at[(x + 1 + i) % 4], self.r2b.at[i], ss, rs, 11 + i, xs[i]) for i in range(3)]
        self.z = [remote(self.p3.at[1 - zh], self.r3, ss, rs, 14, zp)]
        self.rep = [remote(self.p4, self.r4, ss, rs, 15, zr)]
        self.steps = [self.s0, self.s1, self.s2, self.s3, self.s4, self.s5]

    def s0(self):
        self.local.start()
        self.core[0].start()

    def s1(self):
        self.local.wait()
        self.core[0].wait()

        def add(i, _):
            a, b = i // 4, i % 4
            self.p1[a, b] = (self.p1[a, b].astype(F32) + self.r0[a, b].astype(F32)).astype(BF16)
            return 0

        lax.fori_loop(0, 16, add, 0)
        for d in self.one:
            d.start()

    def s2(self):
        for d in self.one:
            d.wait()
        half = self.half

        def add(i, _):
            a = self.p1[self.x, i, :, :, :half].astype(F32)
            b = self.p1[i, self.y, :, :, half:].astype(F32)
            for k in range(3):
                a += self.r1a[k, i].astype(F32)
                b += self.r1b[k, i].astype(F32)
            self.p2a[i] = a
            self.p2b[i] = b
            return 0

        lax.fori_loop(0, 4, add, 0)
        for d in self.two:
            d.start()

    def s3(self):
        for d in self.two:
            d.wait()
        half = self.half

        def add(i, _):
            a, b = self.p2a[self.y, i], self.p2b[self.x, i]
            for k in range(3):
                a += self.r2a[k, i]
                b += self.r2b[k, i]
            self.p3[i, :, :half] = a
            self.p3[i, :, half:] = b
            return 0

        lax.fori_loop(0, 2, add, 0)
        self.z[0].start()

    def s4(self):
        self.z[0].wait()
        self.p4[...] = self.p3[self.zh] + self.r3[...]
        self.rep[0].start()

    def s5(self):
        self.rep[0].wait()
        self.out[...] = self.p4[...] + self.r4[...]


def gather_kernel(a, b, c, fa, fb, fc, *sems):
    meet()
    chunks = [Gather(a, fa, sems[0], sems[1], NA), Gather(b, fb, sems[2], sems[3], NB)]
    chunks += [Gather(c.at[i], fc.at[i], sems[4 + 2 * i], sems[5 + 2 * i], NC) for i in range(BLOCKS)]
    for k in range(5):
        for ch in chunks:
            ch.steps[k]()


def gather_all(a, b, c):
    return pl.pallas_call(
        gather_kernel,
        out_shape=[
            jax.ShapeDtypeStruct((4, 4, 2, 2, 16, NA), BF16),
            jax.ShapeDtypeStruct((4, 4, 2, 2, 16, NB), BF16),
            jax.ShapeDtypeStruct((BLOCKS, 4, 4, 2, 2, 16, NC), BF16),
        ],
        in_specs=[ANY] * 3,
        out_specs=[ANY] * 3,
        scratch_shapes=gather_sems() * 7,
        compiler_params=pltpu.CompilerParams(collective_id=0, has_side_effects=True),
        name="gather_all",
    )(a, b, c)


def scatter_kernel(ga, gb, gc, oa, ob, oc, *scratch):
    meet()
    k = 14
    chunks = [Scatter(gc.at[i], oc.at[i], scratch[k * i : k * i + k], NC) for i in range(BLOCKS)]
    chunks.append(Scatter(gb, ob, scratch[5 * k : 6 * k], NB))
    chunks.append(Scatter(ga, oa, scratch[6 * k : 7 * k], NA))
    for k in range(6):
        for ch in chunks:
            ch.steps[k]()


def scatter_all(ga, gb, gc):
    scratch = []
    for _ in range(BLOCKS):
        scratch += scatter_scratch(NC)
    scratch += scatter_scratch(NB) + scatter_scratch(NA)
    return pl.pallas_call(
        scatter_kernel,
        out_shape=[
            jax.ShapeDtypeStruct((16, NA), F32),
            jax.ShapeDtypeStruct((16, NB), F32),
            jax.ShapeDtypeStruct((BLOCKS, 16, NC), F32),
        ],
        in_specs=[ANY] * 3,
        out_specs=[VMEM] * 3,
        scratch_shapes=scratch,
        compiler_params=pltpu.CompilerParams(collective_id=1, has_side_effects=True, vmem_limit_bytes=VLIM),
        name="scatter_all",
    )(ga, gb, gc)


def gain_row(a_ref, lane):
    tile = a_ref[:, NA - 128 :].astype(F32)
    return jnp.transpose(tile)[lane : lane + 1, :]


def attend_kernel(tok, cot, a_ref, cos_ref, sin_ref, xp_ref, cp_ref, nrm_ref, nt_ref, qt_ref, ho_ref, lt_ref, spread, kx, vx, lse):
    spread[...] = spread_matrix()
    gain = gain_row(a_ref, 64)

    def project(i, _):
        r = span(i, 256)
        x = dot(tok[r, :], spread[...])
        xp_ref[r, :] = x.astype(BF16)
        cp_ref[r, :] = dot(cot[r, :], spread[...]).astype(BF16)
        recip = lax.rsqrt(jnp.sum(x * x, axis=1, keepdims=True) * (1.0 / WIDTH) + EPS)
        normed = (x * recip * gain).astype(BF16)
        nrm_ref[r, :] = normed
        half = span(i % 2, 256)
        cosine, sine = cos_ref[half, :], sin_ref[half, :]
        for t in range(13):
            q = dot(normed, a_ref[:, 128 * t : 128 * t + 128])
            if t < 10:
                q = q * cosine + swapped(q) * sine
            qt_ref[t, r, :] = q.astype(BF16)
        return 0

    lax.fori_loop(0, 4, project, 0)
    for i in range(4):
        nt_ref[:, 256 * i : 256 * i + 256] = jnp.transpose(nrm_ref[256 * i : 256 * i + 256, :])
    split_heads(qt_ref, kx, vx)
    ho_ref[...] = jnp.zeros_like(ho_ref)
    lse[...] = jnp.zeros_like(lse)

    def head(i, _):
        s = i // 15
        h = i - 15 * s
        p, g = h // 2, h // 3
        u = 2 * g + h - 2 * p
        for b in range(2):
            nk = 256 * (b + 1)
            rows = pl.ds(pl.multiple_of(s * SEQ + 256 * b, 256), 256)
            keys = pl.ds(pl.multiple_of(s * SEQ, SEQ), nk)
            sc = dot_nt(qt_ref[p, rows, :], kx[u, keys, :])
            row = lax.broadcasted_iota(jnp.int32, (256, nk), 0) + 256 * b
            col = lax.broadcasted_iota(jnp.int32, (256, nk), 1)
            sc = jnp.where(col <= row, sc, -1e30)
            top = jnp.max(sc, axis=1, keepdims=True)
            e = jnp.exp2((sc - top) * (SCALE * LOG2E))
            total = jnp.sum(e, axis=1, keepdims=True)
            soft = (e * (1.0 / total)).astype(BF16)
            o = dot(soft, vx[u, keys, :])
            ho_ref[p, rows, :] = ho_ref[p, rows, :] + o.astype(BF16)
            lane = lax.broadcasted_iota(jnp.int32, (256, 128), 1)
            stat = top * (SCALE * LOG2E) + jnp.log2(total)
            lse[rows, :] = jnp.where(lane == h, stat, lse[rows, :])
        return 0

    lax.fori_loop(0, 30, head, 0)
    lt_ref[...] = jnp.transpose(lse[...])[:16, :].reshape(16, 1, T)


def split_heads(qt_ref, kx, vx):
    low = low_half((T, 128))
    for g in range(5):
        for to, unit in ((kx, 15 + g), (vx, 20 + g)):
            tile = qt_ref[unit // 2].astype(F32)
            turned = pltpu.roll(tile, 64, 1)
            at_low, at_high = (tile, turned) if unit % 2 == 0 else (turned, tile)
            to[2 * g] = jnp.where(low, at_low, 0.0).astype(BF16)
            to[2 * g + 1] = jnp.where(low, 0.0, at_high).astype(BF16)


def attend(tok, cot, a_full, cosine, sine):
    shape = jax.ShapeDtypeStruct
    return pl.pallas_call(
        attend_kernel,
        out_shape=[
            shape((T, D), BF16),
            shape((T, D), BF16),
            shape((T, D), BF16),
            shape((D, T), BF16),
            shape((13, T, 128), BF16),
            shape((8, T, 128), BF16),
            shape((16, 1, T), F32),
        ],
        in_specs=[VMEM] * 5,
        out_specs=[VMEM] * 7,
        scratch_shapes=[
            pltpu.VMEM((WIDTH, D), BF16),
            pltpu.VMEM((10, T, 128), BF16),
            pltpu.VMEM((10, T, 128), BF16),
            pltpu.VMEM((T, 128), F32),
        ],
        compiler_params=pltpu.CompilerParams(vmem_limit_bytes=VLIM),
        name="attend",
    )(tok, cot, a_full, cosine, sine)


def ffn_kernel(xp, cp, a_ref, b_ref, ho, c_hbm, out_ref, gh_ref, gheads_ref, gb_ref, gc_hbm, gnorm_ref,
               hid, acc, gacc, nrm, nt, ct, w, act, gg, gu, stage, wsem, gsem):
    gain = gain_row(a_ref, 65)
    fetch = [pltpu.make_async_copy(c_hbm.at[b], w.at[b % 2], wsem.at[b % 2]) for b in range(BLOCKS)]
    fetch[0].start()

    def first(i, _):
        r = span(i, 256)
        h = xp[r, :].astype(F32)
        for p in range(8):
            h += dot_nt(ho[p, r, :], b_ref[:, 128 * p : 128 * p + 128])
        hid[r, :] = h
        acc[r, :] = h
        recip = lax.rsqrt(jnp.sum(h * h, axis=1, keepdims=True) * (1.0 / WIDTH) + EPS)
        nrm[r, :] = (h * recip * gain).astype(BF16)
        gacc[r, :] = jnp.zeros((256, D), F32)
        return 0

    lax.fori_loop(0, 4, first, 0)
    for i in range(4):
        k = slice(256 * i, 256 * i + 256)
        nt[:, k] = jnp.transpose(nrm[k, :])
        ct[:, k] = jnp.transpose(cp[k, :])
    store = None
    for b in range(BLOCKS):
        wb = w.at[b % 2]
        fetch[b].wait()
        if b + 1 < BLOCKS:
            fetch[b + 1].start()

        def block(i, _):
            r = span(i, 256)
            x, c = nrm[r, :], cp[r, :]
            gate = dot(x, wb[:, :FB])
            up = dot(x, wb[:, FB : 2 * FB])
            ga = dot(c, wb[:, 2 * FB :])
            sig = 0.5 * jnp.tanh(0.5 * gate) + 0.5
            silu = gate * sig
            act_b = (silu * up).astype(BF16)
            gg_b = (ga * up * (sig + silu * (1.0 - sig))).astype(BF16)
            gu_b = (ga * silu).astype(BF16)
            act[r, :], gg[r, :], gu[r, :] = act_b, gg_b, gu_b
            acc[r, :] += dot_nt(act_b, wb[:, 2 * FB :])
            gacc[r, :] += dot_nt(gg_b, wb[:, :FB]) + dot_nt(gu_b, wb[:, FB : 2 * FB])
            return 0

        lax.fori_loop(0, 4, block, 0)
        if store is not None:
            store.wait()

        def weights(i, _):
            r = span(i, 256)
            stage[r, :FB] = dot(nt[r, :], gg[...]).astype(BF16)
            stage[r, FB : 2 * FB] = dot(nt[r, :], gu[...]).astype(BF16)
            stage[r, 2 * FB :] = dot(ct[r, :], act[...]).astype(BF16)
            return 0

        lax.fori_loop(0, 4, weights, 0)
        store = pltpu.make_async_copy(stage, gc_hbm.at[b], gsem)
        store.start()
    gnorm_ref[...] = jnp.zeros_like(gnorm_ref)

    def last(i, _):
        r = span(i, 256)
        out_ref[r, :] = acc[r, :].astype(BF16)
        h, gn = hid[r, :], gacc[r, :]
        recip = lax.rsqrt(jnp.sum(h * h, axis=1, keepdims=True) * (1.0 / WIDTH) + EPS)
        gnorm_ref[...] += jnp.sum(gn * h * recip, axis=0, keepdims=True)
        scaled = gn * gain
        mean = jnp.sum(scaled * h, axis=1, keepdims=True) * (1.0 / WIDTH)
        gh = cp[r, :].astype(F32) + recip * scaled - h * (recip * recip * recip * mean)
        gh_ref[r, :] = gh
        low = gh.astype(BF16)
        nrm[r, :] = low
        for p in range(8):
            gheads_ref[p, r, :] = dot(low, b_ref[:, 128 * p : 128 * p + 128]).astype(BF16)
        return 0

    lax.fori_loop(0, 4, last, 0)
    for i in range(4):
        k = slice(256 * i, 256 * i + 256)
        nt[:, k] = jnp.transpose(nrm[k, :])

    def out_grad(i, _):
        r = span(i, 256)
        for p in range(8):
            gb_ref[r, 128 * p : 128 * p + 128] = dot(nt[r, :], ho[p]).astype(BF16)
        return 0

    lax.fori_loop(0, 4, out_grad, 0)
    store.wait()


def ffn(xp, cp, a_full, b_full, ho, c_full):
    shape = jax.ShapeDtypeStruct
    return pl.pallas_call(
        ffn_kernel,
        out_shape=[
            shape((T, D), BF16),
            shape((T, D), F32),
            shape((8, T, 128), BF16),
            shape((D, NB), BF16),
            shape((BLOCKS, D, NC), BF16),
            shape((1, D), F32),
        ],
        in_specs=[VMEM] * 5 + [ANY],
        out_specs=[VMEM] * 4 + [ANY, VMEM],
        scratch_shapes=[
            pltpu.VMEM((T, D), F32),
            pltpu.VMEM((T, D), F32),
            pltpu.VMEM((T, D), F32),
            pltpu.VMEM((T, D), BF16),
            pltpu.VMEM((D, T), BF16),
            pltpu.VMEM((D, T), BF16),
            pltpu.VMEM((2, D, NC), BF16),
            pltpu.VMEM((T, FB), BF16),
            pltpu.VMEM((T, FB), BF16),
            pltpu.VMEM((T, FB), BF16),
            pltpu.VMEM((D, NC), BF16),
            pltpu.SemaphoreType.DMA((2,)),
            pltpu.SemaphoreType.DMA,
        ],
        compiler_params=pltpu.CompilerParams(vmem_limit_bytes=VLIM),
        name="ffn",
    )(xp, cp, a_full, b_full, ho, c_full)


def attend_back_kernel(qt_ref, ho_ref, gheads_ref, lt_ref, cos_ref, sin_ref, dt_ref, kx, vx, dq, dk, dv):
    split_heads(qt_ref, kx, vx)
    dq[...] = jnp.zeros_like(dq)
    dk[...] = jnp.zeros_like(dk)
    dv[...] = jnp.zeros_like(dv)

    def head(i, _):
        s = i // 15
        h = i - 15 * s
        p, g = h // 2, h // 3
        par = h - 2 * p
        u = 2 * g + par
        seq = pl.ds(pl.multiple_of(s * SEQ, SEQ), SEQ)
        lane = lax.broadcasted_iota(jnp.int32, (SEQ, 128), 1)
        own = (lane // 64) == par
        q, do = qt_ref[p, seq, :], gheads_ref[p, seq, :]
        q_own = jnp.where(own, q, jnp.zeros_like(q))
        do_own = jnp.where(own, do, jnp.zeros_like(do))
        prod = do_own.astype(F32) * ho_ref[p, seq, :].astype(F32)
        high = prod.astype(BF16)
        rest = (prod - high.astype(F32)).astype(BF16)
        ones = jnp.ones((8, 128), BF16)
        off = (dot_nt(ones, high) + dot_nt(ones, rest))[:1, :]
        lse = lt_ref[h, :, seq]
        for b in range(2):
            nq = SEQ - 256 * b
            keys = pl.ds(pl.multiple_of(s * SEQ + 256 * b, 256), 256)
            kk, vv = kx[u, keys, :], vx[u, keys, :]
            st = dot_nt(kk, q[256 * b :, :])
            e = jnp.exp2(st * (SCALE * LOG2E) - lse[:, 256 * b :])
            row = lax.broadcasted_iota(jnp.int32, (256, nq), 0)
            col = lax.broadcasted_iota(jnp.int32, (256, nq), 1)
            e = jnp.where(row <= col, e, 0.0)
            dv[g, keys, :] += dot(e.astype(BF16), do_own[256 * b :, :])
            gp = dot_nt(vv, do[256 * b :, :])
            ds = (e * (gp - off[:, 256 * b :])).astype(BF16)
            dk[g, keys, :] += dot(ds, q_own[256 * b :, :])
            rows = pl.ds(pl.multiple_of(s * SEQ + 256 * b, 256), nq)
            dq[p, rows, :] += dot_tn(ds, kk)
        return 0

    lax.fori_loop(0, 30, head, 0)

    def finish(i, _):
        r = span(i, 256)
        half = span(i % 2, 256)
        cosine, sine = cos_ref[half, :], sin_ref[half, :]
        low = low_half((256, 128))
        fold = lambda ref, g: ref[g, r, :] + pltpu.roll(ref[g, r, :], 64, 1)
        tiles = [dq[p, r, :] for p in range(7)]
        tiles.append(jnp.where(low, dq[7, r, :], fold(dk, 0)))
        tiles.append(jnp.where(low, fold(dk, 1), fold(dk, 2)))
        tiles.append(jnp.where(low, fold(dk, 3), fold(dk, 4)))
        for t, v in enumerate(tiles):
            v = v * SCALE
            dt_ref[r, 128 * t : 128 * t + 128] = (v * cosine - swapped(v) * sine).astype(BF16)
        dt_ref[r, 1280:1408] = jnp.where(low, fold(dv, 0), fold(dv, 1)).astype(BF16)
        dt_ref[r, 1408:1536] = jnp.where(low, fold(dv, 2), fold(dv, 3)).astype(BF16)
        dt_ref[r, 1536:1664] = jnp.where(low, fold(dv, 4), 0.0).astype(BF16)
        return 0

    lax.fori_loop(0, 4, finish, 0)


def attend_back(qt, ho, gheads, lt, cosine, sine):
    return pl.pallas_call(
        attend_back_kernel,
        out_shape=jax.ShapeDtypeStruct((T, NA), BF16),
        in_specs=[VMEM] * 6,
        out_specs=VMEM,
        scratch_shapes=[
            pltpu.VMEM((10, T, 128), BF16),
            pltpu.VMEM((10, T, 128), BF16),
            pltpu.VMEM((8, T, 128), F32),
            pltpu.VMEM((5, T, 128), F32),
            pltpu.VMEM((5, T, 128), F32),
        ],
        compiler_params=pltpu.CompilerParams(vmem_limit_bytes=VLIM),
        name="attend_back",
    )(qt, ho, gheads, lt, cosine, sine)


def finish_kernel(dt, a_ref, nt, xp, gh, outp, gnf, ga_ref, gtok_ref, out_ref, spread, gsum):
    spread[...] = spread_matrix()
    gain = gain_row(a_ref, 64)
    gsum[...] = jnp.zeros_like(gsum)
    gsum[1:2, :] = gnf[...]

    def tokens(i, _):
        r = span(i, 256)
        gn = dot_nt(dt[r, :], a_ref[...])
        x = xp[r, :].astype(F32)
        recip = lax.rsqrt(jnp.sum(x * x, axis=1, keepdims=True) * (1.0 / WIDTH) + EPS)
        gsum[0:1, :] += jnp.sum(gn * x * recip, axis=0, keepdims=True)
        scaled = gn * gain
        mean = jnp.sum(scaled * x, axis=1, keepdims=True) * (1.0 / WIDTH)
        gt = gh[r, :] + recip * scaled - x * (recip * recip * recip * mean)
        high = gt.astype(BF16)
        left = gt - high.astype(F32)
        mid = left.astype(BF16)
        gtok_ref[r, :] = dot_nt(high, spread[...]) + dot_nt(mid, spread[...])
        out_ref[r, :] = dot_nt(outp[r, :], spread[...]).astype(BF16)
        return 0

    lax.fori_loop(0, 4, tokens, 0)

    def weights(i, _):
        r = span(i, 256)
        ga_ref[r, :] = dot(nt[r, :], dt[...]).astype(BF16)
        return 0

    lax.fori_loop(0, 4, weights, 0)
    cols = jnp.transpose(jnp.concatenate([gsum[...], jnp.zeros((120, D), F32)], axis=0))
    cols = pltpu.roll(cols, 64, 1)
    lane = lax.broadcasted_iota(jnp.int32, (D, 128), 1)
    tile = ga_ref[:, NA - 128 :].astype(F32)
    ga_ref[:, NA - 128 :] = jnp.where(lane < 64, tile, cols).astype(BF16)


def finish(dt, a_full, nt, xp, gh, outp, gnf):
    shape = jax.ShapeDtypeStruct
    return pl.pallas_call(
        finish_kernel,
        out_shape=[shape((D, NA), BF16), shape((T, WIDTH), F32), shape((T, WIDTH), BF16)],
        in_specs=[VMEM] * 7,
        out_specs=[VMEM] * 3,
        scratch_shapes=[pltpu.VMEM((WIDTH, D), BF16), pltpu.VMEM((8, D), F32)],
        compiler_params=pltpu.CompilerParams(vmem_limit_bytes=VLIM),
        name="finish",
    )(dt, a_full, nt, xp, gh, outp, gnf)


def shards(tokens, cotangent, wq, wk, wv, w_gate, w_up, wo, w_down, norm_attn, norm_ffn):
    pad = lambda a, n: jnp.pad(a, ((0, 1), (0, n - a.shape[1])))
    a = pad(jnp.concatenate([wq, wk, wv, norm_attn[:, None], norm_ffn[:, None]], axis=1), NA)
    b = pad(wo.T, NB)
    blocks = lambda w: w.reshape(15, BLOCKS, FB)
    c = jnp.concatenate([blocks(w_gate), blocks(w_up), blocks(w_down.T)], axis=2)
    c = jnp.pad(c.transpose(1, 0, 2), ((0, 0), (0, 1), (0, 0)))
    cosine, sine = rope_tables()
    fa, fb, fc = gather_all(a, b, c)
    fa, fb, fc = fa.reshape(D, NA), fb.reshape(D, NB), fc.reshape(BLOCKS, D, NC)
    xp, cp, _, nt, qt, ho, lt = attend(tokens, cotangent, fa, cosine, sine)
    outp, gh, gheads, gb, gc, gnf = ffn(xp, cp, fa, fb, ho, fc)
    dt = attend_back(qt, ho, gheads, lt, cosine, sine)
    ga, grad_tokens, output = finish(dt, fa, nt, xp, gh, outp, gnf)
    split = (4, 4, 2, 2, 16)
    sa, sb, sc = scatter_all(ga.reshape(*split, NA), gb.reshape(*split, NB), gc.reshape(BLOCKS, *split, NC))
    sc = sc[:, :15]
    unblock = lambda k: sc[:, :, FB * k : FB * k + FB].transpose(1, 0, 2).reshape(15, BLOCKS * FB)
    return (
        output,
        grad_tokens,
        sa[:15, :960],
        sa[:15, 960:1280],
        sa[:15, 1280:1600],
        unblock(0),
        unblock(1),
        sb[:15, :960].T,
        unblock(2).T,
        sa[:15, 1600],
        sa[:15, 1601],
    )


def solution(mesh):
    rows = P(("replica", "shard"), None)
    first, second, one = P("shard", None), P(None, "shard"), P("shard")
    in_specs = (rows, rows, first, first, first, first, first, second, second, one, one)
    out_specs = (rows, rows, first, first, first, first, first, second, second, one, one)
    return jax.shard_map(shards, mesh=mesh, in_specs=in_specs, out_specs=out_specs, check_vma=False)
```

```python
import functools
import math

import jax
import jax.numpy as jnp
import numpy as np
from jax import lax
from jax.experimental import pallas as pl
from jax.experimental.pallas import tpu as pltpu
from jax.sharding import PartitionSpec as P

F32, BF16 = jnp.float32, jnp.bfloat16
MESH = pl.DeviceIdType.MESH
ANY = pl.BlockSpec(memory_space=pl.ANY)
VMEM = pl.BlockSpec(memory_space=pltpu.VMEM)
WIDTH = 960
D = 1024
T = 1024
SEQ = 512
NQ = 1664
NA, NB, NC, BLOCKS, FB = 1792, 1024, 1536, 5, 512
EPS = 1e-05
SCALE = 0.125
LOG2E = math.log2(math.e)
EARLY = 3
VLIM = 60 * 1024 * 1024


def dot(a, b):
    return lax.dot_general(a, b, (((1,), (0,)), ((), ())), preferred_element_type=F32)


def dot_nt(a, b):
    return lax.dot_general(a, b, (((1,), (1,)), ((), ())), preferred_element_type=F32)


def dot_tn(a, b):
    return lax.dot_general(a, b, (((0,), (0,)), ((), ())), preferred_element_type=F32)


def span(i, n):
    return pl.ds(pl.multiple_of(i * n, n), n)


def rope_tables():
    rates = np.exp(np.arange(32) * (-2.0 * math.log(10000.0) / 64))
    angles = np.arange(SEQ)[:, None] * rates[None, :]
    cos, sin = np.cos(angles), np.sin(angles)
    cosine = np.concatenate([cos] * 4, axis=1).astype(np.float32)
    sine = np.concatenate([-sin, sin] * 2, axis=1).astype(np.float32)
    return cosine, sine


def swapped(t):
    lane = lax.broadcasted_iota(jnp.int32, t.shape, 1)
    return jnp.where((lane & 63) < 32, pltpu.roll(t, 96, 1), pltpu.roll(t, 32, 1))


def low_half(shape):
    return lax.broadcasted_iota(jnp.int32, shape, 1) < 64


def spread_matrix():
    row = lax.broadcasted_iota(jnp.int32, (WIDTH, D), 0)
    col = lax.broadcasted_iota(jnp.int32, (WIDTH, D), 1)
    hit = (row == 15 * (col >> 4) + (col & 15)) & ((col & 15) < 15)
    return jnp.where(hit, 1.0, 0.0).astype(BF16)


def place():
    r, s = lax.axis_index("replica"), lax.axis_index("shard")
    return s // 16, (s // 4) % 4, ((s // 2) % 2) * 2 + r, s % 2


def device(x, y, z, c):
    return (z % 2, ((x * 4 + y) * 2 + z // 2) * 2 + c)


def peers():
    x, y, z, c = place()
    along = {
        "x": [device((x + d) % 4, y, z, c) for d in (1, 2, 3)],
        "y": [device(x, (y + d) % 4, z, c) for d in (1, 2, 3)],
        "z": [device(x, y, (z + d) % 4, c) for d in (1, 2, 3)],
    }
    return along, device(x, y, z, 1 - c)


def meet():
    along, other = peers()
    barrier = pltpu.get_barrier_semaphore()
    for d in (*along["x"], *along["y"], *along["z"], other):
        pl.semaphore_signal(barrier, inc=1, device_id=d, device_id_type=MESH)
    pl.semaphore_wait(barrier, 10)


def remote(src, dst, ss, rs, k, to):
    return pltpu.make_async_remote_copy(
        src_ref=src, dst_ref=dst, send_sem=ss.at[k], recv_sem=rs.at[k], device_id=to, device_id_type=MESH
    )


def parts(n):
    tiles = n // 256
    widths = [128 * (tiles // 3), 128 * (tiles // 3), 128 * (tiles - 2 * (tiles // 3))]
    return [(0, widths[0]), (2 * widths[0], widths[1]), (2 * widths[0] + 2 * widths[1], widths[2])]


def half_of(offset, width, k):
    return pl.ds(pl.multiple_of(offset + k * width, 128), width)


SEMS = 30
GATHER_ORDER = ("yxz", "zyx", "xzy")
SCATTER_ORDER = ("zxy", "xyz", "yzx")


class Gather:
    def __init__(self, own, full, ss, rs, n):
        x, y, z, c = place()
        zh, zl = z // 2, z % 2
        along, other = peers()
        self.local, self.stages = [], [[], [], []]
        k = 3
        for (off, w), order in zip(parts(n), GATHER_ORDER):
            mine = half_of(off, w, zl)
            self.local.append(pltpu.make_async_copy(own.at[:, mine], full.at[x, y, zh, c, :, mine], ss.at[len(self.local)]))
            for i, axis in enumerate(order):
                have = order[:i]
                every = slice(None)
                at = (
                    every if "x" in have else x,
                    every if "y" in have else y,
                    every if "z" in have else zh,
                    c,
                    every,
                    pl.ds(off, 2 * w) if "z" in have else mine,
                )
                for to in along[axis]:
                    src = own.at[:, mine] if i == 0 else full.at[at]
                    self.stages[i].append(remote(src, full.at[at], ss, rs, k, to))
                    k += 1
        w = full.at[:, :, :, c]
        self.core = remote(w, w, ss, rs, k, other)

    def move(self, done, begin):
        for d in done:
            d.wait()
        for d in begin:
            d.start()

    def s0(self):
        self.move([], self.local + self.stages[0])

    def s1(self):
        self.move(self.local + self.stages[0], self.stages[1])

    def s2(self):
        self.move(self.stages[1], self.stages[2])

    def s3(self):
        self.move(self.stages[2], [self.core])

    def s4(self):
        self.move([self.core], [])


def gather_sems():
    return [pltpu.SemaphoreType.DMA((SEMS + 1,)), pltpu.SemaphoreType.DMA((SEMS + 1,))]


def extent(left, w):
    return tuple([4] * ("x" in left) + [4] * ("y" in left) + [2] * ("z" in left) + [16, 2 * w if "z" in left else w])


def slot(left, axis, t, off, w):
    every = slice(None)
    cols = pl.ds(off, 2 * w) if "z" in left else every
    if axis == "z":
        cols = half_of(off, w, t % 2)
    at = [every] * ("x" in left) + [every] * ("y" in left) + [every] * ("z" in left)
    lead = [a for a in "xyz" if a in left]
    at[lead.index(axis)] = t // 2 if axis == "z" else t
    return (*at, every, cols)


LANDING, LOCAL = 13, 8


def landing(n):
    one, two, three = [], [], []
    for (_, w), order in zip(parts(n), SCATTER_ORDER):
        one.append(pltpu.VMEM((3, *extent(order[1:], w)), BF16))
        two.append(pltpu.VMEM((3, *extent(order[2:], w)), BF16))
        three.append(pltpu.VMEM((3, 16, w), F32))
    sems = [pltpu.SemaphoreType.DMA((SEMS,)), pltpu.SemaphoreType.DMA((SEMS,))]
    return [pltpu.VMEM((4, 4, 2, 16, n), BF16), *one, *two, *three, pltpu.VMEM((16, n // 2), F32), *sems]


def local(n):
    two, three = [], []
    for (_, w), order in zip(parts(n), SCATTER_ORDER):
        two.append(pltpu.VMEM(extent(order[1:], w), BF16))
        three.append(pltpu.VMEM(extent(order[2:], w), F32))
    return [pltpu.VMEM((4, 4, 2, 16, n), BF16), *two, *three, pltpu.VMEM((16, n // 2), F32)]


class Scatter:
    def __init__(self, part, out, land, loc, n):
        x, y, z, c = place()
        self.at, self.out, self.parts = {"x": x, "y": y, "z": z}, out, parts(n)
        along, other = peers()
        self.r0, self.r4, ss, rs = land[0], *land[10:]
        self.p1, self.p4 = loc[0], loc[7]
        self.took = [land[1:4], land[4:7], land[7:10]]
        self.held = [[self.p1] * 3, loc[1:4], loc[4:7]]
        self.local = pltpu.make_async_copy(part.at[:, :, :, c], self.p1, ss.at[0])
        self.core = remote(part.at[:, :, :, 1 - c], self.r0, ss, rs, 1, other)
        self.sends, k = [[], [], []], 2
        for i in range(3):
            for q, order in enumerate(SCATTER_ORDER):
                for d in (1, 2, 3):
                    axis = order[i]
                    src = self.held[i][q].at[self.index(q, i, (self.at[axis] + d) % 4)]
                    self.sends[i].append(remote(src, self.took[i][q].at[d - 1], ss, rs, k, along[axis][d - 1]))
                    k += 1
        self.rep = remote(self.p4, self.r4, ss, rs, k, device(x, y, z + 1 - 2 * (z % 2), c))

    def index(self, q, i, t):
        off, w = self.parts[q]
        order = SCATTER_ORDER[q]
        return slot(order[i:], order[i], t, off if i == 0 else 0, w)

    def total(self, i, to):
        for q, order in enumerate(SCATTER_ORDER):
            own = self.held[i][q].at[self.index(q, i, self.at[order[i]])]
            took = self.took[i][q]
            lead = own.shape[:-2]

            def add(j, own=own, took=took, q=q):
                value = own[j].astype(F32)
                for k in range(3):
                    value += took[(k, *j)].astype(F32)
                to(q, j, value)

            if len(lead) == 2:

                def turn(a, _, add=add, lead=lead):
                    for b in range(lead[1]):
                        add((a, b))
                    return 0

                lax.fori_loop(0, lead[0], turn, 0)
            elif len(lead) == 1:
                for a in range(lead[0]):
                    add((a,))
            else:
                add(())

    def s0(self):
        self.local.start()
        self.core.start()

    def s1(self):
        self.local.wait()
        self.core.wait()

        def add(i, _):
            a, b = i // 4, i % 4
            self.p1[a, b] = (self.p1[a, b].astype(F32) + self.r0[a, b].astype(F32)).astype(BF16)
            return 0

        lax.fori_loop(0, 16, add, 0)
        for d in self.sends[0]:
            d.start()

    def stage(self, i):
        for d in self.sends[i]:
            d.wait()

        def to(q, j, value):
            ref = self.held[i + 1][q]
            ref[j] = value.astype(ref.dtype)

        self.total(i, to)
        for d in self.sends[i + 1]:
            d.start()

    def s2(self):
        self.stage(0)

    def s3(self):
        self.stage(1)

    def s4(self):
        for d in self.sends[2]:
            d.wait()

        def to(q, j, value):
            off, w = self.parts[q]
            self.p4[:, off // 2 : off // 2 + w] = value

        self.total(2, to)
        self.rep.start()

    def s5(self):
        self.rep.wait()
        k = self.at["z"] % 2
        for off, w in self.parts:
            self.out[:, half_of(off, w, k)] = self.p4[:, off // 2 : off // 2 + w]
            self.out[:, half_of(off, w, 1 - k)] = self.r4[:, off // 2 : off // 2 + w]


def run(plan, i):
    for at, steps in plan.items():

        @pl.when(i == at)
        def _():
            for step in steps:
                step()


def start_kernel(a, tok_hbm, cot_hbm, fa, xp_ref, cp_ref, tok, cot, spread, ss, rs, sem):
    meet()
    chunk = Gather(a, fa, ss, rs, NA)
    chunk.s0()
    reads = [pltpu.make_async_copy(tok_hbm, tok, sem.at[0]), pltpu.make_async_copy(cot_hbm, cot, sem.at[1])]
    for r in reads:
        r.start()
    spread[...] = spread_matrix()
    chunk.s1()
    for r in reads:
        r.wait()

    def widen(i, _):
        r = span(i, 256)
        xp_ref[r, :] = dot(tok[r, :], spread[...]).astype(BF16)
        cp_ref[r, :] = dot(cot[r, :], spread[...]).astype(BF16)
        run({1: [chunk.s2]}, i)
        return 0

    lax.fori_loop(0, 4, widen, 0)
    chunk.s3()
    chunk.s4()


def start(a, tok, cot):
    return pl.pallas_call(
        start_kernel,
        out_shape=[
            jax.ShapeDtypeStruct((4, 4, 2, 2, 16, NA), BF16),
            jax.ShapeDtypeStruct((T, D), BF16),
            jax.ShapeDtypeStruct((T, D), BF16),
        ],
        in_specs=[ANY] * 3,
        out_specs=[ANY, VMEM, VMEM],
        scratch_shapes=[
            pltpu.VMEM((T, WIDTH), BF16),
            pltpu.VMEM((T, WIDTH), BF16),
            pltpu.VMEM((WIDTH, D), BF16),
            *gather_sems(),
            pltpu.SemaphoreType.DMA((2,)),
        ],
        compiler_params=pltpu.CompilerParams(collective_id=0, has_side_effects=True, vmem_limit_bytes=VLIM),
        name="start",
    )(a, tok, cot)


def gain_rows(a_ref):
    return jnp.transpose(a_ref[:, NQ - 128 : NQ].astype(F32))[64:72, :]


def attend_kernel(xp_ref, a_ref, cos_ref, sin_ref, b, c, nt_ref, qt_ref, ho_ref, lt_ref, gains_ref, fb, fc, nrm_ref, kx, vx, lse, *sems):
    meet()
    cb = Gather(b, fb, sems[0], sems[1], NB)
    c0, c1, c2 = (Gather(c.at[i], fc.at[i], sems[2 + 2 * i], sems[3 + 2 * i], NC) for i in range(EARLY))
    for ch in (cb, c0, c1, c2):
        ch.s0()
    gains_ref[...] = gain_rows(a_ref)
    gain = gains_ref[0:1, :]

    def project(i, _):
        r = span(i, 256)
        x = xp_ref[r, :].astype(F32)
        recip = lax.rsqrt(jnp.sum(x * x, axis=1, keepdims=True) * (1.0 / WIDTH) + EPS)
        normed = (x * recip * gain).astype(BF16)
        nrm_ref[r, :] = normed
        half = span(i % 2, 256)
        cosine, sine = cos_ref[half, :], sin_ref[half, :]
        for t in range(13):
            q = dot(normed, a_ref[:, 128 * t : 128 * t + 128])
            if t < 10:
                q = q * cosine + swapped(q) * sine
            qt_ref[t, r, :] = q.astype(BF16)
        run({1: [cb.s1, c0.s1, c1.s1, c2.s1], 3: [cb.s2, c0.s2]}, i)
        return 0

    lax.fori_loop(0, 4, project, 0)
    for i in range(4):
        nt_ref[:, 256 * i : 256 * i + 256] = jnp.transpose(nrm_ref[256 * i : 256 * i + 256, :])
    split_heads(qt_ref, kx, vx)
    ho_ref[...] = jnp.zeros_like(ho_ref)
    lse[...] = jnp.zeros_like(lse)

    def head(i, _):
        s = i // 15
        h = i - 15 * s
        p, g = h // 2, h // 3
        u = 2 * g + h - 2 * p
        for b in range(2):
            nk = 256 * (b + 1)
            rows = pl.ds(pl.multiple_of(s * SEQ + 256 * b, 256), 256)
            keys = pl.ds(pl.multiple_of(s * SEQ, SEQ), nk)
            sc = dot_nt(qt_ref[p, rows, :], kx[u, keys, :])
            row = lax.broadcasted_iota(jnp.int32, (256, nk), 0) + 256 * b
            col = lax.broadcasted_iota(jnp.int32, (256, nk), 1)
            sc = jnp.where(col <= row, sc, -1e30)
            top = jnp.max(sc, axis=1, keepdims=True)
            e = jnp.exp2((sc - top) * (SCALE * LOG2E))
            total = jnp.sum(e, axis=1, keepdims=True)
            soft = (e * (1.0 / total)).astype(BF16)
            o = dot(soft, vx[u, keys, :])
            ho_ref[p, rows, :] = ho_ref[p, rows, :] + o.astype(BF16)
            lane = lax.broadcasted_iota(jnp.int32, (256, 128), 1)
            stat = top * (SCALE * LOG2E) + jnp.log2(total)
            lse[rows, :] = jnp.where(lane == h, stat, lse[rows, :])
        run({5: [cb.s3, c1.s2], 12: [c0.s3, c2.s2], 19: [c1.s3, cb.s4], 22: [c0.s4], 26: [c2.s3]}, i)
        return 0

    lax.fori_loop(0, 30, head, 0)
    lt_ref[...] = jnp.transpose(lse[...])[:16, :].reshape(16, 1, T)
    c1.s4()
    c2.s4()


def split_heads(qt_ref, kx, vx):
    low = low_half((T, 128))
    for g in range(5):
        for to, unit in ((kx, 15 + g), (vx, 20 + g)):
            tile = qt_ref[unit // 2].astype(F32)
            turned = pltpu.roll(tile, 64, 1)
            at_low, at_high = (tile, turned) if unit % 2 == 0 else (turned, tile)
            to[2 * g] = jnp.where(low, at_low, 0.0).astype(BF16)
            to[2 * g + 1] = jnp.where(low, 0.0, at_high).astype(BF16)


def attend(xp, a_full, cosine, sine, b, c):
    shape = jax.ShapeDtypeStruct
    return pl.pallas_call(
        attend_kernel,
        out_shape=[
            shape((D, T), BF16),
            shape((13, T, 128), BF16),
            shape((8, T, 128), BF16),
            shape((16, 1, T), F32),
            shape((8, D), F32),
            shape((4, 4, 2, 2, 16, NB), BF16),
            shape((EARLY, 4, 4, 2, 2, 16, NC), BF16),
        ],
        in_specs=[VMEM] * 4 + [ANY] * 2,
        out_specs=[VMEM] * 5 + [ANY] * 2,
        scratch_shapes=[
            pltpu.VMEM((T, D), BF16),
            pltpu.VMEM((10, T, 128), BF16),
            pltpu.VMEM((10, T, 128), BF16),
            pltpu.VMEM((T, 128), F32),
            *gather_sems() * (1 + EARLY),
        ],
        compiler_params=pltpu.CompilerParams(collective_id=1, has_side_effects=True, vmem_limit_bytes=VLIM),
        name="attend",
    )(xp, a_full, cosine, sine, b, c)


def ffn_kernel(xp, cp, gains, b_ref, ho, c_early, c_own, hid, gheads_ref, gnorm_ref, oc_ref, outp_hbm, gb_hbm, gc_hbm, fc,
               acc, gacc, nrm, nt, ct, w, act, gg, gu, stage, wsem, gsem, *scratch):
    meet()
    late = BLOCKS - EARLY
    gathers = [Gather(c_own.at[EARLY + i], fc.at[i], scratch[2 * i], scratch[2 * i + 1], NC) for i in range(late)]
    rest = scratch[2 * late :]
    lands = [rest[LANDING * i : LANDING * (i + 1)] for i in range(EARLY)]
    rest = rest[LANDING * EARLY :]
    sets = [rest[:LOCAL], rest[LOCAL:]]
    early = [Scatter(gc_hbm.at[i], oc_ref.at[i], lands[i], sets[i % 2], NC) for i in range(EARLY)]
    gain = gains[1:2, :]
    source = lambda b: c_early.at[b] if b < EARLY else fc.at[b - EARLY]
    fetch = [pltpu.make_async_copy(source(b), w.at[b % 2], wsem.at[b % 2]) for b in range(BLOCKS)]
    store = [pltpu.make_async_copy(stage, gc_hbm.at[b], gsem) for b in range(BLOCKS)]
    for ch in gathers:
        ch.s0()
    fetch[0].start()

    def first(i, _):
        r = span(i, 256)
        h = xp[r, :].astype(F32)
        for p in range(8):
            h += dot_nt(ho[p, r, :], b_ref[:, 128 * p : 128 * p + 128])
        hid[r, :] = h
        acc[r, :] = h
        recip = lax.rsqrt(jnp.sum(h * h, axis=1, keepdims=True) * (1.0 / WIDTH) + EPS)
        nrm[r, :] = (h * recip * gain).astype(BF16)
        gacc[r, :] = jnp.zeros((256, D), F32)
        run({1: [ch.s1 for ch in gathers], 3: [ch.s2 for ch in gathers]}, i)
        return 0

    lax.fori_loop(0, 4, first, 0)
    for i in range(4):
        k = slice(256 * i, 256 * i + 256)
        nt[:, k] = jnp.transpose(nrm[k, :])
        ct[:, k] = jnp.transpose(cp[k, :])
    for b in range(BLOCKS):
        wv = w.at[b % 2].reshape(D, NC)
        fetch[b].wait()
        if b + 1 < BLOCKS and b + 1 != EARLY:
            fetch[b + 1].start()
        plan_a, plan_b = {1: [], 3: []}, {1: [], 3: []}
        if b:
            plan_a[1].append(store[b - 1].wait)
        if 0 <= b - 1 < EARLY:
            plan_a[1].append(early[b - 1].s0)
            plan_a[3].append(early[b - 1].s1)
        if 0 <= b - 2 < EARLY:
            plan_a[1].append(early[b - 2].s2)
            plan_a[3].append(early[b - 2].s3)
            plan_b[1].append(early[b - 2].s4)
            plan_b[3].append(early[b - 2].s5)
        if b == 1:
            plan_a[3] += [ch.s3 for ch in gathers]
        if b == EARLY - 1:
            plan_a[3] += [ch.s4 for ch in gathers] + [fetch[EARLY].start]

        def block(i, _):
            r = span(i, 256)
            x, c = nrm[r, :], cp[r, :]
            gate = dot(x, wv[:, :FB])
            up = dot(x, wv[:, FB : 2 * FB])
            ga = dot(c, wv[:, 2 * FB :])
            sig = 0.5 * jnp.tanh(0.5 * gate) + 0.5
            silu = gate * sig
            act_b = (silu * up).astype(BF16)
            gg_b = (ga * up * (sig + silu * (1.0 - sig))).astype(BF16)
            gu_b = (ga * silu).astype(BF16)
            act[r, :], gg[r, :], gu[r, :] = act_b, gg_b, gu_b
            acc[r, :] += dot_nt(act_b, wv[:, 2 * FB :])
            gacc[r, :] += dot_nt(gg_b, wv[:, :FB]) + dot_nt(gu_b, wv[:, FB : 2 * FB])
            run(plan_a, i)
            return 0

        lax.fori_loop(0, 4, block, 0)

        def weights(i, _):
            r = span(i, 256)
            k = span(i, 1)
            to = lambda v: v.astype(BF16).reshape(4, 2, 2, 16, FB)
            stage[i, :, :, :, :, :FB] = to(dot(nt[r, :], gg[...]))
            stage[i, :, :, :, :, FB : 2 * FB] = to(dot(nt[r, :], gu[...]))
            stage[i, :, :, :, :, 2 * FB :] = to(dot(ct[r, :], act[...]))
            run(plan_b, i)
            return 0

        lax.fori_loop(0, 4, weights, 0)
        store[b].start()
    gnorm_ref[...] = jnp.zeros_like(gnorm_ref)
    out_stage = w.at[0].reshape(D, NC).at[:, :D]

    def last(i, _):
        r = span(i, 256)
        out_stage[r, :] = acc[r, :].astype(BF16)
        h, gn = hid[r, :], gacc[r, :]
        recip = lax.rsqrt(jnp.sum(h * h, axis=1, keepdims=True) * (1.0 / WIDTH) + EPS)
        gnorm_ref[...] += jnp.sum(gn * h * recip, axis=0, keepdims=True)
        scaled = gn * gain
        mean = jnp.sum(scaled * h, axis=1, keepdims=True) * (1.0 / WIDTH)
        gh = cp[r, :].astype(F32) + recip * scaled - h * (recip * recip * recip * mean)
        hid[r, :] = gh
        low = gh.astype(BF16)
        nrm[r, :] = low
        for p in range(8):
            gheads_ref[p, r, :] = dot(low, b_ref[:, 128 * p : 128 * p + 128]).astype(BF16)
        return 0

    lax.fori_loop(0, 4, last, 0)
    put_out = pltpu.make_async_copy(out_stage, outp_hbm, wsem.at[0])
    put_out.start()
    for i in range(4):
        k = slice(256 * i, 256 * i + 256)
        nt[:, k] = jnp.transpose(nrm[k, :])
    store[BLOCKS - 1].wait()

    def out_grad(i, _):
        r = span(i, 256)
        for p in range(8):
            stage[i, :, :, :, :, 128 * p : 128 * p + 128] = dot(nt[r, :], ho[p]).astype(BF16).reshape(4, 2, 2, 16, 128)
        return 0

    lax.fori_loop(0, 4, out_grad, 0)
    put_gb = pltpu.make_async_copy(stage.at[:, :, :, :, :, :NB], gb_hbm, gsem)
    put_gb.start()
    put_out.wait()
    put_gb.wait()


def ffn(xp, cp, gains, b_full, ho, c_early, c_own):
    shape = jax.ShapeDtypeStruct
    late = BLOCKS - EARLY
    scratch = gather_sems() * late
    for _ in range(EARLY):
        scratch += landing(NC)
    scratch += local(NC) * 2
    return pl.pallas_call(
        ffn_kernel,
        out_shape=[
            shape((T, D), F32),
            shape((8, T, 128), BF16),
            shape((1, D), F32),
            shape((EARLY, 16, NC), F32),
            shape((T, D), BF16),
            shape((4, 4, 2, 2, 16, NB), BF16),
            shape((BLOCKS, 4, 4, 2, 2, 16, NC), BF16),
            shape((late, 4, 4, 2, 2, 16, NC), BF16),
        ],
        in_specs=[VMEM] * 5 + [ANY] * 2,
        out_specs=[VMEM] * 4 + [ANY] * 4,
        scratch_shapes=[
            pltpu.VMEM((T, D), F32),
            pltpu.VMEM((T, D), F32),
            pltpu.VMEM((T, D), BF16),
            pltpu.VMEM((D, T), BF16),
            pltpu.VMEM((D, T), BF16),
            pltpu.VMEM((2, 4, 4, 2, 2, 16, NC), BF16),
            pltpu.VMEM((T, FB), BF16),
            pltpu.VMEM((T, FB), BF16),
            pltpu.VMEM((T, FB), BF16),
            pltpu.VMEM((4, 4, 2, 2, 16, NC), BF16),
            pltpu.SemaphoreType.DMA((2,)),
            pltpu.SemaphoreType.DMA,
            *scratch,
        ],
        compiler_params=pltpu.CompilerParams(collective_id=2, has_side_effects=True, vmem_limit_bytes=VLIM),
        name="ffn",
    )(xp, cp, gains, b_full, ho, c_early, c_own)


def attend_back_kernel(qt_ref, ho_ref, gheads_ref, lt_ref, cos_ref, sin_ref, gb, gc, dt_ref, ob_ref, oc_ref, kx, vx, dq, dk, dv, *scratch):
    meet()
    late = BLOCKS - EARLY
    lands = [scratch[LANDING * i : LANDING * (i + 1)] for i in range(late + 1)]
    rest = scratch[LANDING * (late + 1) :]
    sets = [rest[LOCAL * i : LOCAL * (i + 1)] for i in range(late + 1)]
    c3, c4 = (Scatter(gc.at[EARLY + i], oc_ref.at[i], lands[i], sets[i], NC) for i in range(late))
    cb = Scatter(gb, ob_ref, lands[late], sets[late], NB)
    for ch in (c3, c4, cb):
        ch.s0()
    split_heads(qt_ref, kx, vx)
    dq[...] = jnp.zeros_like(dq)
    dk[...] = jnp.zeros_like(dk)
    dv[...] = jnp.zeros_like(dv)

    def head(i, _):
        s = i // 15
        h = i - 15 * s
        p, g = h // 2, h // 3
        par = h - 2 * p
        u = 2 * g + par
        seq = pl.ds(pl.multiple_of(s * SEQ, SEQ), SEQ)
        lane = lax.broadcasted_iota(jnp.int32, (SEQ, 128), 1)
        own = (lane // 64) == par
        q, do = qt_ref[p, seq, :], gheads_ref[p, seq, :]
        q_own = jnp.where(own, q, jnp.zeros_like(q))
        do_own = jnp.where(own, do, jnp.zeros_like(do))
        prod = do_own.astype(F32) * ho_ref[p, seq, :].astype(F32)
        high = prod.astype(BF16)
        rest = (prod - high.astype(F32)).astype(BF16)
        ones = jnp.ones((8, 128), BF16)
        off = (dot_nt(ones, high) + dot_nt(ones, rest))[:1, :]
        lse = lt_ref[h, :, seq]
        for b in range(2):
            nq = SEQ - 256 * b
            keys = pl.ds(pl.multiple_of(s * SEQ + 256 * b, 256), 256)
            kk, vv = kx[u, keys, :], vx[u, keys, :]
            st = dot_nt(kk, q[256 * b :, :])
            e = jnp.exp2(st * (SCALE * LOG2E) - lse[:, 256 * b :])
            row = lax.broadcasted_iota(jnp.int32, (256, nq), 0)
            col = lax.broadcasted_iota(jnp.int32, (256, nq), 1)
            e = jnp.where(row <= col, e, 0.0)
            dv[g, keys, :] += dot(e.astype(BF16), do_own[256 * b :, :])
            gp = dot_nt(vv, do[256 * b :, :])
            ds = (e * (gp - off[:, 256 * b :])).astype(BF16)
            dk[g, keys, :] += dot(ds, q_own[256 * b :, :])
            rows = pl.ds(pl.multiple_of(s * SEQ + 256 * b, 256), nq)
            dq[p, rows, :] += dot_tn(ds, kk)
        run({1: [c3.s1], 3: [c4.s1], 5: [cb.s1], 8: [c3.s2], 11: [c3.s3], 14: [c4.s2], 15: [c3.s4], 17: [c4.s3, c3.s5],
             20: [cb.s2, c4.s4], 23: [cb.s3, c4.s5], 26: [cb.s4], 29: [cb.s5]}, i)
        return 0

    lax.fori_loop(0, 30, head, 0)

    def finish(i, _):
        r = span(i, 256)
        half = span(i % 2, 256)
        cosine, sine = cos_ref[half, :], sin_ref[half, :]
        low = low_half((256, 128))
        fold = lambda ref, g: ref[g, r, :] + pltpu.roll(ref[g, r, :], 64, 1)
        tiles = [dq[p, r, :] for p in range(7)]
        tiles.append(jnp.where(low, dq[7, r, :], fold(dk, 0)))
        tiles.append(jnp.where(low, fold(dk, 1), fold(dk, 2)))
        tiles.append(jnp.where(low, fold(dk, 3), fold(dk, 4)))
        for t, v in enumerate(tiles):
            v = v * SCALE
            dt_ref[r, 128 * t : 128 * t + 128] = (v * cosine - swapped(v) * sine).astype(BF16)
        dt_ref[r, 1280:1408] = jnp.where(low, fold(dv, 0), fold(dv, 1)).astype(BF16)
        dt_ref[r, 1408:1536] = jnp.where(low, fold(dv, 2), fold(dv, 3)).astype(BF16)
        dt_ref[r, 1536:1664] = jnp.where(low, fold(dv, 4), 0.0).astype(BF16)
        return 0

    lax.fori_loop(0, 4, finish, 0)


def attend_back(qt, ho, gheads, lt, cosine, sine, gb, gc):
    late = BLOCKS - EARLY
    scratch = landing(NC) * late + landing(NB) + local(NC) * late + local(NB)
    shape = jax.ShapeDtypeStruct
    return pl.pallas_call(
        attend_back_kernel,
        out_shape=[shape((T, NQ), BF16), shape((16, NB), F32), shape((late, 16, NC), F32)],
        in_specs=[VMEM] * 6 + [ANY] * 2,
        out_specs=[VMEM] * 3,
        scratch_shapes=[
            pltpu.VMEM((10, T, 128), BF16),
            pltpu.VMEM((10, T, 128), BF16),
            pltpu.VMEM((8, T, 128), F32),
            pltpu.VMEM((5, T, 128), F32),
            pltpu.VMEM((5, T, 128), F32),
            *scratch,
        ],
        compiler_params=pltpu.CompilerParams(collective_id=3, has_side_effects=True, vmem_limit_bytes=VLIM),
        name="attend_back",
    )(qt, ho, gheads, lt, cosine, sine, gb, gc)


def finish_kernel(dt, a_ref, gains, nt, xp, gh, outp, gnf, gtok_hbm, out_hbm, oa_ref, ga, spread, gsum, cols_ref, gn_ref, gtok, out, osem, *scratch):
    meet()
    chunk = Scatter(ga, oa_ref, scratch[:LANDING], scratch[LANDING:], NA)
    gain = gains[0:1, :]
    gsum[...] = jnp.zeros_like(gsum)
    gsum[1:2, :] = gnf[...]

    def normed(i, _):
        r = span(i, 256)
        gn = dot_nt(dt[r, :], a_ref[:, :NQ])
        gn_ref[r, :] = gn
        x = xp[r, :].astype(F32)
        recip = lax.rsqrt(jnp.sum(x * x, axis=1, keepdims=True) * (1.0 / WIDTH) + EPS)
        gsum[0:1, :] += jnp.sum(gn * x * recip, axis=0, keepdims=True)
        return 0

    lax.fori_loop(0, 4, normed, 0)
    cols = jnp.transpose(jnp.concatenate([gsum[...], jnp.zeros((120, D), F32)], axis=0))
    gn_cols = pltpu.roll(cols, 64, 1)
    cols_ref[...] = gn_cols

    def weights(i, _):
        r = span(i, 256)
        g = dot(nt[r, :], dt[...])
        low = low_half((256, 128))
        tile = jnp.where(low, g[:, NQ - 128 :], cols_ref[r, :])
        to = lambda v: v.astype(BF16).reshape(4, 2, 2, 16, v.shape[1])
        ga[i, :, :, :, :, : NQ - 128] = to(g[:, : NQ - 128])
        ga[i, :, :, :, :, NQ - 128 : NQ] = to(tile)
        ga[i, :, :, :, :, NQ:] = jnp.zeros((4, 2, 2, 16, NA - NQ), BF16)
        return 0

    lax.fori_loop(0, 4, weights, 0)
    chunk.s0()
    spread[...] = spread_matrix()
    chunk.s1()

    def tokens(i, _):
        r = span(i, 256)
        x = xp[r, :].astype(F32)
        recip = lax.rsqrt(jnp.sum(x * x, axis=1, keepdims=True) * (1.0 / WIDTH) + EPS)
        scaled = gn_ref[r, :] * gain
        mean = jnp.sum(scaled * x, axis=1, keepdims=True) * (1.0 / WIDTH)
        gt = gh[r, :] + recip * scaled - x * (recip * recip * recip * mean)
        high = gt.astype(BF16)
        mid = (gt - high.astype(F32)).astype(BF16)
        gtok[r, :] = dot_nt(high, spread[...]) + dot_nt(mid, spread[...])
        out[r, :] = dot_nt(outp[r, :], spread[...]).astype(BF16)
        run({2: [chunk.s2], 3: [chunk.s3]}, i)
        return 0

    lax.fori_loop(0, 4, tokens, 0)
    puts = [pltpu.make_async_copy(gtok, gtok_hbm, osem.at[0]), pltpu.make_async_copy(out, out_hbm, osem.at[1])]
    for p in puts:
        p.start()
    chunk.s4()
    chunk.s5()
    for p in puts:
        p.wait()


def finish(dt, a_full, gains, nt, xp, gh, outp, gnf):
    shape = jax.ShapeDtypeStruct
    return pl.pallas_call(
        finish_kernel,
        out_shape=[shape((T, WIDTH), F32), shape((T, WIDTH), BF16), shape((16, NA), F32)],
        in_specs=[VMEM] * 8,
        out_specs=[ANY, ANY, VMEM],
        scratch_shapes=[
            pltpu.VMEM((4, 4, 2, 2, 16, NA), BF16),
            pltpu.VMEM((WIDTH, D), BF16),
            pltpu.VMEM((8, D), F32),
            pltpu.VMEM((D, 128), F32),
            pltpu.VMEM((T, D), F32),
            pltpu.VMEM((T, WIDTH), F32),
            pltpu.VMEM((T, WIDTH), BF16),
            pltpu.SemaphoreType.DMA((2,)),
            *landing(NA),
            *local(NA),
        ],
        compiler_params=pltpu.CompilerParams(collective_id=4, has_side_effects=True, vmem_limit_bytes=VLIM),
        name="finish",
    )(dt, a_full, gains, nt, xp, gh, outp, gnf)


def shards(tokens, cotangent, wq, wk, wv, w_gate, w_up, wo, w_down, norm_attn, norm_ffn):
    pad = lambda a, n: jnp.pad(a, ((0, 1), (0, n - a.shape[1])))
    a = pad(jnp.concatenate([wq, wk, wv, norm_attn[:, None], norm_ffn[:, None]], axis=1), NA)
    b = pad(wo.T, NB)
    blocks = lambda w: w.reshape(15, BLOCKS, FB)
    c = jnp.concatenate([blocks(w_gate), blocks(w_up), blocks(w_down.T)], axis=2)
    c = jnp.pad(c.transpose(1, 0, 2), ((0, 0), (0, 1), (0, 0)))
    cosine, sine = rope_tables()
    fa, xp, cp = start(a, tokens, cotangent)
    fa = fa.reshape(D, NA)
    nt, qt, ho, lt, gains, fb, fc = attend(xp, fa, cosine, sine, b, c)
    gh, gheads, gnf, sc_early, outp, gb, gc, _ = ffn(xp, cp, gains, fb.reshape(D, NB), ho, fc, c)
    dt, sb, sc_late = attend_back(qt, ho, gheads, lt, cosine, sine, gb, gc)
    grad_tokens, output, sa = finish(dt, fa, gains, nt, xp, gh, outp, gnf)
    sc = jnp.concatenate([sc_early, sc_late])
    sc = sc[:, :15]
    unblock = lambda k: sc[:, :, FB * k : FB * k + FB].transpose(1, 0, 2).reshape(15, BLOCKS * FB)
    return (
        output,
        grad_tokens,
        sa[:15, :960],
        sa[:15, 960:1280],
        sa[:15, 1280:1600],
        unblock(0),
        unblock(1),
        sb[:15, :960].T,
        unblock(2).T,
        sa[:15, 1600],
        sa[:15, 1601],
    )


def solution(mesh):
    rows = P(("replica", "shard"), None)
    first, second, one = P("shard", None), P(None, "shard"), P("shard")
    in_specs = (rows, rows, first, first, first, first, first, second, second, one, one)
    out_specs = (rows, rows, first, first, first, first, first, second, second, one, one)
    return jax.shard_map(shards, mesh=mesh, in_specs=in_specs, out_specs=out_specs, check_vma=False)
```

```python
import functools
import math

import jax
import jax.numpy as jnp
import numpy as np
from jax import lax
from jax.experimental import pallas as pl
from jax.experimental.pallas import tpu as pltpu
from jax.sharding import PartitionSpec as P

F32, BF16 = jnp.float32, jnp.bfloat16
MESH = pl.DeviceIdType.MESH
ANY = pl.BlockSpec(memory_space=pl.ANY)
VMEM = pl.BlockSpec(memory_space=pltpu.VMEM)
WIDTH = 960
D = 1024
T = 1024
SEQ = 512
NQ = 1664
NA, NB, NC, BLOCKS, FB = 1792, 1024, 1536, 5, 512
EARLY = 3
NE, NL = NB + EARLY * NC, (BLOCKS - EARLY) * NC
L0 = 2304
L1 = NL + NB - L0
E0 = NB + NC
E1 = NE - E0
A0 = 1024
A1 = NA - A0
EPS = 1e-05
SCALE = 0.125
LOG2E = math.log2(math.e)
VLIM = 60 * 1024 * 1024


def dot(a, b):
    return lax.dot_general(a, b, (((1,), (0,)), ((), ())), preferred_element_type=F32)


def dot_nt(a, b):
    return lax.dot_general(a, b, (((1,), (1,)), ((), ())), preferred_element_type=F32)


def dot_tn(a, b):
    return lax.dot_general(a, b, (((0,), (0,)), ((), ())), preferred_element_type=F32)


def span(i, n):
    return pl.ds(pl.multiple_of(i * n, n), n)


def rope_tables():
    rates = np.exp(np.arange(32) * (-2.0 * math.log(10000.0) / 64))
    angles = np.arange(SEQ)[:, None] * rates[None, :]
    cos, sin = np.cos(angles), np.sin(angles)
    cosine = np.concatenate([cos] * 4, axis=1).astype(np.float32)
    sine = np.concatenate([-sin, sin] * 2, axis=1).astype(np.float32)
    return cosine, sine


def swapped(t):
    lane = lax.broadcasted_iota(jnp.int32, t.shape, 1)
    return jnp.where((lane & 63) < 32, pltpu.roll(t, 96, 1), pltpu.roll(t, 32, 1))


def tile(p):
    return span(p, 128)


def low_half(shape):
    return lax.broadcasted_iota(jnp.int32, shape, 1) < 64


def spread_matrix():
    row = lax.broadcasted_iota(jnp.int32, (WIDTH, D), 0)
    col = lax.broadcasted_iota(jnp.int32, (WIDTH, D), 1)
    hit = (row == 15 * (col >> 4) + (col & 15)) & ((col & 15) < 15)
    return jnp.where(hit, 1.0, 0.0).astype(BF16)


def place():
    r, s = lax.axis_index("replica"), lax.axis_index("shard")
    return s // 16, (s // 4) % 4, ((s // 2) % 2) * 2 + r, s % 2


def device(x, y, z, c):
    return (z % 2, ((x * 4 + y) * 2 + z // 2) * 2 + c)


def peers():
    x, y, z, c = place()
    along = {
        "x": [device((x + d) % 4, y, z, c) for d in (1, 2, 3)],
        "y": [device(x, (y + d) % 4, z, c) for d in (1, 2, 3)],
        "z": [device(x, y, (z + d) % 4, c) for d in (1, 2, 3)],
    }
    return along, device(x, y, z, 1 - c)


def meet():
    along, other = peers()
    barrier = pltpu.get_barrier_semaphore()
    for d in (*along["x"], *along["y"], *along["z"], other):
        pl.semaphore_signal(barrier, inc=1, device_id=d, device_id_type=MESH)
    pl.semaphore_wait(barrier, 10)


def remote(src, dst, ss, rs, k, to):
    return pltpu.make_async_remote_copy(
        src_ref=src, dst_ref=dst, send_sem=ss.at[k], recv_sem=rs.at[k], device_id=to, device_id_type=MESH
    )


def parts(n):
    tiles = n // 256
    widths = [128 * (tiles // 3), 128 * (tiles // 3), 128 * (tiles - 2 * (tiles // 3))]
    return [(0, widths[0]), (2 * widths[0], widths[1]), (2 * widths[0] + 2 * widths[1], widths[2])]


def half_of(offset, width, k):
    return pl.ds(pl.multiple_of(offset + k * width, 128), width)


SEMS = 30
GATHER_ORDER = ("yxz", "zyx", "xzy")
SCATTER_ORDER = ("zxy", "xyz", "yzx")


class Gather:
    def __init__(self, own, full, ss, rs, n):
        x, y, z, c = place()
        zh, zl = z // 2, z % 2
        along, other = peers()
        self.local, self.stages = [], [[], [], []]
        k = 3
        for (off, w), order in zip(parts(n), GATHER_ORDER):
            mine = half_of(off, w, zl)
            self.local.append(pltpu.make_async_copy(own.at[:, mine], full.at[x, y, zh, c, :, mine], ss.at[len(self.local)]))
            for i, axis in enumerate(order):
                have = order[:i]
                every = slice(None)
                at = (
                    every if "x" in have else x,
                    every if "y" in have else y,
                    every if "z" in have else zh,
                    c,
                    every,
                    pl.ds(off, 2 * w) if "z" in have else mine,
                )
                for to in along[axis]:
                    src = own.at[:, mine] if i == 0 else full.at[at]
                    self.stages[i].append(remote(src, full.at[at], ss, rs, k, to))
                    k += 1
        w = full.at[:, :, :, c]
        self.core = remote(w, w, ss, rs, k, other)

    def move(self, done, begin):
        for d in done:
            d.wait()
        for d in begin:
            d.start()

    def follow(self, i):
        for k in range(0, 9, 3):
            self.move(self.stages[i][k : k + 3], self.stages[i + 1][k : k + 3])

    def s0(self):
        self.move([], self.local + self.stages[0])

    def s1(self):
        self.move(self.local, [])
        self.follow(0)

    def s2(self):
        self.follow(1)

    def s3(self):
        self.move(self.stages[2], [self.core])

    def s4(self):
        self.move([self.core], [])


def gather_sems():
    return [pltpu.SemaphoreType.DMA((SEMS + 1,)), pltpu.SemaphoreType.DMA((SEMS + 1,))]


def extent(left, w):
    return tuple([4] * ("x" in left) + [4] * ("y" in left) + [2] * ("z" in left) + [16, 2 * w if "z" in left else w])


def slot(left, axis, t, off, w):
    every = slice(None)
    cols = pl.ds(off, 2 * w) if "z" in left else every
    if axis == "z":
        cols = half_of(off, w, t % 2)
    at = [every] * ("x" in left) + [every] * ("y" in left) + [every] * ("z" in left)
    lead = [a for a in "xyz" if a in left]
    at[lead.index(axis)] = t // 2 if axis == "z" else t
    return (*at, every, cols)


LANDING, LOCAL = 13, 8


def landing(n):
    one, two, three = [], [], []
    for (_, w), order in zip(parts(n), SCATTER_ORDER):
        one.append(pltpu.VMEM((3, *extent(order[1:], w)), BF16))
        two.append(pltpu.VMEM((3, *extent(order[2:], w)), BF16))
        three.append(pltpu.VMEM((3, 16, w), F32))
    sems = [pltpu.SemaphoreType.DMA((SEMS,)), pltpu.SemaphoreType.DMA((SEMS,))]
    return [pltpu.VMEM((4, 4, 2, 16, n), BF16), *one, *two, *three, pltpu.VMEM((16, n // 2), F32), *sems]


def local(n):
    two, three = [], []
    for (_, w), order in zip(parts(n), SCATTER_ORDER):
        two.append(pltpu.VMEM(extent(order[1:], w), BF16))
        three.append(pltpu.VMEM(extent(order[2:], w), F32))
    return [pltpu.VMEM((4, 4, 2, 16, n), BF16), *two, *three, pltpu.VMEM((16, n // 2), F32)]


def within(loc, n):
    wide = lambda ref, w: ref.at[(*[slice(None)] * (len(ref.shape) - 1), pl.ds(0, w))]
    widths = [2 * w if "z" in order[i:] else w for i in (1, 2) for (_, w), order in zip(parts(n), SCATTER_ORDER)]
    return [wide(ref, w) for ref, w in zip(loc, [n, *widths, n // 2])]


class Scatter:
    def __init__(self, part, out, land, loc, n):
        x, y, z, c = place()
        self.own = part.at[:, :, :, c]
        self.at, self.out, self.parts = {"x": x, "y": y, "z": z}, out, parts(n)
        along, other = peers()
        self.r0, self.r4, ss, rs = land[0], *land[10:]
        self.p1, self.p4 = loc[0], loc[7]
        self.took = [land[1:4], land[4:7], land[7:10]]
        self.held = [[self.p1] * 3, loc[1:4], loc[4:7]]
        self.local = pltpu.make_async_copy(part.at[:, :, :, c], self.p1, ss.at[0])
        self.core = remote(part.at[:, :, :, 1 - c], self.r0, ss, rs, 1, other)
        self.sends, k = [[], [], []], 2
        for i in range(3):
            for q, order in enumerate(SCATTER_ORDER):
                for d in (1, 2, 3):
                    axis = order[i]
                    src = self.held[i][q].at[self.index(q, i, (self.at[axis] + d) % 4)]
                    self.sends[i].append(remote(src, self.took[i][q].at[d - 1], ss, rs, k, along[axis][d - 1]))
                    k += 1
        self.rep = remote(self.p4, self.r4, ss, rs, k, device(x, y, z + 1 - 2 * (z % 2), c))

    def index(self, q, i, t):
        off, w = self.parts[q]
        order = SCATTER_ORDER[q]
        return slot(order[i:], order[i], t, off if i == 0 else 0, w)

    def total(self, i, to):
        for q, order in enumerate(SCATTER_ORDER):
            own = self.held[i][q].at[self.index(q, i, self.at[order[i]])]
            took = self.took[i][q]
            lead = own.shape[:-2]

            def add(j, own=own, took=took, q=q):
                value = own[j].astype(F32)
                for k in range(3):
                    value += took[(k, *j)].astype(F32)
                to(q, j, value)

            if len(lead) == 2:

                def turn(a, _, add=add, lead=lead):
                    for b in range(lead[1]):
                        add((a, b))
                    return 0

                lax.fori_loop(0, lead[0], turn, 0)
            elif len(lead) == 1:
                for a in range(lead[0]):
                    add((a,))
            else:
                add(())

    def s0(self):
        self.local.start()
        self.core.start()

    def s1(self):
        self.local.wait()
        self.core.wait()
        self.merge(self.p1)

    def s0_vmem(self):
        self.core.start()

    def s1_vmem(self):
        self.core.wait()
        self.merge(self.own)

    def merge(self, own):
        def add(i, _):
            a, b = i // 4, i % 4
            self.p1[a, b] = (own[a, b].astype(F32) + self.r0[a, b].astype(F32)).astype(BF16)
            return 0

        lax.fori_loop(0, 16, add, 0)
        for d in self.sends[0]:
            d.start()

    def stage(self, i):
        for d in self.sends[i]:
            d.wait()

        def to(q, j, value):
            ref = self.held[i + 1][q]
            ref[j] = value.astype(ref.dtype)

        self.total(i, to)
        for d in self.sends[i + 1]:
            d.start()

    def s2(self):
        self.stage(0)

    def s3(self):
        self.stage(1)

    def s4(self):
        for d in self.sends[2]:
            d.wait()

        def to(q, j, value):
            off, w = self.parts[q]
            self.p4[:, off // 2 : off // 2 + w] = value

        self.total(2, to)
        self.rep.start()

    def s5(self):
        self.rep.wait()
        k = self.at["z"] % 2
        for off, w in self.parts:
            self.out[:, half_of(off, w, k)] = self.p4[:, off // 2 : off // 2 + w]
            self.out[:, half_of(off, w, 1 - k)] = self.r4[:, off // 2 : off // 2 + w]


def run(plan, i):
    for at, steps in plan.items():

        @pl.when(i == at)
        def _():
            for step in steps:
                step()


def attend_kernel(tok_hbm, cot_hbm, cos_ref, sin_ref, a, e0, e1, xp_ref, cp_ref, nrm_ref, qt_ref, ho_ref, lt_ref, gains_ref, fa, f0, f1,
                  tok, cot, spread, full, kx, vx, lse, bias, sem, *sems):
    meet()
    first = Gather(a, full, sems[0], sems[1], NA)
    c0, c1 = Gather(e0, f0, sems[2], sems[3], E0), Gather(e1, f1, sems[4], sems[5], E1)
    first.s0()
    reads = [pltpu.make_async_copy(tok_hbm, tok, sem.at[0]), pltpu.make_async_copy(cot_hbm, cot, sem.at[1])]
    for r in reads:
        r.start()
    spread[...] = spread_matrix()
    row = lax.broadcasted_iota(jnp.int32, (256, 256), 0)
    col = lax.broadcasted_iota(jnp.int32, (256, 256), 1)
    bias[...] = jnp.where(col <= row, 0.0, -1e30)
    ho_ref[...] = jnp.zeros_like(ho_ref)
    lse[...] = jnp.zeros_like(lse)
    first.s1()
    c0.s0()
    for r in reads:
        r.wait()

    def widen(src, to):
        def turn(i, _):
            r = span(i, 512)
            to[r, :] = dot_tn(src[:, r], spread[...]).astype(BF16)
            return 0

        lax.fori_loop(0, 2, turn, 0)

    widen(tok, xp_ref)
    first.s2()
    c0.s1()
    c1.s0()
    widen(cot, cp_ref)
    first.s3()
    c0.s2()
    c1.s1()
    first.s4()
    keep = pltpu.make_async_copy(full, fa, sem.at[0])
    keep.start()
    a_ref = full.reshape(D, NA)
    gains_ref[...] = jnp.transpose(a_ref[:, NQ - 128 : NQ].astype(F32))[64:72, :]
    gain = gains_ref[0:1, :]

    def project(i, _):
        r = span(i, 512)
        x = xp_ref[r, :].astype(F32)
        recip = lax.rsqrt(jnp.sum(x * x, axis=1, keepdims=True) * (1.0 / WIDTH) + EPS)
        normed = (x * recip * gain).astype(BF16)
        nrm_ref[r, :] = normed
        for at in range(0, NQ, 512):
            width = min(512, NQ - at)
            q = dot(normed, a_ref[:, at : at + width])
            for t in range(at, at + width, 128):
                v = q[:, t - at : t - at + 128]
                if t < 1280:
                    v = v * cos_ref[...] + swapped(v) * sin_ref[...]
                qt_ref[r, t : t + 128] = v.astype(BF16)
        run({0: [c1.s2]}, i)
        return 0

    lax.fori_loop(0, 2, project, 0)
    split_heads(qt_ref, kx, vx)

    def head(h, _):
        p, g = h // 2, h // 3
        u = 2 * g + h - 2 * p
        jobs = [(slice(SEQ * s + 256 * b, SEQ * s + 256 * b + 256), slice(SEQ * s, SEQ * s + 256 * b + 256)) for s in range(2) for b in range(2)]
        scores = [dot_nt(qt_ref[rows, tile(p)], kx[u, keys, :]) * (SCALE * LOG2E) for rows, keys in jobs]
        softs, stats = [], []
        for sc in scores:
            n = sc.shape[1]
            last = sc[:, n - 256 :] + bias[...]
            sc = last if n == 256 else jnp.concatenate([sc[:, : n - 256], last], axis=1)
            top = jnp.max(sc, axis=1, keepdims=True)
            ex = jnp.exp2(sc - top)
            total = jnp.sum(ex, axis=1, keepdims=True)
            softs.append((ex * (1.0 / total)).astype(BF16))
            stats.append(top + jnp.log2(total))
        outs = [dot(soft, vx[u, keys, :]) for soft, (_, keys) in zip(softs, jobs)]
        lane = lax.broadcasted_iota(jnp.int32, (256, 128), 1)
        for (rows, _), o, stat in zip(jobs, outs, stats):
            ho_ref[rows, tile(p)] = ho_ref[rows, tile(p)] + o.astype(BF16)
            lse[rows, :] = jnp.where(lane == h, stat, lse[rows, :])
        run({1: [c0.s3], 10: [c1.s3], 12: [c0.s4]}, h)
        return 0

    lax.fori_loop(0, 15, head, 0)
    lt_ref[...] = jnp.transpose(lse[...])[:16, :].reshape(16, 1, T)
    keep.wait()
    c1.s4()


def split_heads(qt_ref, kx, vx):
    low = low_half((T, 128))
    for g in range(5):
        for to, unit in ((kx, 15 + g), (vx, 20 + g)):
            at = 128 * (unit // 2)
            v = qt_ref[:, at : at + 128].astype(F32)
            turned = pltpu.roll(v, 64, 1)
            at_low, at_high = (v, turned) if unit % 2 == 0 else (turned, v)
            to[2 * g] = jnp.where(low, at_low, 0.0).astype(BF16)
            to[2 * g + 1] = jnp.where(low, 0.0, at_high).astype(BF16)


def attend(tok, cot, cosine, sine, a, e0, e1):
    shape = jax.ShapeDtypeStruct
    return pl.pallas_call(
        attend_kernel,
        out_shape=[
            shape((T, D), BF16),
            shape((T, D), BF16),
            shape((T, D), BF16),
            shape((T, NQ), BF16),
            shape((T, D), BF16),
            shape((16, 1, T), F32),
            shape((8, D), F32),
            shape((4, 4, 2, 2, 16, NA), BF16),
            shape((4, 4, 2, 2, 16, E0), BF16),
            shape((4, 4, 2, 2, 16, E1), BF16),
        ],
        in_specs=[ANY] * 2 + [VMEM] * 2 + [ANY] * 3,
        out_specs=[VMEM] * 7 + [ANY] * 3,
        scratch_shapes=[
            pltpu.VMEM((WIDTH, T), BF16),
            pltpu.VMEM((WIDTH, T), BF16),
            pltpu.VMEM((WIDTH, D), BF16),
            pltpu.VMEM((4, 4, 2, 2, 16, NA), BF16),
            pltpu.VMEM((10, T, 128), BF16),
            pltpu.VMEM((10, T, 128), BF16),
            pltpu.VMEM((T, 128), F32),
            pltpu.VMEM((256, 256), F32),
            pltpu.SemaphoreType.DMA((2,)),
            *gather_sems() * 3,
        ],
        compiler_params=pltpu.CompilerParams(collective_id=0, has_side_effects=True, vmem_limit_bytes=VLIM),
        name="attend",
    )(tok, cot, cosine, sine, a, e0, e1)


def ffn_kernel(xp, cp, gains, ho, f0, f1, c_own, hid, gheads_ref, gnorm_ref, oc_ref, outp_hbm, gl_hbm, fc,
               b_full, acc, gacc, nrm, w, act, ggu, stage, wsem, gsem, *scratch):
    meet()
    gather = Gather(c_own, fc, scratch[0], scratch[1], NL)
    lands, loc = scratch[2 : 2 + LANDING], scratch[2 + LANDING :]
    reduction = lambda j: Scatter(stage, oc_ref.at[j], [ref.at[j] for ref in lands], loc, NC)
    gain = gains[1:2, :]
    get_b = pltpu.make_async_copy(f0.at[:, :, :, :, :, :NB], b_full, gsem)
    get_b.start()

    def fetch(b, begin):
        slot = jnp.asarray(b) % 2

        @pl.when(b == 0)
        def _():
            d = pltpu.make_async_copy(f0.at[:, :, :, :, :, NB:], w.at[slot], wsem.at[slot])
            d.start() if begin else d.wait()

        @pl.when((b > 0) & (b < EARLY))
        def _():
            cols = pl.ds(pl.multiple_of(NC * jnp.clip(b - 1, 0, EARLY - 2), 128), NC)
            d = pltpu.make_async_copy(f1.at[:, :, :, :, :, cols], w.at[slot], wsem.at[slot])
            d.start() if begin else d.wait()

        @pl.when(b >= EARLY)
        def _():
            cols = pl.ds(pl.multiple_of(NC * jnp.maximum(b - EARLY, 0), 128), NC)
            d = pltpu.make_async_copy(fc.at[:, :, :, :, :, cols], w.at[slot], wsem.at[slot])
            d.start() if begin else d.wait()

    gather.s0()
    fetch(0, True)
    get_b.wait()
    b_ref = b_full.reshape(D, NB)

    def first(i, _):
        r = span(i, 512)
        h = xp[r, :].astype(F32) + dot_nt(ho[r, :], b_ref[...])
        hid[r, :] = h
        acc[r, :] = h
        recip = lax.rsqrt(jnp.sum(h * h, axis=1, keepdims=True) * (1.0 / WIDTH) + EPS)
        nrm[r, :] = (h * recip * gain).astype(BF16)
        gacc[r, :] = jnp.zeros((512, D), F32)
        run({0: [gather.s1], 1: [gather.s2]}, i)
        return 0

    lax.fori_loop(0, 2, first, 0)

    def when_chunk(b, ahead, name):
        @pl.when((b >= ahead) & (b < ahead + EARLY))
        def _():
            getattr(reduction(b - ahead), name)()

    def block(b, _):
        wv = w.at[b % 2].reshape(D, NC)
        fetch(b, False)

        @pl.when(b < BLOCKS - 1)
        def _():
            fetch(b + 1, True)

        when_chunk(b, 1, "s0_vmem")
        when_chunk(b, 3, "s3")
        when_chunk(b, 4, "s5")

        @pl.when(b == 1)
        def _():
            gather.s3()

        def rows(i, _):
            r = span(i, 512)
            pre = dot(nrm[r, :], wv[:, : 2 * FB])
            ga = dot(cp[r, :], wv[:, 2 * FB :])
            gate, up = pre[:, :FB], pre[:, FB:]
            sig = 0.5 * jnp.tanh(0.5 * gate) + 0.5
            silu = gate * sig
            act_b = (silu * up).astype(BF16)
            act[r, :] = act_b
            ggu[r, :FB] = (ga * up * (sig + silu * (1.0 - sig))).astype(BF16)
            ggu[r, FB:] = (ga * silu).astype(BF16)
            acc[r, :] += dot_nt(act_b, wv[:, 2 * FB :])
            gacc[r, :] += dot_nt(ggu[r, :], wv[:, : 2 * FB])
            return 0

        lax.fori_loop(0, 2, rows, 0)
        when_chunk(b, 2, "s2")
        when_chunk(b, 1, "s1_vmem")
        when_chunk(b, 3, "s4")

        @pl.when(b == 1)
        def _():
            gather.s4()

        @pl.when(b == BLOCKS - 1)
        def _():
            pltpu.make_async_copy(stage, gl_hbm.at[:, :, :, :, :, :NC], gsem).wait()

        def weights(i, _):
            r = span(i, 512)
            k = pl.ds(pl.multiple_of(2 * i, 2), 2)
            to = lambda v: v.astype(BF16).reshape(2, 4, 2, 2, 16, v.shape[1])
            stage[k, :, :, :, :, : 2 * FB] = to(dot_tn(nrm[:, r], ggu[...]))
            stage[k, :, :, :, :, 2 * FB :] = to(dot_tn(cp[:, r], act[...]))
            return 0

        lax.fori_loop(0, 2, weights, 0)

        @pl.when(b >= EARLY)
        def _():
            cols = pl.ds(pl.multiple_of(NC * jnp.maximum(b - EARLY, 0), 128), NC)
            pltpu.make_async_copy(stage, gl_hbm.at[:, :, :, :, :, cols], gsem).start()

        return 0

    lax.fori_loop(0, BLOCKS, block, 0)
    reduction(1).s5()
    reduction(2).s3()
    gnorm_ref[...] = jnp.zeros_like(gnorm_ref)
    out_stage = w.at[0].reshape(D, NC).at[:, :D]

    def last(i, _):
        r = span(i, 256)
        out_stage[r, :] = acc[r, :].astype(BF16)
        h, gn = hid[r, :], gacc[r, :]
        recip = lax.rsqrt(jnp.sum(h * h, axis=1, keepdims=True) * (1.0 / WIDTH) + EPS)
        gnorm_ref[...] += jnp.sum(gn * h * recip, axis=0, keepdims=True)
        scaled = gn * gain
        mean = jnp.sum(scaled * h, axis=1, keepdims=True) * (1.0 / WIDTH)
        gh = cp[r, :].astype(F32) + recip * scaled - h * (recip * recip * recip * mean)
        hid[r, :] = gh
        nrm[r, :] = gh.astype(BF16)
        return 0

    lax.fori_loop(0, 4, last, 0)
    reduction(2).s4()
    put_out = pltpu.make_async_copy(out_stage, outp_hbm, wsem.at[0])
    put_out.start()
    pltpu.make_async_copy(stage, gl_hbm.at[:, :, :, :, :, :NC], gsem).wait()

    def out_grad(i, _):
        r = span(i, 512)
        k = pl.ds(pl.multiple_of(2 * i, 2), 2)
        stage[k, :, :, :, :, :NB] = dot_tn(nrm[:, r], ho[...]).astype(BF16).reshape(2, 4, 2, 2, 16, NB)
        return 0

    lax.fori_loop(0, 2, out_grad, 0)
    put_gb = pltpu.make_async_copy(stage.at[:, :, :, :, :, :NB], gl_hbm.at[:, :, :, :, :, NL:], gsem)
    put_gb.start()

    def heads(i, _):
        r = span(i, 512)
        gheads_ref[r, :] = dot(nrm[r, :], b_ref[...]).astype(BF16)
        return 0

    lax.fori_loop(0, 2, heads, 0)
    reduction(2).s5()
    put_out.wait()
    put_gb.wait()


def many(shapes, k):
    vmem = lambda s: pltpu.VMEM((k, *s.shape), s.dtype)
    return [vmem(s) if i < len(shapes) - 2 else pltpu.SemaphoreType.DMA((k, SEMS)) for i, s in enumerate(shapes)]


def ffn(xp, cp, gains, ho, f0, f1, c_own):
    shape = jax.ShapeDtypeStruct
    return pl.pallas_call(
        ffn_kernel,
        out_shape=[
            shape((T, D), F32),
            shape((T, D), BF16),
            shape((1, D), F32),
            shape((EARLY, 16, NC), F32),
            shape((T, D), BF16),
            shape((4, 4, 2, 2, 16, NL + NB), BF16),
            shape((4, 4, 2, 2, 16, NL), BF16),
        ],
        in_specs=[VMEM] * 4 + [ANY] * 3,
        out_specs=[VMEM] * 4 + [ANY] * 3,
        scratch_shapes=[
            pltpu.VMEM((4, 4, 2, 2, 16, NB), BF16),
            pltpu.VMEM((T, D), F32),
            pltpu.VMEM((T, D), F32),
            pltpu.VMEM((T, D), BF16),
            pltpu.VMEM((2, 4, 4, 2, 2, 16, NC), BF16),
            pltpu.VMEM((T, FB), BF16),
            pltpu.VMEM((T, 2 * FB), BF16),
            pltpu.VMEM((4, 4, 2, 2, 16, NC), BF16),
            pltpu.SemaphoreType.DMA((2,)),
            pltpu.SemaphoreType.DMA,
            *gather_sems(),
            *many(landing(NC), EARLY),
            *local(NC),
        ],
        compiler_params=pltpu.CompilerParams(collective_id=1, has_side_effects=True, vmem_limit_bytes=VLIM),
        name="ffn",
    )(xp, cp, gains, ho, f0, f1, c_own)


def back_kernel(qt_ref, ho_ref, gheads_ref, lt_ref, cos_ref, sin_ref, gains, nrm, xp, gnf, gl, fa, gh_hbm, outp_hbm,
                o0_ref, o1_ref, oa0_ref, oa1_ref, gtok_hbm, out_hbm, full, dt_ref, gsum, cols_ref, isem, osem, *scratch):
    meet()
    chunks, at = [], 0
    sources = [(gl.at[:, :, :, :, :, :L0], o0_ref, L0), (gl.at[:, :, :, :, :, L0:], o1_ref, L1)]
    k = LANDING + LOCAL
    for i, (src, out, n) in enumerate(sources):
        chunks.append(Scatter(src, out, scratch[k * i : k * i + LANDING], scratch[k * i + LANDING : k * i + k], n))
    c0, c1 = chunks
    loc0, loc1 = scratch[LANDING:k], scratch[k + LANDING : 2 * k]
    scratch = scratch[2 * k :]
    c0.s0()
    c1.s0()
    get_a = pltpu.make_async_copy(fa, full, isem.at[0])
    get_a.start()

    def phase_one(kx, vx, dq, dk, dv, bias):
        split_heads(qt_ref, kx, vx)
        dq[...] = jnp.zeros_like(dq)
        dk[...] = jnp.zeros_like(dk)
        dv[...] = jnp.zeros_like(dv)
        row = lax.broadcasted_iota(jnp.int32, (256, 256), 0)
        col = lax.broadcasted_iota(jnp.int32, (256, 256), 1)
        bias[...] = jnp.where(row <= col, 0.0, -1e30)

        def head(h, _):
            p, g = h // 2, h // 3
            par = h - 2 * p
            u = 2 * g + par
            lane = lax.broadcasted_iota(jnp.int32, (SEQ, 128), 1)
            own = (lane // 64) == par
            ones = jnp.ones((8, 128), BF16)
            c = SCALE * LOG2E
            for s in range(2):
                seq = slice(SEQ * s, SEQ * s + SEQ)
                q, do = qt_ref[seq, tile(p)], gheads_ref[seq, tile(p)]
                q_own = jnp.where(own, q, jnp.zeros_like(q))
                do_own = jnp.where(own, do, jnp.zeros_like(do))
                prod = do_own.astype(F32) * ho_ref[seq, tile(p)].astype(F32)
                high = prod.astype(BF16)
                rest = (prod - high.astype(F32)).astype(BF16)
                off = (dot_nt(ones, high) + dot_nt(ones, rest))[:1, :]
                lse = lt_ref[h, :, seq]
                k0, k1 = kx[u, SEQ * s : SEQ * s + 256, :], kx[u, SEQ * s + 256 : SEQ * s + 512, :]
                v0, v1 = vx[u, SEQ * s : SEQ * s + 256, :], vx[u, SEQ * s + 256 : SEQ * s + 512, :]
                st0, st1 = dot_nt(k0, q), dot_nt(k1, q[256:])
                gp0, gp1 = dot_nt(v0, do), dot_nt(v1, do[256:])
                t0 = st0 * c - lse
                e0 = jnp.exp2(jnp.concatenate([t0[:, :256] + bias[...], t0[:, 256:]], axis=1))
                e1 = jnp.exp2(st1 * c - lse[:, 256:] + bias[...])
                ds0 = (e0 * (gp0 - off)).astype(BF16)
                ds1 = (e1 * (gp1 - off[:, 256:])).astype(BF16)
                dv0, dv1 = dot(e0.astype(BF16), do_own), dot(e1.astype(BF16), do_own[256:])
                dk0, dk1 = dot(ds0, q_own), dot(ds1, q_own[256:])
                dq0 = dot_tn(ds0, k0)
                dq1 = dot_tn(ds1, k1)
                lo, hi = slice(SEQ * s, SEQ * s + 256), slice(SEQ * s + 256, SEQ * s + 512)
                dv[g, lo, :] += dv0
                dv[g, hi, :] += dv1
                dk[g, lo, :] += dk0
                dk[g, hi, :] += dk1
                dq[p, lo, :] += dq0[:256]
                dq[p, hi, :] += dq0[256:] + dq1
            run({1: [c0.s1], 3: [c1.s1], 6: [c0.s2], 8: [c0.s3], 9: [c1.s2], 10: [c0.s4], 11: [c1.s3], 12: [c0.s5], 13: [c1.s4]}, h)
            return 0

        lax.fori_loop(0, 15, head, 0)

        def finish(i, _):
            r = span(i, 256)
            half = span(i % 2, 256)
            cosine, sine = cos_ref[half, :], sin_ref[half, :]
            low = low_half((256, 128))
            fold = lambda ref, g: ref[g, r, :] + pltpu.roll(ref[g, r, :], 64, 1)
            tiles = [dq[p, r, :] for p in range(7)]
            tiles.append(jnp.where(low, dq[7, r, :], fold(dk, 0)))
            tiles.append(jnp.where(low, fold(dk, 1), fold(dk, 2)))
            tiles.append(jnp.where(low, fold(dk, 3), fold(dk, 4)))
            for t, v in enumerate(tiles):
                v = v * SCALE
                dt_ref[r, 128 * t : 128 * t + 128] = (v * cosine - swapped(v) * sine).astype(BF16)
            dt_ref[r, 1280:1408] = jnp.where(low, fold(dv, 0), fold(dv, 1)).astype(BF16)
            dt_ref[r, 1408:1536] = jnp.where(low, fold(dv, 2), fold(dv, 3)).astype(BF16)
            dt_ref[r, 1536:1664] = jnp.where(low, fold(dv, 4), 0.0).astype(BF16)
            return 0

        lax.fori_loop(0, 4, finish, 0)

    pl.run_scoped(
        phase_one,
        pltpu.VMEM((10, T, 128), BF16),
        pltpu.VMEM((10, T, 128), BF16),
        pltpu.VMEM((8, T, 128), F32),
        pltpu.VMEM((5, T, 128), F32),
        pltpu.VMEM((5, T, 128), F32),
        pltpu.VMEM((256, 256), F32),
    )
    get_a.wait()
    a_ref = full.reshape(D, NA)
    gain = gains[0:1, :]
    gsum[...] = jnp.zeros_like(gsum)
    gsum[1:2, :] = gnf[...]

    def phase_two(gn_ref, gtok, out, spread, gh, outp, ga0, ga1):
        get_gh = lambda i: pltpu.make_async_copy(gh_hbm.at[span(i, 256), :], gh.at[i % 2], isem.at[i % 2])
        get_out = pltpu.make_async_copy(outp_hbm, outp, osem.at[0])
        get_gh(0).start()
        get_out.start()
        d0 = Scatter(ga0, oa0_ref, scratch[:LANDING], within(loc0, A0), A0)
        d1 = Scatter(ga1, oa1_ref, scratch[LANDING:], within(loc1, A1), A1)
        to = lambda v: v.astype(BF16).reshape(2, 4, 2, 2, 16, v.shape[1])

        def weights0(i, _):
            ga0[pl.ds(pl.multiple_of(2 * i, 2), 2)] = to(dot_tn(nrm[:, span(i, 512)], dt_ref[:, :A0]))
            return 0

        lax.fori_loop(0, 2, weights0, 0)
        d0.s0_vmem()
        c1.s5()

        def normed(i, _):
            r = span(i, 512)
            gn = dot_nt(dt_ref[r, :], a_ref[:, :NQ])
            gn_ref[r, :] = gn
            x = xp[r, :].astype(F32)
            recip = lax.rsqrt(jnp.sum(x * x, axis=1, keepdims=True) * (1.0 / WIDTH) + EPS)
            gsum[0:1, :] += jnp.sum(gn * x * recip, axis=0, keepdims=True)
            run({1: [d0.s1_vmem]}, i)
            return 0

        lax.fori_loop(0, 2, normed, 0)
        cols = jnp.transpose(jnp.concatenate([gsum[...], jnp.zeros((120, D), F32)], axis=0))
        cols_ref[...] = pltpu.roll(cols, 64, 1)

        def weights1(i, _):
            r = span(i, 512)
            kk = pl.ds(pl.multiple_of(2 * i, 2), 2)
            g = dot_tn(nrm[:, r], dt_ref[:, A0:])
            edge = jnp.where(low_half((512, 128)), g[:, NQ - A0 - 128 :], cols_ref[r, :])
            ga1[kk, :, :, :, :, : NQ - A0 - 128] = to(g[:, : NQ - A0 - 128])
            ga1[kk, :, :, :, :, NQ - A0 - 128 : NQ - A0] = to(edge)
            ga1[kk, :, :, :, :, NQ - A0 :] = jnp.zeros((2, 4, 2, 2, 16, NA - NQ), BF16)
            return 0

        lax.fori_loop(0, 2, weights1, 0)
        d1.s0_vmem()
        spread[...] = spread_matrix()
        get_out.wait()
        d0.s2()
        d1.s1_vmem()

        def tokens(i, _):
            r = span(i, 256)
            get_gh(i).wait()

            @pl.when(i < 3)
            def _():
                get_gh(i + 1).start()

            x = xp[r, :].astype(F32)
            recip = lax.rsqrt(jnp.sum(x * x, axis=1, keepdims=True) * (1.0 / WIDTH) + EPS)
            scaled = gn_ref[r, :] * gain
            mean = jnp.sum(scaled * x, axis=1, keepdims=True) * (1.0 / WIDTH)
            gt = gh[i % 2] + recip * scaled - x * (recip * recip * recip * mean)
            high = gt.astype(BF16)
            mid = (gt - high.astype(F32)).astype(BF16)
            gtok[:, r] = dot_nt(spread[...], high) + dot_nt(spread[...], mid)
            out[:, r] = dot_nt(spread[...], outp[r, :]).astype(BF16)
            run({0: [d0.s3], 1: [d0.s4], 2: [d1.s2, d0.s5], 3: [d1.s3]}, i)
            return 0

        lax.fori_loop(0, 4, tokens, 0)
        puts = [pltpu.make_async_copy(gtok, gtok_hbm, osem.at[0]), pltpu.make_async_copy(out, out_hbm, osem.at[1])]
        for p in puts:
            p.start()
        d1.s4()
        d1.s5()
        for p in puts:
            p.wait()

    pl.run_scoped(
        phase_two,
        pltpu.VMEM((T, D), F32),
        pltpu.VMEM((WIDTH, T), F32),
        pltpu.VMEM((WIDTH, T), BF16),
        pltpu.VMEM((WIDTH, D), BF16),
        pltpu.VMEM((2, 256, D), F32),
        pltpu.VMEM((T, D), BF16),
        pltpu.VMEM((4, 4, 2, 2, 16, A0), BF16),
        pltpu.VMEM((4, 4, 2, 2, 16, A1), BF16),
    )


def back(qt, ho, gheads, lt, cosine, sine, gains, nrm, xp, gnf, gl, fa, gh, outp):
    shape = jax.ShapeDtypeStruct
    return pl.pallas_call(
        back_kernel,
        out_shape=[
            shape((16, L0), F32),
            shape((16, L1), F32),
            shape((16, A0), F32),
            shape((16, A1), F32),
            shape((WIDTH, T), F32),
            shape((WIDTH, T), BF16),
        ],
        in_specs=[VMEM] * 10 + [ANY] * 4,
        out_specs=[VMEM] * 4 + [ANY] * 2,
        scratch_shapes=[
            pltpu.VMEM((4, 4, 2, 2, 16, NA), BF16),
            pltpu.VMEM((T, NQ), BF16),
            pltpu.VMEM((8, D), F32),
            pltpu.VMEM((D, 128), F32),
            pltpu.SemaphoreType.DMA((2,)),
            pltpu.SemaphoreType.DMA((2,)),
            *landing(L0),
            *local(L0),
            *landing(L1),
            *local(L1),
            *landing(A0),
            *landing(A1),
        ],
        compiler_params=pltpu.CompilerParams(collective_id=2, has_side_effects=True, vmem_limit_bytes=VLIM),
        name="back",
    )(qt, ho, gheads, lt, cosine, sine, gains, nrm, xp, gnf, gl, fa, gh, outp)


def shards(tokens, cotangent, wq, wk, wv, w_gate, w_up, wo, w_down, norm_attn, norm_ffn):
    pad = lambda a, n: jnp.pad(a, ((0, 1), (0, n - a.shape[1])))
    a = pad(jnp.concatenate([wq, wk, wv, norm_attn[:, None], norm_ffn[:, None]], axis=1), NA)
    down = w_down.T
    blocks = [jnp.concatenate([w[:, FB * i : FB * i + FB] for w in (w_gate, w_up, down)], axis=1) for i in range(BLOCKS)]
    e0 = pad(jnp.concatenate([jnp.pad(wo.T, ((0, 0), (0, NB - WIDTH))), blocks[0]], axis=1), E0)
    e1 = pad(jnp.concatenate(blocks[1:EARLY], axis=1), E1)
    late = pad(jnp.concatenate(blocks[EARLY:], axis=1), NL)
    cosine, sine = rope_tables()
    xp, cp, nrm, qt, ho, lt, gains, fa, f0, f1 = attend(tokens.T, cotangent.T, cosine, sine, a, e0, e1)
    gh, gheads, gnf, early, outp, gl, _ = ffn(xp, cp, gains, ho, f0, f1, late)
    l0, l1, a0, a1, grad_tokens, output = back(qt, ho, gheads, lt, cosine, sine, gains, nrm, xp, gnf, gl, fa, gh, outp)
    sa = jnp.concatenate([a0, a1], axis=1)
    left = jnp.concatenate([l0, l1], axis=1)[:15]
    pieces = [early[i, :15] for i in range(EARLY)] + [left[:, NC * i : NC * i + NC] for i in range(BLOCKS - EARLY)]
    join = lambda k: jnp.concatenate([v[:, FB * k : FB * k + FB] for v in pieces], axis=1)
    return (
        output.T,
        grad_tokens.T,
        sa[:15, :960],
        sa[:15, 960:1280],
        sa[:15, 1280:1600],
        join(0),
        join(1),
        left[:, NL : NL + WIDTH].T,
        join(2).T,
        sa[:15, 1600],
        sa[:15, 1601],
    )


def solution(mesh):
    rows = P(("replica", "shard"), None)
    first, second, one = P("shard", None), P(None, "shard"), P("shard")
    in_specs = (rows, rows, first, first, first, first, first, second, second, one, one)
    out_specs = (rows, rows, first, first, first, first, first, second, second, one, one)
    return jax.shard_map(shards, mesh=mesh, in_specs=in_specs, out_specs=out_specs, check_vma=False)
```

```python
import functools
import math

import jax
import jax.numpy as jnp
import numpy as np
from jax import lax
from jax.experimental import pallas as pl
from jax.experimental.pallas import tpu as pltpu
from jax.sharding import PartitionSpec as P

F32, BF16 = jnp.float32, jnp.bfloat16
MESH = pl.DeviceIdType.MESH
ANY = pl.BlockSpec(memory_space=pl.ANY)
VMEM = pl.BlockSpec(memory_space=pltpu.VMEM)
WIDTH = 960
D = 1024
T = 1024
SEQ = 512
K_UNIT, V_UNIT = 16, 22
NA, NB, NC, BLOCKS, FB = 1792, 1024, 1536, 5, 512
AHEAD = 2
EARLY = 3
NL = (BLOCKS - EARLY) * NC
L0 = 2304
L1 = NL + NB - L0
E0, E1 = NB + NC, NC
F0, F1 = NC, 2 * NC
A0 = 1024
A1 = NA - A0
EPS = 1e-05
SCALE = 0.125
LOG2E = math.log2(math.e)
VLIM = 60 * 1024 * 1024


def dot(a, b):
    return lax.dot_general(a, b, (((1,), (0,)), ((), ())), preferred_element_type=F32)


def dot_nt(a, b):
    return lax.dot_general(a, b, (((1,), (1,)), ((), ())), preferred_element_type=F32)


def dot_tn(a, b):
    return lax.dot_general(a, b, (((0,), (0,)), ((), ())), preferred_element_type=F32)


def span(i, n):
    return pl.ds(pl.multiple_of(i * n, n), n)


def rope_tables():
    rates = np.exp(np.arange(32) * (-2.0 * math.log(10000.0) / 64))
    angles = np.arange(SEQ)[:, None] * rates[None, :]
    cos, sin = np.cos(angles), np.sin(angles)
    cosine = np.concatenate([cos] * 4, axis=1).astype(np.float32)
    sine = np.concatenate([-sin, sin] * 2, axis=1).astype(np.float32)
    return cosine, sine


def swapped(t):
    lane = lax.broadcasted_iota(jnp.int32, t.shape, 1)
    return jnp.where((lane & 63) < 32, pltpu.roll(t, 96, 1), pltpu.roll(t, 32, 1))


def tile(p):
    return span(p, 128)


def low_half(shape):
    return lax.broadcasted_iota(jnp.int32, shape, 1) < 64


def spread_matrix():
    row = lax.broadcasted_iota(jnp.int32, (WIDTH, D), 0)
    col = lax.broadcasted_iota(jnp.int32, (WIDTH, D), 1)
    hit = (row == 15 * (col >> 4) + (col & 15)) & ((col & 15) < 15)
    return jnp.where(hit, 1.0, 0.0).astype(BF16)


def place():
    r, s = lax.axis_index("replica"), lax.axis_index("shard")
    return s // 16, (s // 4) % 4, ((s // 2) % 2) * 2 + r, s % 2


def device(x, y, z, c):
    return (z % 2, ((x * 4 + y) * 2 + z // 2) * 2 + c)


def peers():
    x, y, z, c = place()
    along = {
        "x": [device((x + d) % 4, y, z, c) for d in (1, 2, 3)],
        "y": [device(x, (y + d) % 4, z, c) for d in (1, 2, 3)],
        "z": [device(x, y, (z + d) % 4, c) for d in (1, 2, 3)],
    }
    return along, device(x, y, z, 1 - c)


def meet():
    along, other = peers()
    barrier = pltpu.get_barrier_semaphore()
    for d in (*along["x"], *along["y"], *along["z"], other):
        pl.semaphore_signal(barrier, inc=1, device_id=d, device_id_type=MESH)
    pl.semaphore_wait(barrier, 10)


def remote(src, dst, ss, rs, k, to):
    return pltpu.make_async_remote_copy(
        src_ref=src, dst_ref=dst, send_sem=ss.at[k], recv_sem=rs.at[k], device_id=to, device_id_type=MESH
    )


def parts(n):
    tiles = n // 256
    widths = [128 * (tiles // 3), 128 * (tiles // 3), 128 * (tiles - 2 * (tiles // 3))]
    return [(0, widths[0]), (2 * widths[0], widths[1]), (2 * widths[0] + 2 * widths[1], widths[2])]


def half_of(offset, width, k):
    return pl.ds(pl.multiple_of(offset + k * width, 128), width)


SEMS = 30
GATHER_ORDER = ("yxz", "zyx", "xzy")
SCATTER_ORDER = ("zxy", "xyz", "yzx")


class Gather:
    def __init__(self, own, full, ss, rs, n):
        x, y, z, c = place()
        zh, zl = z // 2, z % 2
        along, other = peers()
        self.local, self.stages = [], [[], [], []]
        k = 3
        for (off, w), order in zip(parts(n), GATHER_ORDER):
            mine = half_of(off, w, zl)
            self.local.append(pltpu.make_async_copy(own.at[:, mine], full.at[x, y, zh, c, :, mine], ss.at[len(self.local)]))
            for i, axis in enumerate(order):
                have = order[:i]
                every = slice(None)
                at = (
                    every if "x" in have else x,
                    every if "y" in have else y,
                    every if "z" in have else zh,
                    c,
                    every,
                    pl.ds(off, 2 * w) if "z" in have else mine,
                )
                for to in along[axis]:
                    src = own.at[:, mine] if i == 0 else full.at[at]
                    self.stages[i].append(remote(src, full.at[at], ss, rs, k, to))
                    k += 1
        w = full.at[:, :, :, c]
        self.core = remote(w, w, ss, rs, k, other)

    def move(self, done, begin):
        for d in done:
            d.wait()
        for d in begin:
            d.start()

    def follow(self, i):
        for k in range(0, 9, 3):
            self.move(self.stages[i][k : k + 3], self.stages[i + 1][k : k + 3])

    def s0(self):
        self.move([], self.local + self.stages[0])

    def s1(self):
        self.move(self.local, [])
        self.follow(0)

    def s2(self):
        self.follow(1)

    def s3(self):
        self.move(self.stages[2], [self.core])

    def s4(self):
        self.move([self.core], [])


def gather_sems():
    return [pltpu.SemaphoreType.DMA((SEMS + 1,)), pltpu.SemaphoreType.DMA((SEMS + 1,))]


def extent(left, w):
    return tuple([4] * ("x" in left) + [4] * ("y" in left) + [2] * ("z" in left) + [16, 2 * w if "z" in left else w])


def slot(left, axis, t, off, w):
    every = slice(None)
    cols = pl.ds(off, 2 * w) if "z" in left else every
    if axis == "z":
        cols = half_of(off, w, t % 2)
    at = [every] * ("x" in left) + [every] * ("y" in left) + [every] * ("z" in left)
    lead = [a for a in "xyz" if a in left]
    at[lead.index(axis)] = t // 2 if axis == "z" else t
    return (*at, every, cols)


LANDING, LOCAL = 13, 8


def landing(n):
    one, two, three = [], [], []
    for (_, w), order in zip(parts(n), SCATTER_ORDER):
        one.append(pltpu.VMEM((3, *extent(order[1:], w)), BF16))
        two.append(pltpu.VMEM((3, *extent(order[2:], w)), BF16))
        three.append(pltpu.VMEM((3, 16, w), F32))
    sems = [pltpu.SemaphoreType.DMA((SEMS,)), pltpu.SemaphoreType.DMA((SEMS,))]
    return [pltpu.VMEM((4, 4, 2, 16, n), BF16), *one, *two, *three, pltpu.VMEM((16, n // 2), F32), *sems]


def local(n):
    two, three = [], []
    for (_, w), order in zip(parts(n), SCATTER_ORDER):
        two.append(pltpu.VMEM(extent(order[1:], w), BF16))
        three.append(pltpu.VMEM(extent(order[2:], w), F32))
    return [pltpu.VMEM((4, 4, 2, 16, n), BF16), *two, *three, pltpu.VMEM((16, n // 2), F32)]


def within(loc, n):
    wide = lambda ref, w: ref.at[(*[slice(None)] * (len(ref.shape) - 1), pl.ds(0, w))]
    widths = [2 * w if "z" in order[i:] else w for i in (1, 2) for (_, w), order in zip(parts(n), SCATTER_ORDER)]
    return [wide(ref, w) for ref, w in zip(loc, [n, *widths, n // 2])]


class Scatter:
    def __init__(self, part, out, land, loc, n):
        x, y, z, c = place()
        self.own = part.at[:, :, :, c]
        self.at, self.out, self.parts = {"x": x, "y": y, "z": z}, out, parts(n)
        along, other = peers()
        self.r0, self.r4, ss, rs = land[0], *land[10:]
        self.p1, self.p4 = loc[0], loc[7]
        self.took = [land[1:4], land[4:7], land[7:10]]
        self.held = [[self.p1] * 3, loc[1:4], loc[4:7]]
        self.local = pltpu.make_async_copy(part.at[:, :, :, c], self.p1, ss.at[0])
        self.core = remote(part.at[:, :, :, 1 - c], self.r0, ss, rs, 1, other)
        self.sends, k = [[], [], []], 2
        for i in range(3):
            for q, order in enumerate(SCATTER_ORDER):
                for d in (1, 2, 3):
                    axis = order[i]
                    src = self.held[i][q].at[self.index(q, i, (self.at[axis] + d) % 4)]
                    self.sends[i].append(remote(src, self.took[i][q].at[d - 1], ss, rs, k, along[axis][d - 1]))
                    k += 1
        self.rep = remote(self.p4, self.r4, ss, rs, k, device(x, y, z + 1 - 2 * (z % 2), c))

    def index(self, q, i, t):
        off, w = self.parts[q]
        order = SCATTER_ORDER[q]
        return slot(order[i:], order[i], t, off if i == 0 else 0, w)

    def total(self, i, to):
        for q, order in enumerate(SCATTER_ORDER):
            own = self.held[i][q].at[self.index(q, i, self.at[order[i]])]
            took = self.took[i][q]
            lead = own.shape[:-2]

            def add(j, own=own, took=took, q=q):
                value = own[j].astype(F32)
                for k in range(3):
                    value += took[(k, *j)].astype(F32)
                to(q, j, value)

            if len(lead) == 2:

                def turn(a, _, add=add, lead=lead):
                    for b in range(lead[1]):
                        add((a, b))
                    return 0

                lax.fori_loop(0, lead[0], turn, 0)
            elif len(lead) == 1:
                for a in range(lead[0]):
                    add((a,))
            else:
                add(())

    def s0(self):
        self.local.start()
        self.core.start()

    def s1(self):
        self.local.wait()
        self.core.wait()
        self.merge(self.p1)

    def s0_vmem(self):
        self.core.start()

    def s1_vmem(self):
        self.core.wait()
        self.merge(self.own)

    def merge(self, own):
        def add(i, _):
            a, b = i // 4, i % 4
            self.p1[a, b] = (own[a, b].astype(F32) + self.r0[a, b].astype(F32)).astype(BF16)
            return 0

        lax.fori_loop(0, 16, add, 0)
        for d in self.sends[0]:
            d.start()

    def stage(self, i):
        for d in self.sends[i]:
            d.wait()

        def to(q, j, value):
            ref = self.held[i + 1][q]
            ref[j] = value.astype(ref.dtype)

        self.total(i, to)
        for d in self.sends[i + 1]:
            d.start()

    def s2(self):
        self.stage(0)

    def s3(self):
        self.stage(1)

    def s4(self):
        for d in self.sends[2]:
            d.wait()

        def to(q, j, value):
            off, w = self.parts[q]
            self.p4[:, off // 2 : off // 2 + w] = value

        self.total(2, to)
        self.rep.start()

    def s5(self):
        self.rep.wait()
        k = self.at["z"] % 2
        for off, w in self.parts:
            self.out[:, half_of(off, w, k)] = self.p4[:, off // 2 : off // 2 + w]
            self.out[:, half_of(off, w, 1 - k)] = self.r4[:, off // 2 : off // 2 + w]


def run(plan, i):
    for at, steps in plan.items():

        @pl.when(i == at)
        def _():
            for step in steps:
                step()


def lay(own, at, raw, start=0, width=None):
    width = raw.shape[1] if width is None else width
    own[:15, at : at + width] = raw[:, start : start + width]


def lay_blocks(own, at, blocks, gate, up, down):
    for b in blocks:
        for raw in (gate, up, down):
            lay(own, at, raw, FB * b, FB)
            at += FB


def attend_kernel(tok_hbm, cot_hbm, cos_ref, sin_ref, gain_ref, *refs):
    raw_hbm, refs = refs[:7], refs[7:]
    xp_ref, cp_ref, nrm_ref, qt_ref, ho_ref, lt_ref, gains_ref, fa, f0, f1, tok, cot, spread, full, kx, vx, lse, bias, a, e0, e1, sem, *refs = refs
    raw, (rsem, *sems) = refs[:7], refs[7:]
    wq, wk, wv, wo, gate, up, down = raw
    loads = [pltpu.make_async_copy(h, v, rsem.at[i]) for i, (h, v) in enumerate(zip(raw_hbm, raw))]
    for d in loads:
        d.start()
    for own in (a, e0, e1):
        own[...] = jnp.zeros_like(own)
    diagonal = lax.broadcasted_iota(jnp.int32, (15, 15), 0) == lax.broadcasted_iota(jnp.int32, (15, 15), 1)
    lane = lax.broadcasted_iota(jnp.int32, (15, 128), 1)
    edge = jnp.zeros((15, 128), F32)
    for i in range(2):
        column = jnp.sum(jnp.where(diagonal, gain_ref[i : i + 1, :].astype(F32), 0.0), axis=1, keepdims=True)
        edge = jnp.where(lane == 64 + i, column, edge)
    meet()
    for d in loads[:3]:
        d.wait()
    lay(a, 0, wq)
    lay(a, 64 * K_UNIT, wk)
    a[:15, NA - 128 :] = edge.astype(BF16)
    lay(a, 64 * V_UNIT, wv)
    first = Gather(a, full, sems[0], sems[1], NA)
    c0, c1 = Gather(e0, f0, sems[2], sems[3], E0), Gather(e1, f1, sems[4], sems[5], E1)
    first.s0()
    reads = [pltpu.make_async_copy(tok_hbm, tok, sem.at[0]), pltpu.make_async_copy(cot_hbm, cot, sem.at[1])]
    for r in reads:
        r.start()
    for d in loads[3:]:
        d.wait()
    lay(e0, 0, wo)
    lay_blocks(e0, NB, [0], gate, up, down)
    lay_blocks(e1, 0, [1], gate, up, down)
    spread[...] = spread_matrix()
    row = lax.broadcasted_iota(jnp.int32, (256, 256), 0)
    col = lax.broadcasted_iota(jnp.int32, (256, 256), 1)
    bias[...] = jnp.where(col <= row, 0.0, -1e30)
    ho_ref[...] = jnp.zeros_like(ho_ref)
    lse[...] = jnp.zeros_like(lse)
    first.s1()
    c0.s0()
    for r in reads:
        r.wait()

    def widen(src, to):
        def turn(i, _):
            r = span(i, 512)
            to[r, :] = dot_tn(src[:, r], spread[...]).astype(BF16)
            return 0

        lax.fori_loop(0, 2, turn, 0)

    widen(tok, xp_ref)
    first.s2()
    c0.s1()
    c1.s0()
    widen(cot, cp_ref)
    first.s3()
    c0.s2()
    c1.s1()
    first.s4()
    keep = pltpu.make_async_copy(full, fa, sem.at[0])
    keep.start()
    a_ref = full.reshape(D, NA)
    gains_ref[...] = jnp.transpose(a_ref[:, NA - 128 :].astype(F32))[64:72, :]
    gain = gains_ref[0:1, :]

    def project(i, _):
        r = span(i, 512)
        x = xp_ref[r, :].astype(F32)
        recip = lax.rsqrt(jnp.sum(x * x, axis=1, keepdims=True) * (1.0 / WIDTH) + EPS)
        normed = (x * recip * gain).astype(BF16)
        nrm_ref[r, :] = normed
        for at in range(0, NA, 512):
            width = min(512, NA - at)
            q = dot(normed, a_ref[:, at : at + width])
            for t in range(at, at + width, 128):
                v = q[:, t - at : t - at + 128]
                if t < 64 * V_UNIT:
                    v = v * cos_ref[...] + swapped(v) * sin_ref[...]
                qt_ref[r, t : t + 128] = v.astype(BF16)
        run({0: [c1.s2]}, i)
        return 0

    lax.fori_loop(0, 2, project, 0)
    split_heads(qt_ref, kx, vx)

    def head(h, _):
        p, g = h // 2, h // 3
        u = 2 * g + h - 2 * p
        jobs = [(slice(SEQ * s + 256 * b, SEQ * s + 256 * b + 256), slice(SEQ * s, SEQ * s + 256 * b + 256)) for s in range(2) for b in range(2)]
        scores = [dot_nt(qt_ref[rows, tile(p)], kx[u, keys, :]) * (SCALE * LOG2E) for rows, keys in jobs]
        softs, stats = [], []
        for sc in scores:
            n = sc.shape[1]
            last = sc[:, n - 256 :] + bias[...]
            sc = last if n == 256 else jnp.concatenate([sc[:, : n - 256], last], axis=1)
            top = jnp.max(sc, axis=1, keepdims=True)
            ex = jnp.exp2(sc - top)
            total = jnp.sum(ex, axis=1, keepdims=True)
            softs.append((ex * (1.0 / total)).astype(BF16))
            stats.append(top + jnp.log2(total))
        outs = [dot(soft, vx[u, keys, :]) for soft, (_, keys) in zip(softs, jobs)]
        lane = lax.broadcasted_iota(jnp.int32, (256, 128), 1)
        for (rows, _), o, stat in zip(jobs, outs, stats):
            ho_ref[rows, tile(p)] = ho_ref[rows, tile(p)] + o.astype(BF16)
            lse[rows, :] = jnp.where(lane == h, stat, lse[rows, :])
        run({1: [c0.s3], 10: [c1.s3], 12: [c0.s4]}, h)
        return 0

    lax.fori_loop(0, 15, head, 0)
    lt_ref[...] = jnp.transpose(lse[...])[:16, :].reshape(16, 1, T)
    keep.wait()
    c1.s4()


def split_heads(qt_ref, kx, vx):
    low = low_half((T, 128))
    for g in range(5):
        for to, unit in ((kx, K_UNIT + g), (vx, V_UNIT + g)):
            at = 128 * (unit // 2)
            v = qt_ref[:, at : at + 128].astype(F32)
            turned = pltpu.roll(v, 64, 1)
            at_low, at_high = (v, turned) if unit % 2 == 0 else (turned, v)
            to[2 * g] = jnp.where(low, at_low, 0.0).astype(BF16)
            to[2 * g + 1] = jnp.where(low, 0.0, at_high).astype(BF16)


def attend(tok, cot, cosine, sine, gain, raw):
    shape = jax.ShapeDtypeStruct
    return pl.pallas_call(
        attend_kernel,
        out_shape=[
            shape((T, D), BF16),
            shape((T, D), BF16),
            shape((T, D), BF16),
            shape((T, NA), BF16),
            shape((T, D), BF16),
            shape((16, 1, T), F32),
            shape((8, D), F32),
            shape((4, 4, 2, 2, 16, NA), BF16),
            shape((4, 4, 2, 2, 16, E0), BF16),
            shape((4, 4, 2, 2, 16, E1), BF16),
        ],
        in_specs=[ANY] * 2 + [VMEM] * 3 + [ANY] * 7,
        out_specs=[VMEM] * 7 + [ANY] * 3,
        scratch_shapes=[
            pltpu.VMEM((WIDTH, T), BF16),
            pltpu.VMEM((WIDTH, T), BF16),
            pltpu.VMEM((WIDTH, D), BF16),
            pltpu.VMEM((4, 4, 2, 2, 16, NA), BF16),
            pltpu.VMEM((10, T, 128), BF16),
            pltpu.VMEM((10, T, 128), BF16),
            pltpu.VMEM((T, 128), F32),
            pltpu.VMEM((256, 256), F32),
            pltpu.VMEM((16, NA), BF16),
            pltpu.VMEM((16, E0), BF16),
            pltpu.VMEM((16, E1), BF16),
            pltpu.SemaphoreType.DMA((2,)),
            *[pltpu.VMEM(r.shape, BF16) for r in raw],
            pltpu.SemaphoreType.DMA((7,)),
            *gather_sems() * 3,
        ],
        compiler_params=pltpu.CompilerParams(collective_id=0, has_side_effects=True, vmem_limit_bytes=VLIM),
        name="attend",
    )(tok, cot, cosine, sine, gain, *raw)


def ffn_kernel(xp, cp, gains, ho, e0, e1, gate_hbm, up_hbm, down_hbm, hid, gheads_ref, gnorm_ref, oc_ref, outp_hbm, gl_hbm, f0, f1,
               b_full, acc, gacc, nrm, w, act, ggu, stage, own0, own1, gate, up, down, rsem, wsem, gsem, *scratch):
    loads = [pltpu.make_async_copy(h, v, rsem.at[i]) for i, (h, v) in enumerate(((gate_hbm, gate), (up_hbm, up), (down_hbm, down)))]
    for d in loads:
        d.start()
    own0[...] = jnp.zeros_like(own0)
    own1[...] = jnp.zeros_like(own1)
    meet()
    for d in loads:
        d.wait()
    lay_blocks(own0, 0, [AHEAD], gate, up, down)
    lay_blocks(own1, 0, range(AHEAD + 1, BLOCKS), gate, up, down)
    g0, g1 = Gather(own0, f0, scratch[0], scratch[1], F0), Gather(own1, f1, scratch[2], scratch[3], F1)
    lands, loc = scratch[4 : 4 + LANDING], scratch[4 + LANDING :]
    reduction = lambda j: Scatter(stage, oc_ref.at[j], [ref.at[j] for ref in lands], loc, NC)
    gain = gains[1:2, :]
    get_b = pltpu.make_async_copy(e0.at[:, :, :, :, :, :NB], b_full, gsem)
    get_b.start()

    def fetch(b, begin):
        slot = jnp.asarray(b) % 2

        for at, src in ((0, e0.at[:, :, :, :, :, NB:]), (1, e1), (2, f0), (3, f1.at[:, :, :, :, :, :NC]), (4, f1.at[:, :, :, :, :, NC:])):

            @pl.when(b == at)
            def _():
                d = pltpu.make_async_copy(src, w.at[slot], wsem.at[slot])
                d.start() if begin else d.wait()

    g0.s0()
    fetch(0, True)
    get_b.wait()
    b_ref = b_full.reshape(D, NB)

    def first(i, _):
        r = span(i, 512)
        h = xp[r, :].astype(F32) + dot_nt(ho[r, :], b_ref[...])
        hid[r, :] = h
        acc[r, :] = h
        recip = lax.rsqrt(jnp.sum(h * h, axis=1, keepdims=True) * (1.0 / WIDTH) + EPS)
        nrm[r, :] = (h * recip * gain).astype(BF16)
        gacc[r, :] = jnp.zeros((512, D), F32)
        run({0: [g0.s1, g1.s0], 1: [g0.s2, g1.s1]}, i)
        return 0

    lax.fori_loop(0, 2, first, 0)

    def when_chunk(b, ahead, name):
        @pl.when((b >= ahead) & (b < ahead + EARLY))
        def _():
            getattr(reduction(b - ahead), name)()

    def block(b, _):
        wv = w.at[b % 2].reshape(D, NC)
        fetch(b, False)

        when_chunk(b, 1, "s0_vmem")
        when_chunk(b, 3, "s3")
        when_chunk(b, 4, "s5")
        run({1: [g0.s4], 2: [g1.s4]}, b)

        def rows(i, _):
            r = span(i, 512)
            pre = dot(nrm[r, :], wv[:, : 2 * FB])
            ga = dot(cp[r, :], wv[:, 2 * FB :])
            gate, up = pre[:, :FB], pre[:, FB:]
            sig = 0.5 * jnp.tanh(0.5 * gate) + 0.5
            silu = gate * sig
            act_b = (silu * up).astype(BF16)
            act[r, :] = act_b
            ggu[r, :FB] = (ga * up * (sig + silu * (1.0 - sig))).astype(BF16)
            ggu[r, FB:] = (ga * silu).astype(BF16)
            acc[r, :] += dot_nt(act_b, wv[:, 2 * FB :])
            gacc[r, :] += dot_nt(ggu[r, :], wv[:, : 2 * FB])
            return 0

        lax.fori_loop(0, 2, rows, 0)
        when_chunk(b, 2, "s2")
        when_chunk(b, 1, "s1_vmem")
        when_chunk(b, 3, "s4")

        run({0: [g0.s3, g1.s2], 1: [g1.s3]}, b)

        @pl.when(b < BLOCKS - 1)
        def _():
            fetch(b + 1, True)

        @pl.when(b == BLOCKS - 1)
        def _():
            pltpu.make_async_copy(stage, gl_hbm.at[:, :, :, :, :, :NC], gsem).wait()

        def weights(i, _):
            r = span(i, 512)
            k = pl.ds(pl.multiple_of(2 * i, 2), 2)
            to = lambda v: v.astype(BF16).reshape(2, 4, 2, 2, 16, v.shape[1])
            stage[k, :, :, :, :, : 2 * FB] = to(dot_tn(nrm[:, r], ggu[...]))
            stage[k, :, :, :, :, 2 * FB :] = to(dot_tn(cp[:, r], act[...]))
            return 0

        lax.fori_loop(0, 2, weights, 0)

        @pl.when(b >= EARLY)
        def _():
            cols = pl.ds(pl.multiple_of(NC * jnp.maximum(b - EARLY, 0), 128), NC)
            pltpu.make_async_copy(stage, gl_hbm.at[:, :, :, :, :, cols], gsem).start()

        return 0

    lax.fori_loop(0, BLOCKS, block, 0)
    reduction(1).s5()
    reduction(2).s3()
    gnorm_ref[...] = jnp.zeros_like(gnorm_ref)
    out_stage = w.at[0].reshape(D, NC).at[:, :D]

    def last(i, _):
        r = span(i, 256)
        out_stage[r, :] = acc[r, :].astype(BF16)
        h, gn = hid[r, :], gacc[r, :]
        recip = lax.rsqrt(jnp.sum(h * h, axis=1, keepdims=True) * (1.0 / WIDTH) + EPS)
        gnorm_ref[...] += jnp.sum(gn * h * recip, axis=0, keepdims=True)
        scaled = gn * gain
        mean = jnp.sum(scaled * h, axis=1, keepdims=True) * (1.0 / WIDTH)
        gh = cp[r, :].astype(F32) + recip * scaled - h * (recip * recip * recip * mean)
        hid[r, :] = gh
        nrm[r, :] = gh.astype(BF16)
        return 0

    lax.fori_loop(0, 4, last, 0)
    reduction(2).s4()
    put_out = pltpu.make_async_copy(out_stage, outp_hbm, wsem.at[0])
    put_out.start()
    pltpu.make_async_copy(stage, gl_hbm.at[:, :, :, :, :, :NC], gsem).wait()

    def out_grad(i, _):
        r = span(i, 512)
        k = pl.ds(pl.multiple_of(2 * i, 2), 2)
        stage[k, :, :, :, :, :NB] = dot_tn(nrm[:, r], ho[...]).astype(BF16).reshape(2, 4, 2, 2, 16, NB)
        return 0

    lax.fori_loop(0, 2, out_grad, 0)
    put_gb = pltpu.make_async_copy(stage.at[:, :, :, :, :, :NB], gl_hbm.at[:, :, :, :, :, NL:], gsem)
    put_gb.start()

    def heads(i, _):
        r = span(i, 512)
        gheads_ref[r, :] = dot(nrm[r, :], b_ref[...]).astype(BF16)
        return 0

    lax.fori_loop(0, 2, heads, 0)
    reduction(2).s5()
    put_out.wait()
    put_gb.wait()


def many(shapes, k):
    vmem = lambda s: pltpu.VMEM((k, *s.shape), s.dtype)
    return [vmem(s) if i < len(shapes) - 2 else pltpu.SemaphoreType.DMA((k, SEMS)) for i, s in enumerate(shapes)]


def ffn(xp, cp, gains, ho, e0, e1, raw):
    shape = jax.ShapeDtypeStruct
    return pl.pallas_call(
        ffn_kernel,
        out_shape=[
            shape((T, D), F32),
            shape((T, D), BF16),
            shape((1, D), F32),
            shape((EARLY, 16, NC), F32),
            shape((T, D), BF16),
            shape((4, 4, 2, 2, 16, NL + NB), BF16),
            shape((4, 4, 2, 2, 16, F0), BF16),
            shape((4, 4, 2, 2, 16, F1), BF16),
        ],
        in_specs=[VMEM] * 4 + [ANY] * 5,
        out_specs=[VMEM] * 4 + [ANY] * 4,
        scratch_shapes=[
            pltpu.VMEM((4, 4, 2, 2, 16, NB), BF16),
            pltpu.VMEM((T, D), F32),
            pltpu.VMEM((T, D), F32),
            pltpu.VMEM((T, D), BF16),
            pltpu.VMEM((2, 4, 4, 2, 2, 16, NC), BF16),
            pltpu.VMEM((T, FB), BF16),
            pltpu.VMEM((T, 2 * FB), BF16),
            pltpu.VMEM((4, 4, 2, 2, 16, NC), BF16),
            pltpu.VMEM((16, F0), BF16),
            pltpu.VMEM((16, F1), BF16),
            *[pltpu.VMEM(r.shape, BF16) for r in raw],
            pltpu.SemaphoreType.DMA((3,)),
            pltpu.SemaphoreType.DMA((2,)),
            pltpu.SemaphoreType.DMA,
            *gather_sems() * 2,
            *many(landing(NC), EARLY),
            *local(NC),
        ],
        compiler_params=pltpu.CompilerParams(collective_id=1, has_side_effects=True, vmem_limit_bytes=VLIM),
        name="ffn",
    )(xp, cp, gains, ho, e0, e1, *raw)


def back_kernel(qt_ref, ho_ref, gheads_ref, lt_ref, cos_ref, sin_ref, gains, nrm, xp, gnf, early, gl, fa, gh_hbm, outp_hbm,
                oq, ok, ov, og, ou, od, oo, on, gtok_hbm, out_hbm, full, dt_ref, gsum, cols_ref, left, oa0_ref, oa1_ref, isem, osem, *scratch):
    meet()
    chunks = []
    sources = [
        (gl.at[:, :, :, :, :, :L0], left.at[:, :L0], L0),
        (gl.at[:, :, :, :, :, L0:], left.at[:, L0:], L1),
    ]
    k = LANDING + LOCAL
    for i, (src, out, n) in enumerate(sources):
        chunks.append(Scatter(src, out, scratch[k * i : k * i + LANDING], scratch[k * i + LANDING : k * i + k], n))
    c0, c1 = chunks
    loc0, loc1 = scratch[LANDING:k], scratch[k + LANDING : 2 * k]
    scratch = scratch[2 * k :]
    c0.s0()
    c1.s0()
    get_a = pltpu.make_async_copy(fa, full, isem.at[0])
    get_a.start()

    def phase_one(kx, vx, dq, dk, dv, bias):
        split_heads(qt_ref, kx, vx)
        dq[...] = jnp.zeros_like(dq)
        dk[...] = jnp.zeros_like(dk)
        dv[...] = jnp.zeros_like(dv)
        row = lax.broadcasted_iota(jnp.int32, (256, 256), 0)
        col = lax.broadcasted_iota(jnp.int32, (256, 256), 1)
        bias[...] = jnp.where(row <= col, 0.0, -1e30)

        def head(h, _):
            p, g = h // 2, h // 3
            par = h - 2 * p
            u = 2 * g + par
            lane = lax.broadcasted_iota(jnp.int32, (SEQ, 128), 1)
            own = (lane // 64) == par
            ones = jnp.ones((8, 128), BF16)
            c = SCALE * LOG2E
            for s in range(2):
                seq = slice(SEQ * s, SEQ * s + SEQ)
                q, do = qt_ref[seq, tile(p)], gheads_ref[seq, tile(p)]
                q_own = jnp.where(own, q, jnp.zeros_like(q))
                do_own = jnp.where(own, do, jnp.zeros_like(do))
                prod = do_own.astype(F32) * ho_ref[seq, tile(p)].astype(F32)
                high = prod.astype(BF16)
                rest = (prod - high.astype(F32)).astype(BF16)
                off = (dot_nt(ones, high) + dot_nt(ones, rest))[:1, :]
                lse = lt_ref[h, :, seq]
                k0, k1 = kx[u, SEQ * s : SEQ * s + 256, :], kx[u, SEQ * s + 256 : SEQ * s + 512, :]
                v0, v1 = vx[u, SEQ * s : SEQ * s + 256, :], vx[u, SEQ * s + 256 : SEQ * s + 512, :]
                st0, st1 = dot_nt(k0, q), dot_nt(k1, q[256:])
                gp0, gp1 = dot_nt(v0, do), dot_nt(v1, do[256:])
                t0 = st0 * c - lse
                e0 = jnp.exp2(jnp.concatenate([t0[:, :256] + bias[...], t0[:, 256:]], axis=1))
                e1 = jnp.exp2(st1 * c - lse[:, 256:] + bias[...])
                ds0 = (e0 * (gp0 - off)).astype(BF16)
                ds1 = (e1 * (gp1 - off[:, 256:])).astype(BF16)
                dv0, dv1 = dot(e0.astype(BF16), do_own), dot(e1.astype(BF16), do_own[256:])
                dk0, dk1 = dot(ds0, q_own), dot(ds1, q_own[256:])
                dq0 = dot_tn(ds0, k0)
                dq1 = dot_tn(ds1, k1)
                lo, hi = slice(SEQ * s, SEQ * s + 256), slice(SEQ * s + 256, SEQ * s + 512)
                dv[g, lo, :] += dv0
                dv[g, hi, :] += dv1
                dk[g, lo, :] += dk0
                dk[g, hi, :] += dk1
                dq[p, lo, :] += dq0[:256]
                dq[p, hi, :] += dq0[256:] + dq1
            run({1: [c0.s1], 3: [c1.s1], 6: [c0.s2], 8: [c0.s3], 9: [c1.s2], 10: [c0.s4], 11: [c1.s3], 12: [c0.s5], 13: [c1.s4]}, h)
            return 0

        lax.fori_loop(0, 15, head, 0)

        def finish(i, _):
            r = span(i, 256)
            half = span(i % 2, 256)
            cosine, sine = cos_ref[half, :], sin_ref[half, :]
            low = low_half((256, 128))
            fold = lambda ref, g: ref[g, r, :] + pltpu.roll(ref[g, r, :], 64, 1)
            pair = lambda ref, g: jnp.where(low, fold(ref, g), fold(ref, g + 1) if g < 4 else 0.0)
            for t, v in enumerate([dq[p, r, :] for p in range(8)] + [pair(dk, g) for g in (0, 2, 4)]):
                v = v * SCALE
                dt_ref[r, 128 * t : 128 * t + 128] = (v * cosine - swapped(v) * sine).astype(BF16)
            for t, g in ((11, 0), (12, 2), (13, 4)):
                dt_ref[r, 128 * t : 128 * t + 128] = pair(dv, g).astype(BF16)
            return 0

        lax.fori_loop(0, 4, finish, 0)

    pl.run_scoped(
        phase_one,
        pltpu.VMEM((10, T, 128), BF16),
        pltpu.VMEM((10, T, 128), BF16),
        pltpu.VMEM((8, T, 128), F32),
        pltpu.VMEM((5, T, 128), F32),
        pltpu.VMEM((5, T, 128), F32),
        pltpu.VMEM((256, 256), F32),
    )
    get_a.wait()
    a_ref = full.reshape(D, NA)
    gain = gains[0:1, :]
    gsum[...] = jnp.zeros_like(gsum)
    gsum[1:2, :] = gnf[...]

    def phase_two(gn_ref, gtok, out, spread, gh, outp, ga0, ga1):
        get_gh = lambda i: pltpu.make_async_copy(gh_hbm.at[span(i, 256), :], gh.at[i % 2], isem.at[i % 2])
        get_out = pltpu.make_async_copy(outp_hbm, outp, osem.at[0])
        get_gh(0).start()
        get_out.start()
        d0 = Scatter(ga0, oa0_ref, scratch[:LANDING], within(loc0, A0), A0)
        d1 = Scatter(ga1, oa1_ref, scratch[LANDING:], within(loc1, A1), A1)
        to = lambda v: v.astype(BF16).reshape(2, 4, 2, 2, 16, v.shape[1])

        def weights0(i, _):
            ga0[pl.ds(pl.multiple_of(2 * i, 2), 2)] = to(dot_tn(nrm[:, span(i, 512)], dt_ref[:, :A0]))
            return 0

        lax.fori_loop(0, 2, weights0, 0)
        d0.s0_vmem()
        c1.s5()

        def normed(i, _):
            r = span(i, 512)
            gn = dot_nt(dt_ref[r, :], a_ref[...])
            gn_ref[r, :] = gn
            x = xp[r, :].astype(F32)
            recip = lax.rsqrt(jnp.sum(x * x, axis=1, keepdims=True) * (1.0 / WIDTH) + EPS)
            gsum[0:1, :] += jnp.sum(gn * x * recip, axis=0, keepdims=True)
            run({1: [d0.s1_vmem]}, i)
            return 0

        lax.fori_loop(0, 2, normed, 0)
        cols = jnp.transpose(jnp.concatenate([gsum[...], jnp.zeros((120, D), F32)], axis=0))
        cols_ref[...] = pltpu.roll(cols, 64, 1)

        def weights1(i, _):
            r = span(i, 512)
            kk = pl.ds(pl.multiple_of(2 * i, 2), 2)
            g = dot_tn(nrm[:, r], dt_ref[:, A0:])
            edge = jnp.where(low_half((512, 128)), g[:, A1 - 128 :], cols_ref[r, :])
            ga1[kk, :, :, :, :, : A1 - 128] = to(g[:, : A1 - 128])
            ga1[kk, :, :, :, :, A1 - 128 :] = to(edge)
            return 0

        lax.fori_loop(0, 2, weights1, 0)
        d1.s0_vmem()
        spread[...] = spread_matrix()
        get_out.wait()
        d0.s2()
        d1.s1_vmem()

        def tokens(i, _):
            r = span(i, 256)
            get_gh(i).wait()

            @pl.when(i < 3)
            def _():
                get_gh(i + 1).start()

            x = xp[r, :].astype(F32)
            recip = lax.rsqrt(jnp.sum(x * x, axis=1, keepdims=True) * (1.0 / WIDTH) + EPS)
            scaled = gn_ref[r, :] * gain
            mean = jnp.sum(scaled * x, axis=1, keepdims=True) * (1.0 / WIDTH)
            gt = gh[i % 2] + recip * scaled - x * (recip * recip * recip * mean)
            high = gt.astype(BF16)
            mid = (gt - high.astype(F32)).astype(BF16)
            gtok[:, r] = dot_nt(spread[...], high) + dot_nt(spread[...], mid)
            out[:, r] = dot_nt(spread[...], outp[r, :]).astype(BF16)
            run({0: [d0.s3], 1: [d0.s4], 2: [d1.s2, d0.s5], 3: [d1.s3]}, i)
            return 0

        lax.fori_loop(0, 4, tokens, 0)
        puts = [pltpu.make_async_copy(gtok, gtok_hbm, osem.at[0]), pltpu.make_async_copy(out, out_hbm, osem.at[1])]
        for p in puts:
            p.start()
        d1.s4()
        at = NL
        oo[...] = left[:15, at : at + WIDTH]
        for b in range(BLOCKS):
            for i, to_ref in enumerate((og, ou, od)):
                cols = slice(FB * b, FB * b + FB)
                if b < EARLY:
                    to_ref[:, cols] = early[b, :15, FB * i : FB * i + FB]
                else:
                    at = NC * (b - EARLY) + FB * i
                    to_ref[:, cols] = left[:15, at : at + FB]
        oq[...] = oa0_ref[:15, :WIDTH]
        d1.s5()
        ok[...] = oa1_ref[:15, :320]
        ov[...] = oa1_ref[:15, 64 * V_UNIT - A0 : 64 * V_UNIT - A0 + 320]
        edge = jnp.concatenate([oa1_ref[:, A1 - 128 :], jnp.zeros((112, 128), F32)], axis=0)
        on[...] = jnp.transpose(edge)[64:72, :]
        for p in puts:
            p.wait()

    pl.run_scoped(
        phase_two,
        pltpu.VMEM((T, D), F32),
        pltpu.VMEM((WIDTH, T), F32),
        pltpu.VMEM((WIDTH, T), BF16),
        pltpu.VMEM((WIDTH, D), BF16),
        pltpu.VMEM((2, 256, D), F32),
        pltpu.VMEM((T, D), BF16),
        pltpu.VMEM((4, 4, 2, 2, 16, A0), BF16),
        pltpu.VMEM((4, 4, 2, 2, 16, A1), BF16),
    )


def back(qt, ho, gheads, lt, cosine, sine, gains, nrm, xp, gnf, early, gl, fa, gh, outp):
    shape = jax.ShapeDtypeStruct
    return pl.pallas_call(
        back_kernel,
        out_shape=[
            *[shape((15, n), F32) for n in (960, 320, 320, 2560, 2560, 2560, 960)],
            shape((8, 128), F32),
            shape((WIDTH, T), F32),
            shape((WIDTH, T), BF16),
        ],
        in_specs=[VMEM] * 11 + [ANY] * 4,
        out_specs=[VMEM] * 8 + [ANY] * 2,
        scratch_shapes=[
            pltpu.VMEM((4, 4, 2, 2, 16, NA), BF16),
            pltpu.VMEM((T, NA), BF16),
            pltpu.VMEM((8, D), F32),
            pltpu.VMEM((D, 128), F32),
            pltpu.VMEM((16, L0 + L1), F32),
            pltpu.VMEM((16, A0), F32),
            pltpu.VMEM((16, A1), F32),
            pltpu.SemaphoreType.DMA((2,)),
            pltpu.SemaphoreType.DMA((2,)),
            *landing(L0),
            *local(L0),
            *landing(L1),
            *local(L1),
            *landing(A0),
            *landing(A1),
        ],
        compiler_params=pltpu.CompilerParams(collective_id=2, has_side_effects=True, vmem_limit_bytes=VLIM),
        name="back",
    )(qt, ho, gheads, lt, cosine, sine, gains, nrm, xp, gnf, early, gl, fa, gh, outp)


def settle_kernel(*refs):
    n = len(refs) // 2
    for src, dst in zip(refs[: n - 2], refs[n:]):

        @pl.when(pl.program_id(0) == 0)
        def _():
            dst[...] = src[...]

    for src, dst in zip(refs[n - 2 : n], refs[2 * n - 2 :]):
        dst[...] = src[...]


def settle(*results):
    whole = [pl.BlockSpec(r.shape, lambda i: (0, 0)) for r in results[:-2]]
    rows = [pl.BlockSpec((WIDTH // 4, T), lambda i: (i, 0))] * 2
    return pl.pallas_call(
        settle_kernel,
        grid=(4,),
        out_shape=[jax.ShapeDtypeStruct(r.shape, r.dtype) for r in results],
        in_specs=whole + rows,
        out_specs=whole + rows,
        name="settle",
    )(*results)


def shards(tokens, cotangent, wq, wk, wv, w_gate, w_up, wo, w_down, norm_attn, norm_ffn):
    cosine, sine = rope_tables()
    gain = jnp.stack([norm_attn, norm_ffn])
    ffn_raw = (w_gate, w_up, w_down.T)
    xp, cp, nrm, qt, ho, lt, gains, fa, e0, e1 = attend(tokens.T, cotangent.T, cosine, sine, gain, (wq, wk, wv, wo.T, *ffn_raw))
    gh, gheads, gnf, early, outp, gl, _, _ = ffn(xp, cp, gains, ho, e0, e1, ffn_raw)
    results = back(qt, ho, gheads, lt, cosine, sine, gains, nrm, xp, gnf, early, gl, fa, gh, outp)
    oq, ok, ov, og, ou, od, oo, on, grad_tokens, output = settle(*results)
    return output.T, grad_tokens.T, oq, ok, ov, og, ou, oo.T, od.T, on[0, :15], on[1, :15]


def solution(mesh):
    rows = P(("replica", "shard"), None)
    first, second, one = P("shard", None), P(None, "shard"), P("shard")
    in_specs = (rows, rows, first, first, first, first, first, second, second, one, one)
    out_specs = (rows, rows, first, first, first, first, first, second, second, one, one)
    return jax.shard_map(shards, mesh=mesh, in_specs=in_specs, out_specs=out_specs, check_vma=False)
```

```python
import functools
import math

import jax
import jax.numpy as jnp
import numpy as np
from jax import lax
from jax.experimental import pallas as pl
from jax.experimental.pallas import tpu as pltpu
from jax.sharding import PartitionSpec as P

F32, BF16 = jnp.float32, jnp.bfloat16
MESH = pl.DeviceIdType.MESH
ANY = pl.BlockSpec(memory_space=pl.ANY)
VMEM = pl.BlockSpec(memory_space=pltpu.VMEM)
WIDTH = 960
D = 1024
T = 1024
SEQ = 512
K_UNIT, V_UNIT = 16, 22
NA, NB, NC, BLOCKS, FB = 1792, 1024, 1536, 5, 512
AHEAD = 2
EARLY = 3
NL = (BLOCKS - EARLY) * NC
L0 = 2304
L1 = NL + NB - L0
E0, E1 = NB + NC, NC
F0, F1 = NC, 2 * NC
A0 = 1024
A1 = NA - A0
EPS = 1e-05
SCALE = 0.125
LOG2E = math.log2(math.e)
VLIM = 60 * 1024 * 1024


def dot(a, b):
    return lax.dot_general(a, b, (((1,), (0,)), ((), ())), preferred_element_type=F32)


def dot_nt(a, b):
    return lax.dot_general(a, b, (((1,), (1,)), ((), ())), preferred_element_type=F32)


def dot_tn(a, b):
    return lax.dot_general(a, b, (((0,), (0,)), ((), ())), preferred_element_type=F32)


def span(i, n):
    return pl.ds(pl.multiple_of(i * n, n), n)


def rope_tables():
    rates = np.exp(np.arange(32) * (-2.0 * math.log(10000.0) / 64))
    angles = np.arange(SEQ)[:, None] * rates[None, :]
    cos, sin = np.cos(angles), np.sin(angles)
    cosine = np.concatenate([cos] * 4, axis=1).astype(np.float32)
    sine = np.concatenate([-sin, sin] * 2, axis=1).astype(np.float32)
    return cosine, sine


def swapped(t):
    lane = lax.broadcasted_iota(jnp.int32, t.shape, 1)
    return jnp.where((lane & 63) < 32, pltpu.roll(t, 96, 1), pltpu.roll(t, 32, 1))


def tile(p):
    return span(p, 128)


def low_half(shape):
    return lax.broadcasted_iota(jnp.int32, shape, 1) < 64


def spread_matrix():
    row = lax.broadcasted_iota(jnp.int32, (WIDTH, D), 0)
    col = lax.broadcasted_iota(jnp.int32, (WIDTH, D), 1)
    hit = (row == 15 * (col >> 4) + (col & 15)) & ((col & 15) < 15)
    return jnp.where(hit, 1.0, 0.0).astype(BF16)


def place():
    r, s = lax.axis_index("replica"), lax.axis_index("shard")
    return s // 16, (s // 4) % 4, ((s // 2) % 2) * 2 + r, s % 2


def device(x, y, z, c):
    return (z % 2, ((x * 4 + y) * 2 + z // 2) * 2 + c)


def peers():
    x, y, z, c = place()
    along = {
        "x": [device((x + d) % 4, y, z, c) for d in (1, 2, 3)],
        "y": [device(x, (y + d) % 4, z, c) for d in (1, 2, 3)],
        "z": [device(x, y, (z + d) % 4, c) for d in (1, 2, 3)],
    }
    return along, device(x, y, z, 1 - c)


def meet():
    along, other = peers()
    barrier = pltpu.get_barrier_semaphore()
    for d in (*along["x"], *along["y"], *along["z"], other):
        pl.semaphore_signal(barrier, inc=1, device_id=d, device_id_type=MESH)
    pl.semaphore_wait(barrier, 10)


def remote(src, dst, ss, rs, k, to):
    return pltpu.make_async_remote_copy(
        src_ref=src, dst_ref=dst, send_sem=ss.at[k], recv_sem=rs.at[k], device_id=to, device_id_type=MESH
    )


def parts(n):
    tiles = n // 256
    widths = [128 * (tiles // 3), 128 * (tiles // 3), 128 * (tiles - 2 * (tiles // 3))]
    return [(0, widths[0]), (2 * widths[0], widths[1]), (2 * widths[0] + 2 * widths[1], widths[2])]


def half_of(offset, width, k):
    return pl.ds(pl.multiple_of(offset + k * width, 128), width)


SEMS = 30
GATHER_ORDER = ("yxz", "zyx", "xzy")
SCATTER_ORDER = ("zxy", "xyz", "yzx")


class Gather:
    def __init__(self, own, full, ss, rs, n):
        x, y, z, c = place()
        zh, zl = z // 2, z % 2
        along, other = peers()
        self.local, self.stages = [], [[], [], []]
        k = 3
        for (off, w), order in zip(parts(n), GATHER_ORDER):
            mine = half_of(off, w, zl)
            self.local.append(pltpu.make_async_copy(own.at[:, mine], full.at[x, y, zh, c, :, mine], ss.at[len(self.local)]))
            for i, axis in enumerate(order):
                have = order[:i]
                every = slice(None)
                at = (
                    every if "x" in have else x,
                    every if "y" in have else y,
                    every if "z" in have else zh,
                    c,
                    every,
                    pl.ds(off, 2 * w) if "z" in have else mine,
                )
                for to in along[axis]:
                    src = own.at[:, mine] if i == 0 else full.at[at]
                    self.stages[i].append(remote(src, full.at[at], ss, rs, k, to))
                    k += 1
        w = full.at[:, :, :, c]
        self.core = remote(w, w, ss, rs, k, other)

    def move(self, done, begin):
        for d in done:
            d.wait()
        for d in begin:
            d.start()

    def follow(self, i):
        for k in range(0, 9, 3):
            self.move(self.stages[i][k : k + 3], self.stages[i + 1][k : k + 3])

    def s0(self):
        self.move([], self.local + self.stages[0])

    def s1(self):
        self.move(self.local, [])
        self.follow(0)

    def s2(self):
        self.follow(1)

    def s3(self):
        self.move(self.stages[2], [self.core])

    def s4(self):
        self.move([self.core], [])


def gather_sems():
    return [pltpu.SemaphoreType.DMA((SEMS + 1,)), pltpu.SemaphoreType.DMA((SEMS + 1,))]


def extent(left, w):
    return tuple([4] * ("x" in left) + [4] * ("y" in left) + [2] * ("z" in left) + [16, 2 * w if "z" in left else w])


def slot(left, axis, t, off, w):
    every = slice(None)
    cols = pl.ds(off, 2 * w) if "z" in left else every
    if axis == "z":
        cols = half_of(off, w, t % 2)
    at = [every] * ("x" in left) + [every] * ("y" in left) + [every] * ("z" in left)
    lead = [a for a in "xyz" if a in left]
    at[lead.index(axis)] = t // 2 if axis == "z" else t
    return (*at, every, cols)


LANDING, LOCAL = 13, 8


def landing(n):
    one, two, three = [], [], []
    for (_, w), order in zip(parts(n), SCATTER_ORDER):
        one.append(pltpu.VMEM((3, *extent(order[1:], w)), BF16))
        two.append(pltpu.VMEM((3, *extent(order[2:], w)), BF16))
        three.append(pltpu.VMEM((3, 16, w), F32))
    sems = [pltpu.SemaphoreType.DMA((SEMS,)), pltpu.SemaphoreType.DMA((SEMS,))]
    return [pltpu.VMEM((4, 4, 2, 16, n), BF16), *one, *two, *three, pltpu.VMEM((16, n // 2), F32), *sems]


def local(n):
    two, three = [], []
    for (_, w), order in zip(parts(n), SCATTER_ORDER):
        two.append(pltpu.VMEM(extent(order[1:], w), BF16))
        three.append(pltpu.VMEM(extent(order[2:], w), F32))
    return [pltpu.VMEM((4, 4, 2, 16, n), BF16), *two, *three, pltpu.VMEM((16, n // 2), F32)]


def within(loc, n):
    wide = lambda ref, w: ref.at[(*[slice(None)] * (len(ref.shape) - 1), pl.ds(0, w))]
    widths = [2 * w if "z" in order[i:] else w for i in (1, 2) for (_, w), order in zip(parts(n), SCATTER_ORDER)]
    return [wide(ref, w) for ref, w in zip(loc, [n, *widths, n // 2])]


class Scatter:
    def __init__(self, part, out, land, loc, n):
        x, y, z, c = place()
        self.own = part.at[:, :, :, c]
        self.at, self.out, self.parts = {"x": x, "y": y, "z": z}, out, parts(n)
        along, other = peers()
        self.r0, self.r4, ss, rs = land[0], *land[10:]
        self.p1, self.p4 = loc[0], loc[7]
        self.took = [land[1:4], land[4:7], land[7:10]]
        self.held = [[self.p1] * 3, loc[1:4], loc[4:7]]
        self.local = pltpu.make_async_copy(part.at[:, :, :, c], self.p1, ss.at[0])
        self.core = remote(part.at[:, :, :, 1 - c], self.r0, ss, rs, 1, other)
        self.sends, k = [[], [], []], 2
        for i in range(3):
            for q, order in enumerate(SCATTER_ORDER):
                for d in (1, 2, 3):
                    axis = order[i]
                    src = self.held[i][q].at[self.index(q, i, (self.at[axis] + d) % 4)]
                    self.sends[i].append(remote(src, self.took[i][q].at[d - 1], ss, rs, k, along[axis][d - 1]))
                    k += 1
        self.rep = remote(self.p4, self.r4, ss, rs, k, device(x, y, z + 1 - 2 * (z % 2), c))

    def index(self, q, i, t):
        off, w = self.parts[q]
        order = SCATTER_ORDER[q]
        return slot(order[i:], order[i], t, off if i == 0 else 0, w)

    def total(self, i, to):
        for q, order in enumerate(SCATTER_ORDER):
            own = self.held[i][q].at[self.index(q, i, self.at[order[i]])]
            took = self.took[i][q]
            lead = own.shape[:-2]

            def add(j, own=own, took=took, q=q):
                value = own[j].astype(F32)
                for k in range(3):
                    value += took[(k, *j)].astype(F32)
                to(q, j, value)

            if len(lead) == 2:

                def turn(a, _, add=add, lead=lead):
                    for b in range(lead[1]):
                        add((a, b))
                    return 0

                lax.fori_loop(0, lead[0], turn, 0)
            elif len(lead) == 1:
                for a in range(lead[0]):
                    add((a,))
            else:
                add(())

    def s0(self):
        self.local.start()
        self.core.start()

    def s1(self):
        self.local.wait()
        self.core.wait()
        self.merge(self.p1)

    def s0_vmem(self):
        self.core.start()

    def s1_vmem(self):
        self.core.wait()
        self.merge(self.own)

    def merge(self, own):
        def add(i, _):
            a, b = i // 4, i % 4
            self.p1[a, b] = (own[a, b].astype(F32) + self.r0[a, b].astype(F32)).astype(BF16)
            return 0

        lax.fori_loop(0, 16, add, 0)
        for d in self.sends[0]:
            d.start()

    def stage(self, i):
        for d in self.sends[i]:
            d.wait()

        def to(q, j, value):
            ref = self.held[i + 1][q]
            ref[j] = value.astype(ref.dtype)

        self.total(i, to)
        for d in self.sends[i + 1]:
            d.start()

    def s2(self):
        self.stage(0)

    def s3(self):
        self.stage(1)

    def s4(self):
        for d in self.sends[2]:
            d.wait()

        def to(q, j, value):
            off, w = self.parts[q]
            self.p4[:, off // 2 : off // 2 + w] = value

        self.total(2, to)
        self.rep.start()

    def s5(self):
        self.rep.wait()
        k = self.at["z"] % 2
        for off, w in self.parts:
            self.out[:, half_of(off, w, k)] = self.p4[:, off // 2 : off // 2 + w]
            self.out[:, half_of(off, w, 1 - k)] = self.r4[:, off // 2 : off // 2 + w]


def run(plan, i):
    for at, steps in plan.items():

        @pl.when(i == at)
        def _():
            for step in steps:
                step()


def lay(own, at, raw, start=0, width=None):
    width = raw.shape[1] if width is None else width
    own[:15, at : at + width] = raw[:, start : start + width]


def lay_blocks(own, at, blocks, gate, up, down):
    for b in blocks:
        for raw in (gate, up, down):
            lay(own, at, raw, FB * b, FB)
            at += FB


def attend_kernel(tok_hbm, cot_hbm, cos_ref, sin_ref, gain_ref, *refs):
    raw_hbm, refs = refs[:7], refs[7:]
    xp_ref, cp_ref, nrm_ref, qt_ref, ho_ref, lt_ref, gains_ref, fa, f0, f1, tok, cot, spread, full, kx, vx, lse, bias, a, e0, e1, sem, *refs = refs
    raw, (rsem, *sems) = refs[:7], refs[7:]
    wq, wk, wv, wo, gate, up, down = raw
    loads = [pltpu.make_async_copy(h, v, rsem.at[i]) for i, (h, v) in enumerate(zip(raw_hbm, raw))]
    for d in loads:
        d.start()
    for own in (a, e0, e1):
        own[...] = jnp.zeros_like(own)
    diagonal = lax.broadcasted_iota(jnp.int32, (15, 15), 0) == lax.broadcasted_iota(jnp.int32, (15, 15), 1)
    lane = lax.broadcasted_iota(jnp.int32, (15, 128), 1)
    edge = jnp.zeros((15, 128), F32)
    for i in range(2):
        column = jnp.sum(jnp.where(diagonal, gain_ref[i : i + 1, :].astype(F32), 0.0), axis=1, keepdims=True)
        edge = jnp.where(lane == 64 + i, column, edge)
    meet()
    for d in loads[:3]:
        d.wait()
    lay(a, 0, wq)
    lay(a, 64 * K_UNIT, wk)
    a[:15, NA - 128 :] = edge.astype(BF16)
    lay(a, 64 * V_UNIT, wv)
    first = Gather(a, full, sems[0], sems[1], NA)
    c0, c1 = Gather(e0, f0, sems[2], sems[3], E0), Gather(e1, f1, sems[4], sems[5], E1)
    first.s0()
    reads = [pltpu.make_async_copy(tok_hbm, tok, sem.at[0]), pltpu.make_async_copy(cot_hbm, cot, sem.at[1])]
    for r in reads:
        r.start()
    for d in loads[3:]:
        d.wait()
    lay(e0, 0, wo)
    lay_blocks(e0, NB, [0], gate, up, down)
    lay_blocks(e1, 0, [1], gate, up, down)
    spread[...] = spread_matrix()
    row = lax.broadcasted_iota(jnp.int32, (256, 256), 0)
    col = lax.broadcasted_iota(jnp.int32, (256, 256), 1)
    bias[...] = jnp.where(col <= row, 0.0, -1e30)
    ho_ref[...] = jnp.zeros_like(ho_ref)
    lse[...] = jnp.zeros_like(lse)
    first.s1()
    c0.s0()
    for r in reads:
        r.wait()

    def widen(src, to):
        def turn(i, _):
            r = span(i, 512)
            to[r, :] = dot_tn(src[:, r], spread[...]).astype(BF16)
            return 0

        lax.fori_loop(0, 2, turn, 0)

    widen(tok, xp_ref)
    first.s2()
    c0.s1()
    c1.s0()
    widen(cot, cp_ref)
    first.s3()
    c1.s1()
    first.s4()
    c0.s2()
    keep = pltpu.make_async_copy(full, fa, sem.at[0])
    keep.start()
    a_ref = full.reshape(D, NA)
    gains_ref[...] = jnp.transpose(a_ref[:, NA - 128 :].astype(F32))[64:72, :]
    gain = gains_ref[0:1, :]

    def project(i, _):
        r = span(i, 512)
        x = xp_ref[r, :].astype(F32)
        recip = lax.rsqrt(jnp.sum(x * x, axis=1, keepdims=True) * (1.0 / WIDTH) + EPS)
        normed = (x * recip * gain).astype(BF16)
        nrm_ref[r, :] = normed
        for at in range(0, NA, 512):
            width = min(512, NA - at)
            q = dot(normed, a_ref[:, at : at + width])
            for t in range(at, at + width, 128):
                v = q[:, t - at : t - at + 128]
                if t < 64 * V_UNIT:
                    v = v * cos_ref[...] + swapped(v) * sin_ref[...]
                qt_ref[r, t : t + 128] = v.astype(BF16)
        run({1: [c1.s2]}, i)
        return 0

    lax.fori_loop(0, 2, project, 0)
    split_heads(qt_ref, kx, vx)

    def head(h, _):
        p, g = h // 2, h // 3
        u = 2 * g + h - 2 * p
        jobs = [(slice(SEQ * s + 256 * b, SEQ * s + 256 * b + 256), slice(SEQ * s, SEQ * s + 256 * b + 256)) for s in range(2) for b in range(2)]
        scores = [dot_nt(qt_ref[rows, tile(p)], kx[u, keys, :]) * (SCALE * LOG2E) for rows, keys in jobs]
        softs, stats = [], []
        for sc in scores:
            n = sc.shape[1]
            last = sc[:, n - 256 :] + bias[...]
            sc = last if n == 256 else jnp.concatenate([sc[:, : n - 256], last], axis=1)
            top = jnp.max(sc, axis=1, keepdims=True)
            ex = jnp.exp2(sc - top)
            total = jnp.sum(ex, axis=1, keepdims=True)
            softs.append((ex * (1.0 / total)).astype(BF16))
            stats.append(top + jnp.log2(total))
        outs = [dot(soft, vx[u, keys, :]) for soft, (_, keys) in zip(softs, jobs)]
        lane = lax.broadcasted_iota(jnp.int32, (256, 128), 1)
        for (rows, _), o, stat in zip(jobs, outs, stats):
            ho_ref[rows, tile(p)] = ho_ref[rows, tile(p)] + o.astype(BF16)
            lse[rows, :] = jnp.where(lane == h, stat, lse[rows, :])
        run({4: [c0.s3], 11: [c1.s3], 12: [c0.s4]}, h)
        return 0

    lax.fori_loop(0, 15, head, 0)
    lt_ref[...] = jnp.transpose(lse[...])[:16, :].reshape(16, 1, T)
    keep.wait()
    c1.s4()


def split_heads(qt_ref, kx, vx):
    low = low_half((T, 128))
    for g in range(5):
        for to, unit in ((kx, K_UNIT + g), (vx, V_UNIT + g)):
            at = 128 * (unit // 2)
            v = qt_ref[:, at : at + 128].astype(F32)
            turned = pltpu.roll(v, 64, 1)
            at_low, at_high = (v, turned) if unit % 2 == 0 else (turned, v)
            to[2 * g] = jnp.where(low, at_low, 0.0).astype(BF16)
            to[2 * g + 1] = jnp.where(low, 0.0, at_high).astype(BF16)


def attend(tok, cot, cosine, sine, gain, raw):
    shape = jax.ShapeDtypeStruct
    return pl.pallas_call(
        attend_kernel,
        out_shape=[
            shape((T, D), BF16),
            shape((T, D), BF16),
            shape((T, D), BF16),
            shape((T, NA), BF16),
            shape((T, D), BF16),
            shape((16, 1, T), F32),
            shape((8, D), F32),
            shape((4, 4, 2, 2, 16, NA), BF16),
            shape((4, 4, 2, 2, 16, E0), BF16),
            shape((4, 4, 2, 2, 16, E1), BF16),
        ],
        in_specs=[ANY] * 2 + [VMEM] * 3 + [ANY] * 7,
        out_specs=[VMEM] * 7 + [ANY] * 3,
        scratch_shapes=[
            pltpu.VMEM((WIDTH, T), BF16),
            pltpu.VMEM((WIDTH, T), BF16),
            pltpu.VMEM((WIDTH, D), BF16),
            pltpu.VMEM((4, 4, 2, 2, 16, NA), BF16),
            pltpu.VMEM((10, T, 128), BF16),
            pltpu.VMEM((10, T, 128), BF16),
            pltpu.VMEM((T, 128), F32),
            pltpu.VMEM((256, 256), F32),
            pltpu.VMEM((16, NA), BF16),
            pltpu.VMEM((16, E0), BF16),
            pltpu.VMEM((16, E1), BF16),
            pltpu.SemaphoreType.DMA((2,)),
            *[pltpu.VMEM(r.shape, BF16) for r in raw],
            pltpu.SemaphoreType.DMA((7,)),
            *gather_sems() * 3,
        ],
        compiler_params=pltpu.CompilerParams(collective_id=0, has_side_effects=True, vmem_limit_bytes=VLIM),
        name="attend",
    )(tok, cot, cosine, sine, gain, *raw)


def ffn_kernel(xp, cp, gains, ho, e0, e1, gate_hbm, up_hbm, down_hbm, hid, gheads_ref, gnorm_ref, oc_ref, outp_hbm, gl_hbm, f0, f1,
               b_full, acc, gacc, nrm, w, act, ggu, stage, own0, own1, gate, up, down, rsem, wsem, gsem, *scratch):
    loads = [pltpu.make_async_copy(h, v, rsem.at[i]) for i, (h, v) in enumerate(((gate_hbm, gate), (up_hbm, up), (down_hbm, down)))]
    for d in loads:
        d.start()
    own0[...] = jnp.zeros_like(own0)
    own1[...] = jnp.zeros_like(own1)
    meet()
    for d in loads:
        d.wait()
    lay_blocks(own0, 0, [AHEAD], gate, up, down)
    lay_blocks(own1, 0, range(AHEAD + 1, BLOCKS), gate, up, down)
    g0, g1 = Gather(own0, f0, scratch[0], scratch[1], F0), Gather(own1, f1, scratch[2], scratch[3], F1)
    lands, loc = scratch[4 : 4 + LANDING], scratch[4 + LANDING :]
    reduction = lambda j: Scatter(stage, oc_ref.at[j], [ref.at[j] for ref in lands], loc, NC)
    gain = gains[1:2, :]
    get_b = pltpu.make_async_copy(e0.at[:, :, :, :, :, :NB], b_full, gsem)
    get_b.start()

    def fetch(b, begin):
        slot = jnp.asarray(b) % 2

        for at, src in ((0, e0.at[:, :, :, :, :, NB:]), (1, e1), (2, f0), (3, f1.at[:, :, :, :, :, :NC]), (4, f1.at[:, :, :, :, :, NC:])):

            @pl.when(b == at)
            def _():
                d = pltpu.make_async_copy(src, w.at[slot], wsem.at[slot])
                d.start() if begin else d.wait()

    g0.s0()
    fetch(0, True)
    get_b.wait()
    b_ref = b_full.reshape(D, NB)

    def first(i, _):
        r = span(i, 512)
        h = xp[r, :].astype(F32) + dot_nt(ho[r, :], b_ref[...])
        hid[r, :] = h
        acc[r, :] = h
        recip = lax.rsqrt(jnp.sum(h * h, axis=1, keepdims=True) * (1.0 / WIDTH) + EPS)
        nrm[r, :] = (h * recip * gain).astype(BF16)
        gacc[r, :] = jnp.zeros((512, D), F32)
        run({1: [g0.s1, g1.s0]}, i)
        return 0

    lax.fori_loop(0, 2, first, 0)

    def when_chunk(b, ahead, name):
        @pl.when((b >= ahead) & (b < ahead + EARLY))
        def _():
            getattr(reduction(b - ahead), name)()

    def block(b, _):
        wv = w.at[b % 2].reshape(D, NC)
        fetch(b, False)

        when_chunk(b, 1, "s0_vmem")
        when_chunk(b, 3, "s3")
        when_chunk(b, 4, "s5")
        run({0: [g0.s2, g1.s1], 1: [g0.s3, g1.s2], 2: [g1.s3]}, b)

        def rows(i, _):
            r = span(i, 512)
            pre = dot(nrm[r, :], wv[:, : 2 * FB])
            ga = dot(cp[r, :], wv[:, 2 * FB :])
            gate, up = pre[:, :FB], pre[:, FB:]
            sig = 0.5 * jnp.tanh(0.5 * gate) + 0.5
            silu = gate * sig
            act_b = (silu * up).astype(BF16)
            act[r, :] = act_b
            ggu[r, :FB] = (ga * up * (sig + silu * (1.0 - sig))).astype(BF16)
            ggu[r, FB:] = (ga * silu).astype(BF16)
            acc[r, :] += dot_nt(act_b, wv[:, 2 * FB :])
            gacc[r, :] += dot_nt(ggu[r, :], wv[:, : 2 * FB])
            return 0

        lax.fori_loop(0, 2, rows, 0)
        when_chunk(b, 2, "s2")
        when_chunk(b, 1, "s1_vmem")
        when_chunk(b, 3, "s4")

        run({1: [g0.s4], 2: [g1.s4]}, b)

        @pl.when(b < BLOCKS - 1)
        def _():
            fetch(b + 1, True)

        @pl.when(b == BLOCKS - 1)
        def _():
            pltpu.make_async_copy(stage, gl_hbm.at[:, :, :, :, :, :NC], gsem).wait()

        def weights(i, _):
            r = span(i, 512)
            k = pl.ds(pl.multiple_of(2 * i, 2), 2)
            to = lambda v: v.astype(BF16).reshape(2, 4, 2, 2, 16, v.shape[1])
            stage[k, :, :, :, :, : 2 * FB] = to(dot_tn(nrm[:, r], ggu[...]))
            stage[k, :, :, :, :, 2 * FB :] = to(dot_tn(cp[:, r], act[...]))
            return 0

        lax.fori_loop(0, 2, weights, 0)

        @pl.when(b >= EARLY)
        def _():
            cols = pl.ds(pl.multiple_of(NC * jnp.maximum(b - EARLY, 0), 128), NC)
            pltpu.make_async_copy(stage, gl_hbm.at[:, :, :, :, :, cols], gsem).start()

        return 0

    lax.fori_loop(0, BLOCKS, block, 0)
    reduction(1).s5()
    reduction(2).s3()
    gnorm_ref[...] = jnp.zeros_like(gnorm_ref)
    out_stage = w.at[0].reshape(D, NC).at[:, :D]

    def last(i, _):
        r = span(i, 256)
        out_stage[r, :] = acc[r, :].astype(BF16)
        h, gn = hid[r, :], gacc[r, :]
        recip = lax.rsqrt(jnp.sum(h * h, axis=1, keepdims=True) * (1.0 / WIDTH) + EPS)
        gnorm_ref[...] += jnp.sum(gn * h * recip, axis=0, keepdims=True)
        scaled = gn * gain
        mean = jnp.sum(scaled * h, axis=1, keepdims=True) * (1.0 / WIDTH)
        gh = cp[r, :].astype(F32) + recip * scaled - h * (recip * recip * recip * mean)
        hid[r, :] = gh
        nrm[r, :] = gh.astype(BF16)
        return 0

    lax.fori_loop(0, 4, last, 0)
    reduction(2).s4()
    put_out = pltpu.make_async_copy(out_stage, outp_hbm, wsem.at[0])
    put_out.start()
    pltpu.make_async_copy(stage, gl_hbm.at[:, :, :, :, :, :NC], gsem).wait()

    def out_grad(i, _):
        r = span(i, 512)
        k = pl.ds(pl.multiple_of(2 * i, 2), 2)
        stage[k, :, :, :, :, :NB] = dot_tn(nrm[:, r], ho[...]).astype(BF16).reshape(2, 4, 2, 2, 16, NB)
        return 0

    lax.fori_loop(0, 2, out_grad, 0)
    put_gb = pltpu.make_async_copy(stage.at[:, :, :, :, :, :NB], gl_hbm.at[:, :, :, :, :, NL:], gsem)
    put_gb.start()

    def heads(i, _):
        r = span(i, 512)
        gheads_ref[r, :] = dot(nrm[r, :], b_ref[...]).astype(BF16)
        return 0

    lax.fori_loop(0, 2, heads, 0)
    reduction(2).s5()
    put_out.wait()
    put_gb.wait()


def many(shapes, k):
    vmem = lambda s: pltpu.VMEM((k, *s.shape), s.dtype)
    return [vmem(s) if i < len(shapes) - 2 else pltpu.SemaphoreType.DMA((k, SEMS)) for i, s in enumerate(shapes)]


def ffn(xp, cp, gains, ho, e0, e1, raw):
    shape = jax.ShapeDtypeStruct
    return pl.pallas_call(
        ffn_kernel,
        out_shape=[
            shape((T, D), F32),
            shape((T, D), BF16),
            shape((1, D), F32),
            shape((EARLY, 16, NC), F32),
            shape((T, D), BF16),
            shape((4, 4, 2, 2, 16, NL + NB), BF16),
            shape((4, 4, 2, 2, 16, F0), BF16),
            shape((4, 4, 2, 2, 16, F1), BF16),
        ],
        in_specs=[VMEM] * 4 + [ANY] * 5,
        out_specs=[VMEM] * 4 + [ANY] * 4,
        scratch_shapes=[
            pltpu.VMEM((4, 4, 2, 2, 16, NB), BF16),
            pltpu.VMEM((T, D), F32),
            pltpu.VMEM((T, D), F32),
            pltpu.VMEM((T, D), BF16),
            pltpu.VMEM((2, 4, 4, 2, 2, 16, NC), BF16),
            pltpu.VMEM((T, FB), BF16),
            pltpu.VMEM((T, 2 * FB), BF16),
            pltpu.VMEM((4, 4, 2, 2, 16, NC), BF16),
            pltpu.VMEM((16, F0), BF16),
            pltpu.VMEM((16, F1), BF16),
            *[pltpu.VMEM(r.shape, BF16) for r in raw],
            pltpu.SemaphoreType.DMA((3,)),
            pltpu.SemaphoreType.DMA((2,)),
            pltpu.SemaphoreType.DMA,
            *gather_sems() * 2,
            *many(landing(NC), EARLY),
            *local(NC),
        ],
        compiler_params=pltpu.CompilerParams(collective_id=1, has_side_effects=True, vmem_limit_bytes=VLIM),
        name="ffn",
    )(xp, cp, gains, ho, e0, e1, *raw)


def back_kernel(qt_ref, ho_ref, gheads_ref, lt_ref, cos_ref, sin_ref, gains, nrm, xp, gnf, early, gl, fa, gh_hbm, outp_hbm,
                oq, ok, ov, og, ou, od, oo, on, gtok_hbm, out_hbm, full, dt_ref, gsum, cols_ref, left, oa0_ref, oa1_ref, isem, osem, *scratch):
    meet()
    chunks = []
    sources = [
        (gl.at[:, :, :, :, :, :L0], left.at[:, :L0], L0),
        (gl.at[:, :, :, :, :, L0:], left.at[:, L0:], L1),
    ]
    k = LANDING + LOCAL
    for i, (src, out, n) in enumerate(sources):
        chunks.append(Scatter(src, out, scratch[k * i : k * i + LANDING], scratch[k * i + LANDING : k * i + k], n))
    c0, c1 = chunks
    loc0, loc1 = scratch[LANDING:k], scratch[k + LANDING : 2 * k]
    scratch = scratch[2 * k :]
    c0.s0()
    get_a = pltpu.make_async_copy(fa, full, isem.at[0])
    get_a.start()

    def phase_one(kx, vx, dq, dk, dv, bias):
        split_heads(qt_ref, kx, vx)
        dq[...] = jnp.zeros_like(dq)
        dk[...] = jnp.zeros_like(dk)
        dv[...] = jnp.zeros_like(dv)
        row = lax.broadcasted_iota(jnp.int32, (256, 256), 0)
        col = lax.broadcasted_iota(jnp.int32, (256, 256), 1)
        bias[...] = jnp.where(row <= col, 0.0, -1e30)

        def head(h, _):
            p, g = h // 2, h // 3
            par = h - 2 * p
            u = 2 * g + par
            lane = lax.broadcasted_iota(jnp.int32, (SEQ, 128), 1)
            own = (lane // 64) == par
            ones = jnp.ones((8, 128), BF16)
            c = SCALE * LOG2E
            for s in range(2):
                seq = slice(SEQ * s, SEQ * s + SEQ)
                q, do = qt_ref[seq, tile(p)], gheads_ref[seq, tile(p)]
                q_own = jnp.where(own, q, jnp.zeros_like(q))
                do_own = jnp.where(own, do, jnp.zeros_like(do))
                prod = do_own.astype(F32) * ho_ref[seq, tile(p)].astype(F32)
                high = prod.astype(BF16)
                rest = (prod - high.astype(F32)).astype(BF16)
                off = (dot_nt(ones, high) + dot_nt(ones, rest))[:1, :]
                lse = lt_ref[h, :, seq]
                k0, k1 = kx[u, SEQ * s : SEQ * s + 256, :], kx[u, SEQ * s + 256 : SEQ * s + 512, :]
                v0, v1 = vx[u, SEQ * s : SEQ * s + 256, :], vx[u, SEQ * s + 256 : SEQ * s + 512, :]
                st0, st1 = dot_nt(k0, q), dot_nt(k1, q[256:])
                gp0, gp1 = dot_nt(v0, do), dot_nt(v1, do[256:])
                t0 = st0 * c - lse
                e0 = jnp.exp2(jnp.concatenate([t0[:, :256] + bias[...], t0[:, 256:]], axis=1))
                e1 = jnp.exp2(st1 * c - lse[:, 256:] + bias[...])
                ds0 = (e0 * (gp0 - off)).astype(BF16)
                ds1 = (e1 * (gp1 - off[:, 256:])).astype(BF16)
                dv0, dv1 = dot(e0.astype(BF16), do_own), dot(e1.astype(BF16), do_own[256:])
                dk0, dk1 = dot(ds0, q_own), dot(ds1, q_own[256:])
                dq0 = dot_tn(ds0, k0)
                dq1 = dot_tn(ds1, k1)
                lo, hi = slice(SEQ * s, SEQ * s + 256), slice(SEQ * s + 256, SEQ * s + 512)
                dv[g, lo, :] += dv0
                dv[g, hi, :] += dv1
                dk[g, lo, :] += dk0
                dk[g, hi, :] += dk1
                dq[p, lo, :] += dq0[:256]
                dq[p, hi, :] += dq0[256:] + dq1
            run({1: [c0.s1, c1.s0], 4: [c1.s1], 8: [c0.s2], 11: [c0.s3, c1.s2], 14: [c0.s4, c1.s3]}, h)
            return 0

        lax.fori_loop(0, 15, head, 0)

        def finish(i, _):
            r = span(i, 256)
            half = span(i % 2, 256)
            cosine, sine = cos_ref[half, :], sin_ref[half, :]
            low = low_half((256, 128))
            fold = lambda ref, g: ref[g, r, :] + pltpu.roll(ref[g, r, :], 64, 1)
            pair = lambda ref, g: jnp.where(low, fold(ref, g), fold(ref, g + 1) if g < 4 else 0.0)
            for t, v in enumerate([dq[p, r, :] for p in range(8)] + [pair(dk, g) for g in (0, 2, 4)]):
                v = v * SCALE
                dt_ref[r, 128 * t : 128 * t + 128] = (v * cosine - swapped(v) * sine).astype(BF16)
            for t, g in ((11, 0), (12, 2), (13, 4)):
                dt_ref[r, 128 * t : 128 * t + 128] = pair(dv, g).astype(BF16)
            return 0

        lax.fori_loop(0, 4, finish, 0)
        c0.s5()
        c1.s4()

    pl.run_scoped(
        phase_one,
        pltpu.VMEM((10, T, 128), BF16),
        pltpu.VMEM((10, T, 128), BF16),
        pltpu.VMEM((8, T, 128), F32),
        pltpu.VMEM((5, T, 128), F32),
        pltpu.VMEM((5, T, 128), F32),
        pltpu.VMEM((256, 256), F32),
    )
    get_a.wait()
    a_ref = full.reshape(D, NA)
    gain = gains[0:1, :]
    gsum[...] = jnp.zeros_like(gsum)
    gsum[1:2, :] = gnf[...]

    def phase_two(gn_ref, gtok, out, spread, gh, outp, ga0, ga1):
        get_gh = lambda i: pltpu.make_async_copy(gh_hbm.at[span(i, 256), :], gh.at[i % 2], isem.at[i % 2])
        get_out = pltpu.make_async_copy(outp_hbm, outp, osem.at[0])
        get_gh(0).start()
        get_out.start()
        d0 = Scatter(ga0, oa0_ref, scratch[:LANDING], within(loc0, A0), A0)
        d1 = Scatter(ga1, oa1_ref, scratch[LANDING:], within(loc1, A1), A1)
        to = lambda v: v.astype(BF16).reshape(2, 4, 2, 2, 16, v.shape[1])

        def weights0(i, _):
            ga0[pl.ds(pl.multiple_of(2 * i, 2), 2)] = to(dot_tn(nrm[:, span(i, 512)], dt_ref[:, :A0]))
            return 0

        lax.fori_loop(0, 2, weights0, 0)
        d0.s0_vmem()
        c1.s5()

        def normed(i, _):
            r = span(i, 512)
            gn = dot_nt(dt_ref[r, :], a_ref[...])
            gn_ref[r, :] = gn
            x = xp[r, :].astype(F32)
            recip = lax.rsqrt(jnp.sum(x * x, axis=1, keepdims=True) * (1.0 / WIDTH) + EPS)
            gsum[0:1, :] += jnp.sum(gn * x * recip, axis=0, keepdims=True)
            run({1: [d0.s1_vmem]}, i)
            return 0

        lax.fori_loop(0, 2, normed, 0)
        cols = jnp.transpose(jnp.concatenate([gsum[...], jnp.zeros((120, D), F32)], axis=0))
        cols_ref[...] = pltpu.roll(cols, 64, 1)

        def weights1(i, _):
            r = span(i, 512)
            kk = pl.ds(pl.multiple_of(2 * i, 2), 2)
            g = dot_tn(nrm[:, r], dt_ref[:, A0:])
            edge = jnp.where(low_half((512, 128)), g[:, A1 - 128 :], cols_ref[r, :])
            ga1[kk, :, :, :, :, : A1 - 128] = to(g[:, : A1 - 128])
            ga1[kk, :, :, :, :, A1 - 128 :] = to(edge)
            return 0

        lax.fori_loop(0, 2, weights1, 0)
        d1.s0_vmem()
        spread[...] = spread_matrix()
        get_out.wait()
        d0.s2()
        d1.s1_vmem()

        def tokens(i, _):
            r = span(i, 256)
            get_gh(i).wait()

            @pl.when(i < 3)
            def _():
                get_gh(i + 1).start()

            x = xp[r, :].astype(F32)
            recip = lax.rsqrt(jnp.sum(x * x, axis=1, keepdims=True) * (1.0 / WIDTH) + EPS)
            scaled = gn_ref[r, :] * gain
            mean = jnp.sum(scaled * x, axis=1, keepdims=True) * (1.0 / WIDTH)
            gt = gh[i % 2] + recip * scaled - x * (recip * recip * recip * mean)
            high = gt.astype(BF16)
            mid = (gt - high.astype(F32)).astype(BF16)
            gtok[:, r] = dot_nt(spread[...], high) + dot_nt(spread[...], mid)
            out[:, r] = dot_nt(spread[...], outp[r, :]).astype(BF16)
            run({0: [d0.s3], 1: [d1.s2, d0.s4], 2: [d1.s3, d0.s5], 3: [d1.s4]}, i)
            return 0

        lax.fori_loop(0, 4, tokens, 0)
        puts = [pltpu.make_async_copy(gtok, gtok_hbm, osem.at[0]), pltpu.make_async_copy(out, out_hbm, osem.at[1])]
        for p in puts:
            p.start()
        at = NL
        oo[...] = left[:15, at : at + WIDTH]
        for b in range(BLOCKS):
            for i, to_ref in enumerate((og, ou, od)):
                cols = slice(FB * b, FB * b + FB)
                if b < EARLY:
                    to_ref[:, cols] = early[b, :15, FB * i : FB * i + FB]
                else:
                    at = NC * (b - EARLY) + FB * i
                    to_ref[:, cols] = left[:15, at : at + FB]
        oq[...] = oa0_ref[:15, :WIDTH]
        d1.s5()
        ok[...] = oa1_ref[:15, :320]
        ov[...] = oa1_ref[:15, 64 * V_UNIT - A0 : 64 * V_UNIT - A0 + 320]
        edge = jnp.concatenate([oa1_ref[:, A1 - 128 :], jnp.zeros((112, 128), F32)], axis=0)
        on[...] = jnp.transpose(edge)[64:72, :]
        for p in puts:
            p.wait()

    pl.run_scoped(
        phase_two,
        pltpu.VMEM((T, D), F32),
        pltpu.VMEM((WIDTH, T), F32),
        pltpu.VMEM((WIDTH, T), BF16),
        pltpu.VMEM((WIDTH, D), BF16),
        pltpu.VMEM((2, 256, D), F32),
        pltpu.VMEM((T, D), BF16),
        pltpu.VMEM((4, 4, 2, 2, 16, A0), BF16),
        pltpu.VMEM((4, 4, 2, 2, 16, A1), BF16),
    )


def back(qt, ho, gheads, lt, cosine, sine, gains, nrm, xp, gnf, early, gl, fa, gh, outp):
    shape = jax.ShapeDtypeStruct
    return pl.pallas_call(
        back_kernel,
        out_shape=[
            *[shape((15, n), F32) for n in (960, 320, 320, 2560, 2560, 2560, 960)],
            shape((8, 128), F32),
            shape((WIDTH, T), F32),
            shape((WIDTH, T), BF16),
        ],
        in_specs=[VMEM] * 11 + [ANY] * 4,
        out_specs=[VMEM] * 8 + [ANY] * 2,
        scratch_shapes=[
            pltpu.VMEM((4, 4, 2, 2, 16, NA), BF16),
            pltpu.VMEM((T, NA), BF16),
            pltpu.VMEM((8, D), F32),
            pltpu.VMEM((D, 128), F32),
            pltpu.VMEM((16, L0 + L1), F32),
            pltpu.VMEM((16, A0), F32),
            pltpu.VMEM((16, A1), F32),
            pltpu.SemaphoreType.DMA((2,)),
            pltpu.SemaphoreType.DMA((2,)),
            *landing(L0),
            *local(L0),
            *landing(L1),
            *local(L1),
            *landing(A0),
            *landing(A1),
        ],
        compiler_params=pltpu.CompilerParams(collective_id=2, has_side_effects=True, vmem_limit_bytes=VLIM),
        name="back",
    )(qt, ho, gheads, lt, cosine, sine, gains, nrm, xp, gnf, early, gl, fa, gh, outp)


def settle_kernel(*refs):
    n = len(refs) // 2
    for src, dst in zip(refs[: n - 2], refs[n:]):

        @pl.when(pl.program_id(0) == 0)
        def _():
            dst[...] = src[...]

    for src, dst in zip(refs[n - 2 : n], refs[2 * n - 2 :]):
        dst[...] = src[...]


def settle(*results):
    whole = [pl.BlockSpec(r.shape, lambda i: (0, 0)) for r in results[:-2]]
    rows = [pl.BlockSpec((WIDTH // 4, T), lambda i: (i, 0))] * 2
    return pl.pallas_call(
        settle_kernel,
        grid=(4,),
        out_shape=[jax.ShapeDtypeStruct(r.shape, r.dtype) for r in results],
        in_specs=whole + rows,
        out_specs=whole + rows,
        name="settle",
    )(*results)


def shards(tokens, cotangent, wq, wk, wv, w_gate, w_up, wo, w_down, norm_attn, norm_ffn):
    cosine, sine = rope_tables()
    gain = jnp.stack([norm_attn, norm_ffn])
    ffn_raw = (w_gate, w_up, w_down.T)
    xp, cp, nrm, qt, ho, lt, gains, fa, e0, e1 = attend(tokens.T, cotangent.T, cosine, sine, gain, (wq, wk, wv, wo.T, *ffn_raw))
    gh, gheads, gnf, early, outp, gl, _, _ = ffn(xp, cp, gains, ho, e0, e1, ffn_raw)
    results = back(qt, ho, gheads, lt, cosine, sine, gains, nrm, xp, gnf, early, gl, fa, gh, outp)
    oq, ok, ov, og, ou, od, oo, on, grad_tokens, output = settle(*results)
    return output.T, grad_tokens.T, oq, ok, ov, og, ou, oo.T, od.T, on[0, :15], on[1, :15]


def solution(mesh):
    rows = P(("replica", "shard"), None)
    first, second, one = P("shard", None), P(None, "shard"), P("shard")
    in_specs = (rows, rows, first, first, first, first, first, second, second, one, one)
    out_specs = (rows, rows, first, first, first, first, first, second, second, one, one)
    return jax.shard_map(shards, mesh=mesh, in_specs=in_specs, out_specs=out_specs, check_vma=False)
```

```python
import functools
import math

import jax
import jax.numpy as jnp
import numpy as np
from jax import lax
from jax.experimental import pallas as pl
from jax.experimental.pallas import tpu as pltpu
from jax.sharding import PartitionSpec as P

F32, BF16 = jnp.float32, jnp.bfloat16
MESH = pl.DeviceIdType.MESH
ANY = pl.BlockSpec(memory_space=pl.ANY)
VMEM = pl.BlockSpec(memory_space=pltpu.VMEM)
WIDTH = 960
D = 1024
T = 1024
SEQ = 512
K_UNIT, V_UNIT = 16, 22
NA, NB, NC, BLOCKS, FB = 1792, 1024, 1536, 5, 512
AHEAD = 2
EARLY = 3
NL = (BLOCKS - EARLY) * NC
L0 = 2304
L1 = NL + NB - L0
E0, E1 = NB + NC, NC
F0, F1 = NC, 2 * NC
A0 = 1024
A1 = NA - A0
EPS = 1e-05
SCALE = 0.125
LOG2E = math.log2(math.e)
VLIM = 60 * 1024 * 1024


def dot(a, b):
    return lax.dot_general(a, b, (((1,), (0,)), ((), ())), preferred_element_type=F32)


def dot_nt(a, b):
    return lax.dot_general(a, b, (((1,), (1,)), ((), ())), preferred_element_type=F32)


def dot_tn(a, b):
    return lax.dot_general(a, b, (((0,), (0,)), ((), ())), preferred_element_type=F32)


def span(i, n):
    return pl.ds(pl.multiple_of(i * n, n), n)


def rope_tables():
    rates = np.exp(np.arange(32) * (-2.0 * math.log(10000.0) / 64))
    angles = np.arange(SEQ)[:, None] * rates[None, :]
    cos, sin = np.cos(angles), np.sin(angles)
    cosine = np.concatenate([cos] * 4, axis=1).astype(np.float32)
    sine = np.concatenate([-sin, sin] * 2, axis=1).astype(np.float32)
    return cosine, sine


def swapped(t):
    lane = lax.broadcasted_iota(jnp.int32, t.shape, 1)
    return jnp.where((lane & 63) < 32, pltpu.roll(t, 96, 1), pltpu.roll(t, 32, 1))


def tile(p):
    return span(p, 128)


def low_half(shape):
    return lax.broadcasted_iota(jnp.int32, shape, 1) < 64


def spread_matrix():
    row = lax.broadcasted_iota(jnp.int32, (WIDTH, D), 0)
    col = lax.broadcasted_iota(jnp.int32, (WIDTH, D), 1)
    hit = (row == 15 * (col >> 4) + (col & 15)) & ((col & 15) < 15)
    return jnp.where(hit, 1.0, 0.0).astype(BF16)


def place():
    r, s = lax.axis_index("replica"), lax.axis_index("shard")
    return s // 16, (s // 4) % 4, ((s // 2) % 2) * 2 + r, s % 2


def device(x, y, z, c):
    return (z % 2, ((x * 4 + y) * 2 + z // 2) * 2 + c)


def peers():
    x, y, z, c = place()
    along = {
        "x": [device((x + d) % 4, y, z, c) for d in (1, 2, 3)],
        "y": [device(x, (y + d) % 4, z, c) for d in (1, 2, 3)],
        "z": [device(x, y, (z + d) % 4, c) for d in (1, 2, 3)],
    }
    return along, device(x, y, z, 1 - c)


def meet():
    along, other = peers()
    barrier = pltpu.get_barrier_semaphore()
    for d in (*along["x"], *along["y"], *along["z"], other):
        pl.semaphore_signal(barrier, inc=1, device_id=d, device_id_type=MESH)
    pl.semaphore_wait(barrier, 10)


def remote(src, dst, ss, rs, k, to):
    return pltpu.make_async_remote_copy(
        src_ref=src, dst_ref=dst, send_sem=ss.at[k], recv_sem=rs.at[k], device_id=to, device_id_type=MESH
    )


def parts(n):
    tiles = n // 256
    widths = [128 * (tiles // 3), 128 * (tiles // 3), 128 * (tiles - 2 * (tiles // 3))]
    return [(0, widths[0]), (2 * widths[0], widths[1]), (2 * widths[0] + 2 * widths[1], widths[2])]


def half_of(offset, width, k):
    return pl.ds(pl.multiple_of(offset + k * width, 128), width)


SEMS = 30
GATHER_ORDER = ("yxz", "zyx", "xzy")
SCATTER_ORDER = ("zxy", "xyz", "yzx")


class Gather:
    def __init__(self, own, full, ss, rs, n):
        x, y, z, c = place()
        zh, zl = z // 2, z % 2
        along, other = peers()
        self.local, self.stages = [], [[], [], []]
        k = 3
        for (off, w), order in zip(parts(n), GATHER_ORDER):
            mine = half_of(off, w, zl)
            self.local.append(pltpu.make_async_copy(own.at[:, mine], full.at[x, y, zh, c, :, mine], ss.at[len(self.local)]))
            for i, axis in enumerate(order):
                have = order[:i]
                every = slice(None)
                at = (
                    every if "x" in have else x,
                    every if "y" in have else y,
                    every if "z" in have else zh,
                    c,
                    every,
                    pl.ds(off, 2 * w) if "z" in have else mine,
                )
                for to in along[axis]:
                    src = own.at[:, mine] if i == 0 else full.at[at]
                    self.stages[i].append(remote(src, full.at[at], ss, rs, k, to))
                    k += 1
        w = full.at[:, :, :, c]
        self.core = remote(w, w, ss, rs, k, other)

    def move(self, done, begin):
        for d in done:
            d.wait()
        for d in begin:
            d.start()

    def follow(self, i):
        for k in range(0, 9, 3):
            self.move(self.stages[i][k : k + 3], self.stages[i + 1][k : k + 3])

    def s0(self):
        self.move([], self.local + self.stages[0])

    def s1(self):
        self.move(self.local, [])
        self.follow(0)

    def s2(self):
        self.follow(1)

    def s3(self):
        self.move(self.stages[2], [self.core])

    def s4(self):
        self.move([self.core], [])


def gather_sems():
    return [pltpu.SemaphoreType.DMA((SEMS + 1,)), pltpu.SemaphoreType.DMA((SEMS + 1,))]


def extent(left, w):
    return tuple([4] * ("x" in left) + [4] * ("y" in left) + [2] * ("z" in left) + [16, 2 * w if "z" in left else w])


def slot(left, axis, t, off, w):
    every = slice(None)
    cols = pl.ds(off, 2 * w) if "z" in left else every
    if axis == "z":
        cols = half_of(off, w, t % 2)
    at = [every] * ("x" in left) + [every] * ("y" in left) + [every] * ("z" in left)
    lead = [a for a in "xyz" if a in left]
    at[lead.index(axis)] = t // 2 if axis == "z" else t
    return (*at, every, cols)


LANDING, LOCAL = 13, 8


def landing(n):
    one, two, three = [], [], []
    for (_, w), order in zip(parts(n), SCATTER_ORDER):
        one.append(pltpu.VMEM((3, *extent(order[1:], w)), BF16))
        two.append(pltpu.VMEM((3, *extent(order[2:], w)), BF16))
        three.append(pltpu.VMEM((3, 16, w), F32))
    sems = [pltpu.SemaphoreType.DMA((SEMS,)), pltpu.SemaphoreType.DMA((SEMS,))]
    return [pltpu.VMEM((4, 4, 2, 16, n), BF16), *one, *two, *three, pltpu.VMEM((16, n // 2), F32), *sems]


def local(n):
    two, three = [], []
    for (_, w), order in zip(parts(n), SCATTER_ORDER):
        two.append(pltpu.VMEM(extent(order[1:], w), BF16))
        three.append(pltpu.VMEM(extent(order[2:], w), F32))
    return [pltpu.VMEM((4, 4, 2, 16, n), BF16), *two, *three, pltpu.VMEM((16, n // 2), F32)]


def within(loc, n):
    wide = lambda ref, w: ref.at[(*[slice(None)] * (len(ref.shape) - 1), pl.ds(0, w))]
    widths = [2 * w if "z" in order[i:] else w for i in (1, 2) for (_, w), order in zip(parts(n), SCATTER_ORDER)]
    return [wide(ref, w) for ref, w in zip(loc, [n, *widths, n // 2])]


class Scatter:
    def __init__(self, part, out, land, loc, n):
        x, y, z, c = place()
        self.own = part.at[:, :, :, c]
        self.at, self.out, self.parts = {"x": x, "y": y, "z": z}, out, parts(n)
        along, other = peers()
        self.r0, self.r4, ss, rs = land[0], *land[10:]
        self.p1, self.p4 = loc[0], loc[7]
        self.took = [land[1:4], land[4:7], land[7:10]]
        self.held = [[self.p1] * 3, loc[1:4], loc[4:7]]
        self.local = pltpu.make_async_copy(part.at[:, :, :, c], self.p1, ss.at[0])
        self.core = remote(part.at[:, :, :, 1 - c], self.r0, ss, rs, 1, other)
        self.sends, k = [[], [], []], 2
        for i in range(3):
            for q, order in enumerate(SCATTER_ORDER):
                for d in (1, 2, 3):
                    axis = order[i]
                    src = self.held[i][q].at[self.index(q, i, (self.at[axis] + d) % 4)]
                    self.sends[i].append(remote(src, self.took[i][q].at[d - 1], ss, rs, k, along[axis][d - 1]))
                    k += 1
        self.rep = remote(self.p4, self.r4, ss, rs, k, device(x, y, z + 1 - 2 * (z % 2), c))

    def index(self, q, i, t):
        off, w = self.parts[q]
        order = SCATTER_ORDER[q]
        return slot(order[i:], order[i], t, off if i == 0 else 0, w)

    def total(self, i, to):
        for q, order in enumerate(SCATTER_ORDER):
            own = self.held[i][q].at[self.index(q, i, self.at[order[i]])]
            took = self.took[i][q]
            lead = own.shape[:-2]

            def add(j, own=own, took=took, q=q):
                value = own[j].astype(F32)
                for k in range(3):
                    value += took[(k, *j)].astype(F32)
                to(q, j, value)

            if len(lead) == 2:

                def turn(a, _, add=add, lead=lead):
                    for b in range(lead[1]):
                        add((a, b))
                    return 0

                lax.fori_loop(0, lead[0], turn, 0)
            elif len(lead) == 1:
                for a in range(lead[0]):
                    add((a,))
            else:
                add(())

    def s0(self):
        self.local.start()
        self.core.start()

    def s1(self):
        self.local.wait()
        self.core.wait()
        self.merge(self.p1)

    def s0_vmem(self):
        self.core.start()

    def s1_vmem(self):
        self.core.wait()
        self.merge(self.own)

    def merge(self, own):
        def add(i, _):
            a, b = i // 4, i % 4
            self.p1[a, b] = (own[a, b].astype(F32) + self.r0[a, b].astype(F32)).astype(BF16)
            return 0

        lax.fori_loop(0, 16, add, 0)
        for d in self.sends[0]:
            d.start()

    def stage(self, i):
        for d in self.sends[i]:
            d.wait()

        def to(q, j, value):
            ref = self.held[i + 1][q]
            ref[j] = value.astype(ref.dtype)

        self.total(i, to)
        for d in self.sends[i + 1]:
            d.start()

    def s2(self):
        self.stage(0)

    def s3(self):
        self.stage(1)

    def s4(self):
        for d in self.sends[2]:
            d.wait()

        def to(q, j, value):
            off, w = self.parts[q]
            self.p4[:, off // 2 : off // 2 + w] = value

        self.total(2, to)
        self.rep.start()

    def s5(self):
        self.rep.wait()
        k = self.at["z"] % 2
        for off, w in self.parts:
            self.out[:, half_of(off, w, k)] = self.p4[:, off // 2 : off // 2 + w]
            self.out[:, half_of(off, w, 1 - k)] = self.r4[:, off // 2 : off // 2 + w]


def run(plan, i):
    for at, steps in plan.items():

        @pl.when(i == at)
        def _():
            for step in steps:
                step()


def lay(own, at, raw, start=0, width=None):
    width = raw.shape[1] if width is None else width
    own[:15, at : at + width] = raw[:, start : start + width]


def lay_blocks(own, at, blocks, gate, up, down):
    for b in blocks:
        for raw in (gate, up, down):
            lay(own, at, raw, FB * b, FB)
            at += FB


def attend_kernel(tok_hbm, cot_hbm, cos_ref, sin_ref, gain_ref, *refs):
    raw_hbm, refs = refs[:7], refs[7:]
    xp_ref, cp_ref, nrm_ref, qt_ref, ho_ref, lt_ref, gains_ref, fa, f0, f1, tok, cot, spread, full, kx, vx, lse, bias, a, e0, e1, sem, *refs = refs
    raw, (rsem, *sems) = refs[:7], refs[7:]
    wq, wk, wv, wo, gate, up, down = raw
    loads = [pltpu.make_async_copy(h, v, rsem.at[i]) for i, (h, v) in enumerate(zip(raw_hbm, raw))]
    for d in loads:
        d.start()
    for own in (a, e0, e1):
        own[...] = jnp.zeros_like(own)
    diagonal = lax.broadcasted_iota(jnp.int32, (15, 15), 0) == lax.broadcasted_iota(jnp.int32, (15, 15), 1)
    lane = lax.broadcasted_iota(jnp.int32, (15, 128), 1)
    edge = jnp.zeros((15, 128), F32)
    for i in range(2):
        column = jnp.sum(jnp.where(diagonal, gain_ref[i : i + 1, :].astype(F32), 0.0), axis=1, keepdims=True)
        edge = jnp.where(lane == 64 + i, column, edge)
    meet()
    for d in loads[:3]:
        d.wait()
    lay(a, 0, wq)
    lay(a, 64 * K_UNIT, wk)
    a[:15, NA - 128 :] = edge.astype(BF16)
    lay(a, 64 * V_UNIT, wv)
    first = Gather(a, full, sems[0], sems[1], NA)
    c0, c1 = Gather(e0, f0, sems[2], sems[3], E0), Gather(e1, f1, sems[4], sems[5], E1)
    first.s0()
    reads = [pltpu.make_async_copy(tok_hbm, tok, sem.at[0]), pltpu.make_async_copy(cot_hbm, cot, sem.at[1])]
    for r in reads:
        r.start()
    for d in loads[3:]:
        d.wait()
    lay(e0, 0, wo)
    lay_blocks(e0, NB, [0], gate, up, down)
    lay_blocks(e1, 0, [1], gate, up, down)
    spread[...] = spread_matrix()
    row = lax.broadcasted_iota(jnp.int32, (256, 256), 0)
    col = lax.broadcasted_iota(jnp.int32, (256, 256), 1)
    bias[...] = jnp.where(col <= row, 0.0, -1e30)
    ho_ref[...] = jnp.zeros_like(ho_ref)
    lse[...] = jnp.zeros_like(lse)
    first.s1()
    c0.s0()
    for r in reads:
        r.wait()

    def widen(src, to):
        def turn(i, _):
            r = span(i, 512)
            to[r, :] = dot_tn(src[:, r], spread[...]).astype(BF16)
            return 0

        lax.fori_loop(0, 2, turn, 0)

    widen(tok, xp_ref)
    first.s2()
    c0.s1()
    c1.s0()
    widen(cot, cp_ref)
    first.s3()
    c1.s1()
    first.s4()
    c0.s2()
    keep = pltpu.make_async_copy(full, fa, sem.at[0])
    keep.start()
    a_ref = full.reshape(D, NA)
    gains_ref[...] = jnp.transpose(a_ref[:, NA - 128 :].astype(F32))[64:72, :]
    gain = gains_ref[0:1, :]

    def project(i, _):
        r = span(i, 512)
        x = xp_ref[r, :].astype(F32)
        recip = lax.rsqrt(jnp.sum(x * x, axis=1, keepdims=True) * (1.0 / WIDTH) + EPS)
        normed = (x * recip * gain).astype(BF16)
        nrm_ref[r, :] = normed
        for at in range(0, NA, 512):
            width = min(512, NA - at)
            q = dot(normed, a_ref[:, at : at + width])
            for t in range(at, at + width, 128):
                v = q[:, t - at : t - at + 128]
                if t < 64 * V_UNIT:
                    v = v * cos_ref[...] + swapped(v) * sin_ref[...]
                qt_ref[r, t : t + 128] = v.astype(BF16)
        run({1: [c1.s2]}, i)
        return 0

    lax.fori_loop(0, 2, project, 0)
    split_heads(qt_ref, kx, vx)

    def head(h, _):
        p, g = h // 2, h // 3
        u = 2 * g + h - 2 * p
        jobs = [(slice(SEQ * s + 256 * b, SEQ * s + 256 * b + 256), slice(SEQ * s, SEQ * s + 256 * b + 256)) for s in range(2) for b in range(2)]
        scores = [dot_nt(qt_ref[rows, tile(p)], kx[u, keys, :]) * (SCALE * LOG2E) for rows, keys in jobs]
        softs, stats = [], []
        for sc in scores:
            n = sc.shape[1]
            last = sc[:, n - 256 :] + bias[...]
            sc = last if n == 256 else jnp.concatenate([sc[:, : n - 256], last], axis=1)
            top = jnp.max(sc, axis=1, keepdims=True)
            ex = jnp.exp2(sc - top)
            total = jnp.sum(ex, axis=1, keepdims=True)
            softs.append((ex * (1.0 / total)).astype(BF16))
            stats.append(top + jnp.log2(total))
        outs = [dot(soft, vx[u, keys, :]) for soft, (_, keys) in zip(softs, jobs)]
        lane = lax.broadcasted_iota(jnp.int32, (256, 128), 1)
        for (rows, _), o, stat in zip(jobs, outs, stats):
            ho_ref[rows, tile(p)] = ho_ref[rows, tile(p)] + o.astype(BF16)
            lse[rows, :] = jnp.where(lane == h, stat, lse[rows, :])
        run({4: [c0.s3], 11: [c1.s3], 12: [c0.s4]}, h)
        return 0

    lax.fori_loop(0, 15, head, 0)
    lt_ref[...] = jnp.transpose(lse[...])[:16, :].reshape(16, 1, T)
    keep.wait()
    c1.s4()


def split_heads(qt_ref, kx, vx):
    low = low_half((T, 128))
    for g in range(5):
        for to, unit in ((kx, K_UNIT + g), (vx, V_UNIT + g)):
            at = 128 * (unit // 2)
            v = qt_ref[:, at : at + 128].astype(F32)
            turned = pltpu.roll(v, 64, 1)
            at_low, at_high = (v, turned) if unit % 2 == 0 else (turned, v)
            to[2 * g] = jnp.where(low, at_low, 0.0).astype(BF16)
            to[2 * g + 1] = jnp.where(low, 0.0, at_high).astype(BF16)


def attend(tok, cot, cosine, sine, gain, raw):
    shape = jax.ShapeDtypeStruct
    return pl.pallas_call(
        attend_kernel,
        out_shape=[
            shape((T, D), BF16),
            shape((T, D), BF16),
            shape((T, D), BF16),
            shape((T, NA), BF16),
            shape((T, D), BF16),
            shape((16, 1, T), F32),
            shape((8, D), F32),
            shape((4, 4, 2, 2, 16, NA), BF16),
            shape((4, 4, 2, 2, 16, E0), BF16),
            shape((4, 4, 2, 2, 16, E1), BF16),
        ],
        in_specs=[ANY] * 2 + [VMEM] * 3 + [ANY] * 7,
        out_specs=[VMEM] * 7 + [ANY] * 3,
        scratch_shapes=[
            pltpu.VMEM((WIDTH, T), BF16),
            pltpu.VMEM((WIDTH, T), BF16),
            pltpu.VMEM((WIDTH, D), BF16),
            pltpu.VMEM((4, 4, 2, 2, 16, NA), BF16),
            pltpu.VMEM((10, T, 128), BF16),
            pltpu.VMEM((10, T, 128), BF16),
            pltpu.VMEM((T, 128), F32),
            pltpu.VMEM((256, 256), F32),
            pltpu.VMEM((16, NA), BF16),
            pltpu.VMEM((16, E0), BF16),
            pltpu.VMEM((16, E1), BF16),
            pltpu.SemaphoreType.DMA((2,)),
            *[pltpu.VMEM(r.shape, BF16) for r in raw],
            pltpu.SemaphoreType.DMA((7,)),
            *gather_sems() * 3,
        ],
        compiler_params=pltpu.CompilerParams(collective_id=0, has_side_effects=True, vmem_limit_bytes=VLIM),
        name="attend",
    )(tok, cot, cosine, sine, gain, *raw)


def ffn_kernel(xp, cp, gains, ho, e0, e1, gate_hbm, up_hbm, down_hbm, hid, gheads_ref, gnorm_ref, oc_ref, outp_hbm, gl_hbm, f0, f1,
               b_full, acc, gacc, nrm, w, act, ggu, stage, own0, own1, gate, up, down, rsem, wsem, gsem, *scratch):
    loads = [pltpu.make_async_copy(h, v, rsem.at[i]) for i, (h, v) in enumerate(((gate_hbm, gate), (up_hbm, up), (down_hbm, down)))]
    for d in loads:
        d.start()
    get_b = pltpu.make_async_copy(e0.at[:, :, :, :, :, :NB], b_full, gsem)
    get_b.start()
    own0[...] = jnp.zeros_like(own0)
    own1[...] = jnp.zeros_like(own1)
    meet()
    for d in loads:
        d.wait()
    lay_blocks(own0, 0, [AHEAD], gate, up, down)
    lay_blocks(own1, 0, range(AHEAD + 1, BLOCKS), gate, up, down)
    g0, g1 = Gather(own0, f0, scratch[0], scratch[1], F0), Gather(own1, f1, scratch[2], scratch[3], F1)
    lands, loc = scratch[4 : 4 + LANDING], scratch[4 + LANDING :]
    reduction = lambda j: Scatter(stage, oc_ref.at[j], [ref.at[j] for ref in lands], loc, NC)
    gain = gains[1:2, :]

    def fetch(b, begin):
        slot = jnp.asarray(b) % 2

        for at, src in ((0, e0.at[:, :, :, :, :, NB:]), (1, e1), (2, f0), (3, f1.at[:, :, :, :, :, :NC]), (4, f1.at[:, :, :, :, :, NC:])):

            @pl.when(b == at)
            def _():
                d = pltpu.make_async_copy(src, w.at[slot], wsem.at[slot])
                d.start() if begin else d.wait()

    g0.s0()
    fetch(0, True)
    get_b.wait()
    b_ref = b_full.reshape(D, NB)

    def first(i, _):
        r = span(i, 512)
        h = xp[r, :].astype(F32) + dot_nt(ho[r, :], b_ref[...])
        hid[r, :] = h
        acc[r, :] = h
        recip = lax.rsqrt(jnp.sum(h * h, axis=1, keepdims=True) * (1.0 / WIDTH) + EPS)
        nrm[r, :] = (h * recip * gain).astype(BF16)
        gacc[r, :] = jnp.zeros((512, D), F32)
        run({0: [g0.s1, g1.s0], 1: [g0.s2]}, i)
        return 0

    lax.fori_loop(0, 2, first, 0)

    def when_chunk(b, ahead, name):
        @pl.when((b >= ahead) & (b < ahead + EARLY))
        def _():
            getattr(reduction(b - ahead), name)()

    def block(b, _):
        wv = w.at[b % 2].reshape(D, NC)
        fetch(b, False)

        when_chunk(b, 1, "s0_vmem")
        when_chunk(b, 3, "s3")
        when_chunk(b, 4, "s5")
        run({0: [g1.s1], 1: [g0.s3, g1.s2], 2: [g1.s3]}, b)

        def rows(i, _):
            r = span(i, 512)
            pre = dot(nrm[r, :], wv[:, : 2 * FB])
            ga = dot(cp[r, :], wv[:, 2 * FB :])
            gate, up = pre[:, :FB], pre[:, FB:]
            sig = 0.5 * jnp.tanh(0.5 * gate) + 0.5
            silu = gate * sig
            act_b = (silu * up).astype(BF16)
            act[r, :] = act_b
            ggu[r, :FB] = (ga * up * (sig + silu * (1.0 - sig))).astype(BF16)
            ggu[r, FB:] = (ga * silu).astype(BF16)
            acc[r, :] += dot_nt(act_b, wv[:, 2 * FB :])
            gacc[r, :] += dot_nt(ggu[r, :], wv[:, : 2 * FB])
            return 0

        lax.fori_loop(0, 2, rows, 0)
        when_chunk(b, 2, "s2")
        when_chunk(b, 1, "s1_vmem")
        when_chunk(b, 3, "s4")

        run({1: [g0.s4], 2: [g1.s4]}, b)

        @pl.when(b < BLOCKS - 1)
        def _():
            fetch(b + 1, True)

        @pl.when(b == BLOCKS - 1)
        def _():
            pltpu.make_async_copy(stage, gl_hbm.at[:, :, :, :, :, :NC], gsem).wait()

        def weights(i, _):
            r = span(i, 512)
            k = pl.ds(pl.multiple_of(2 * i, 2), 2)
            to = lambda v: v.astype(BF16).reshape(2, 4, 2, 2, 16, v.shape[1])
            stage[k, :, :, :, :, : 2 * FB] = to(dot_tn(nrm[:, r], ggu[...]))
            stage[k, :, :, :, :, 2 * FB :] = to(dot_tn(cp[:, r], act[...]))
            return 0

        lax.fori_loop(0, 2, weights, 0)

        @pl.when(b >= EARLY)
        def _():
            cols = pl.ds(pl.multiple_of(NC * jnp.maximum(b - EARLY, 0), 128), NC)
            pltpu.make_async_copy(stage, gl_hbm.at[:, :, :, :, :, cols], gsem).start()

        return 0

    lax.fori_loop(0, BLOCKS, block, 0)
    reduction(1).s5()
    reduction(2).s3()
    gnorm_ref[...] = jnp.zeros_like(gnorm_ref)
    out_stage = w.at[0].reshape(D, NC).at[:, :D]

    def last(i, _):
        r = span(i, 256)
        out_stage[r, :] = acc[r, :].astype(BF16)
        h, gn = hid[r, :], gacc[r, :]
        recip = lax.rsqrt(jnp.sum(h * h, axis=1, keepdims=True) * (1.0 / WIDTH) + EPS)
        gnorm_ref[...] += jnp.sum(gn * h * recip, axis=0, keepdims=True)
        scaled = gn * gain
        mean = jnp.sum(scaled * h, axis=1, keepdims=True) * (1.0 / WIDTH)
        gh = cp[r, :].astype(F32) + recip * scaled - h * (recip * recip * recip * mean)
        hid[r, :] = gh
        nrm[r, :] = gh.astype(BF16)
        return 0

    lax.fori_loop(0, 4, last, 0)
    reduction(2).s4()
    put_out = pltpu.make_async_copy(out_stage, outp_hbm, wsem.at[0])
    put_out.start()
    pltpu.make_async_copy(stage, gl_hbm.at[:, :, :, :, :, :NC], gsem).wait()

    def out_grad(i, _):
        r = span(i, 512)
        k = pl.ds(pl.multiple_of(2 * i, 2), 2)
        stage[k, :, :, :, :, :NB] = dot_tn(nrm[:, r], ho[...]).astype(BF16).reshape(2, 4, 2, 2, 16, NB)
        return 0

    lax.fori_loop(0, 2, out_grad, 0)
    put_gb = pltpu.make_async_copy(stage.at[:, :, :, :, :, :NB], gl_hbm.at[:, :, :, :, :, NL:], gsem)
    put_gb.start()

    def heads(i, _):
        r = span(i, 512)
        gheads_ref[r, :] = dot(nrm[r, :], b_ref[...]).astype(BF16)
        return 0

    lax.fori_loop(0, 2, heads, 0)
    reduction(2).s5()
    put_out.wait()
    put_gb.wait()


def many(shapes, k):
    vmem = lambda s: pltpu.VMEM((k, *s.shape), s.dtype)
    return [vmem(s) if i < len(shapes) - 2 else pltpu.SemaphoreType.DMA((k, SEMS)) for i, s in enumerate(shapes)]


def ffn(xp, cp, gains, ho, e0, e1, raw):
    shape = jax.ShapeDtypeStruct
    return pl.pallas_call(
        ffn_kernel,
        out_shape=[
            shape((T, D), F32),
            shape((T, D), BF16),
            shape((1, D), F32),
            shape((EARLY, 16, NC), F32),
            shape((T, D), BF16),
            shape((4, 4, 2, 2, 16, NL + NB), BF16),
            shape((4, 4, 2, 2, 16, F0), BF16),
            shape((4, 4, 2, 2, 16, F1), BF16),
        ],
        in_specs=[VMEM] * 4 + [ANY] * 5,
        out_specs=[VMEM] * 4 + [ANY] * 4,
        scratch_shapes=[
            pltpu.VMEM((4, 4, 2, 2, 16, NB), BF16),
            pltpu.VMEM((T, D), F32),
            pltpu.VMEM((T, D), F32),
            pltpu.VMEM((T, D), BF16),
            pltpu.VMEM((2, 4, 4, 2, 2, 16, NC), BF16),
            pltpu.VMEM((T, FB), BF16),
            pltpu.VMEM((T, 2 * FB), BF16),
            pltpu.VMEM((4, 4, 2, 2, 16, NC), BF16),
            pltpu.VMEM((16, F0), BF16),
            pltpu.VMEM((16, F1), BF16),
            *[pltpu.VMEM(r.shape, BF16) for r in raw],
            pltpu.SemaphoreType.DMA((3,)),
            pltpu.SemaphoreType.DMA((2,)),
            pltpu.SemaphoreType.DMA,
            *gather_sems() * 2,
            *many(landing(NC), EARLY),
            *local(NC),
        ],
        compiler_params=pltpu.CompilerParams(collective_id=1, has_side_effects=True, vmem_limit_bytes=VLIM),
        name="ffn",
    )(xp, cp, gains, ho, e0, e1, *raw)


def back_kernel(qt_ref, ho_ref, gheads_ref, lt_ref, cos_ref, sin_ref, gains, nrm, xp, gnf, early, gl, fa, gh_hbm, outp_hbm,
                oq, ok, ov, og, ou, od, oo, on, gtok_hbm, out_hbm, full, dt_ref, gsum, cols_ref, left, oa0_ref, oa1_ref, isem, osem, *scratch):
    meet()
    chunks = []
    sources = [
        (gl.at[:, :, :, :, :, :L0], left.at[:, :L0], L0),
        (gl.at[:, :, :, :, :, L0:], left.at[:, L0:], L1),
    ]
    k = LANDING + LOCAL
    for i, (src, out, n) in enumerate(sources):
        chunks.append(Scatter(src, out, scratch[k * i : k * i + LANDING], scratch[k * i + LANDING : k * i + k], n))
    c0, c1 = chunks
    loc0, loc1 = scratch[LANDING:k], scratch[k + LANDING : 2 * k]
    scratch = scratch[2 * k :]
    c0.s0()
    get_a = pltpu.make_async_copy(fa, full, isem.at[0])
    get_a.start()

    def phase_one(kx, vx, dq, dk, dv, bias):
        split_heads(qt_ref, kx, vx)
        dq[...] = jnp.zeros_like(dq)
        dk[...] = jnp.zeros_like(dk)
        dv[...] = jnp.zeros_like(dv)
        row = lax.broadcasted_iota(jnp.int32, (256, 256), 0)
        col = lax.broadcasted_iota(jnp.int32, (256, 256), 1)
        bias[...] = jnp.where(row <= col, 0.0, -1e30)

        def head(h, _):
            p, g = h // 2, h // 3
            par = h - 2 * p
            u = 2 * g + par
            lane = lax.broadcasted_iota(jnp.int32, (SEQ, 128), 1)
            own = (lane // 64) == par
            ones = jnp.ones((8, 128), BF16)
            c = SCALE * LOG2E
            for s in range(2):
                seq = slice(SEQ * s, SEQ * s + SEQ)
                q, do = qt_ref[seq, tile(p)], gheads_ref[seq, tile(p)]
                q_own = jnp.where(own, q, jnp.zeros_like(q))
                do_own = jnp.where(own, do, jnp.zeros_like(do))
                prod = do_own.astype(F32) * ho_ref[seq, tile(p)].astype(F32)
                high = prod.astype(BF16)
                rest = (prod - high.astype(F32)).astype(BF16)
                off = (dot_nt(ones, high) + dot_nt(ones, rest))[:1, :]
                lse = lt_ref[h, :, seq]
                k0, k1 = kx[u, SEQ * s : SEQ * s + 256, :], kx[u, SEQ * s + 256 : SEQ * s + 512, :]
                v0, v1 = vx[u, SEQ * s : SEQ * s + 256, :], vx[u, SEQ * s + 256 : SEQ * s + 512, :]
                st0, st1 = dot_nt(k0, q), dot_nt(k1, q[256:])
                gp0, gp1 = dot_nt(v0, do), dot_nt(v1, do[256:])
                t0 = st0 * c - lse
                e0 = jnp.exp2(jnp.concatenate([t0[:, :256] + bias[...], t0[:, 256:]], axis=1))
                e1 = jnp.exp2(st1 * c - lse[:, 256:] + bias[...])
                ds0 = (e0 * (gp0 - off)).astype(BF16)
                ds1 = (e1 * (gp1 - off[:, 256:])).astype(BF16)
                dv0, dv1 = dot(e0.astype(BF16), do_own), dot(e1.astype(BF16), do_own[256:])
                dk0, dk1 = dot(ds0, q_own), dot(ds1, q_own[256:])
                dq0 = dot_tn(ds0, k0)
                dq1 = dot_tn(ds1, k1)
                lo, hi = slice(SEQ * s, SEQ * s + 256), slice(SEQ * s + 256, SEQ * s + 512)
                dv[g, lo, :] += dv0
                dv[g, hi, :] += dv1
                dk[g, lo, :] += dk0
                dk[g, hi, :] += dk1
                dq[p, lo, :] += dq0[:256]
                dq[p, hi, :] += dq0[256:] + dq1
            run({1: [c0.s1, c1.s0], 4: [c1.s1], 8: [c0.s2], 11: [c0.s3, c1.s2], 14: [c0.s4, c1.s3]}, h)
            return 0

        lax.fori_loop(0, 15, head, 0)

        def finish(i, _):
            r = span(i, 256)
            half = span(i % 2, 256)
            cosine, sine = cos_ref[half, :], sin_ref[half, :]
            low = low_half((256, 128))
            fold = lambda ref, g: ref[g, r, :] + pltpu.roll(ref[g, r, :], 64, 1)
            pair = lambda ref, g: jnp.where(low, fold(ref, g), fold(ref, g + 1) if g < 4 else 0.0)
            for t, v in enumerate([dq[p, r, :] for p in range(8)] + [pair(dk, g) for g in (0, 2, 4)]):
                v = v * SCALE
                dt_ref[r, 128 * t : 128 * t + 128] = (v * cosine - swapped(v) * sine).astype(BF16)
            for t, g in ((11, 0), (12, 2), (13, 4)):
                dt_ref[r, 128 * t : 128 * t + 128] = pair(dv, g).astype(BF16)
            return 0

        lax.fori_loop(0, 4, finish, 0)
        c0.s5()
        c1.s4()

    pl.run_scoped(
        phase_one,
        pltpu.VMEM((10, T, 128), BF16),
        pltpu.VMEM((10, T, 128), BF16),
        pltpu.VMEM((8, T, 128), F32),
        pltpu.VMEM((5, T, 128), F32),
        pltpu.VMEM((5, T, 128), F32),
        pltpu.VMEM((256, 256), F32),
    )
    get_a.wait()
    a_ref = full.reshape(D, NA)
    gain = gains[0:1, :]
    gsum[...] = jnp.zeros_like(gsum)
    gsum[1:2, :] = gnf[...]

    def phase_two(gn_ref, gtok, out, spread, gh, outp, ga0, ga1):
        get_gh = lambda i: pltpu.make_async_copy(gh_hbm.at[span(i, 256), :], gh.at[i % 2], isem.at[i % 2])
        get_out = pltpu.make_async_copy(outp_hbm, outp, osem.at[0])
        get_gh(0).start()
        get_out.start()
        d0 = Scatter(ga0, oa0_ref, scratch[:LANDING], within(loc0, A0), A0)
        d1 = Scatter(ga1, oa1_ref, scratch[LANDING:], within(loc1, A1), A1)
        to = lambda v: v.astype(BF16).reshape(2, 4, 2, 2, 16, v.shape[1])

        def weights0(i, _):
            ga0[pl.ds(pl.multiple_of(2 * i, 2), 2)] = to(dot_tn(nrm[:, span(i, 512)], dt_ref[:, :A0]))
            return 0

        lax.fori_loop(0, 2, weights0, 0)
        d0.s0_vmem()
        c1.s5()

        def normed(i, _):
            r = span(i, 512)
            gn = dot_nt(dt_ref[r, :], a_ref[...])
            gn_ref[r, :] = gn
            x = xp[r, :].astype(F32)
            recip = lax.rsqrt(jnp.sum(x * x, axis=1, keepdims=True) * (1.0 / WIDTH) + EPS)
            gsum[0:1, :] += jnp.sum(gn * x * recip, axis=0, keepdims=True)
            run({1: [d0.s1_vmem]}, i)
            return 0

        lax.fori_loop(0, 2, normed, 0)
        cols = jnp.transpose(jnp.concatenate([gsum[...], jnp.zeros((120, D), F32)], axis=0))
        cols_ref[...] = pltpu.roll(cols, 64, 1)

        def weights1(i, _):
            r = span(i, 512)
            kk = pl.ds(pl.multiple_of(2 * i, 2), 2)
            g = dot_tn(nrm[:, r], dt_ref[:, A0:])
            edge = jnp.where(low_half((512, 128)), g[:, A1 - 128 :], cols_ref[r, :])
            ga1[kk, :, :, :, :, : A1 - 128] = to(g[:, : A1 - 128])
            ga1[kk, :, :, :, :, A1 - 128 :] = to(edge)
            return 0

        lax.fori_loop(0, 2, weights1, 0)
        d1.s0_vmem()
        spread[...] = spread_matrix()
        get_out.wait()
        d0.s2()
        d1.s1_vmem()

        def tokens(i, _):
            r = span(i, 256)
            get_gh(i).wait()

            @pl.when(i < 3)
            def _():
                get_gh(i + 1).start()

            x = xp[r, :].astype(F32)
            recip = lax.rsqrt(jnp.sum(x * x, axis=1, keepdims=True) * (1.0 / WIDTH) + EPS)
            scaled = gn_ref[r, :] * gain
            mean = jnp.sum(scaled * x, axis=1, keepdims=True) * (1.0 / WIDTH)
            gt = gh[i % 2] + recip * scaled - x * (recip * recip * recip * mean)
            high = gt.astype(BF16)
            mid = (gt - high.astype(F32)).astype(BF16)
            gtok[:, r] = dot_nt(spread[...], high) + dot_nt(spread[...], mid)
            out[:, r] = dot_nt(spread[...], outp[r, :]).astype(BF16)
            run({0: [d0.s3], 1: [d1.s2, d0.s4], 2: [d1.s3, d0.s5], 3: [d1.s4]}, i)
            return 0

        lax.fori_loop(0, 4, tokens, 0)
        puts = [pltpu.make_async_copy(gtok, gtok_hbm, osem.at[0]), pltpu.make_async_copy(out, out_hbm, osem.at[1])]
        for p in puts:
            p.start()
        at = NL
        oo[...] = left[:15, at : at + WIDTH]
        for b in range(BLOCKS):
            for i, to_ref in enumerate((og, ou, od)):
                cols = slice(FB * b, FB * b + FB)
                if b < EARLY:
                    to_ref[:, cols] = early[b, :15, FB * i : FB * i + FB]
                else:
                    at = NC * (b - EARLY) + FB * i
                    to_ref[:, cols] = left[:15, at : at + FB]
        oq[...] = oa0_ref[:15, :WIDTH]
        d1.s5()
        ok[...] = oa1_ref[:15, :320]
        ov[...] = oa1_ref[:15, 64 * V_UNIT - A0 : 64 * V_UNIT - A0 + 320]
        edge = jnp.concatenate([oa1_ref[:, A1 - 128 :], jnp.zeros((112, 128), F32)], axis=0)
        on[...] = jnp.transpose(edge)[64:72, :]
        for p in puts:
            p.wait()

    pl.run_scoped(
        phase_two,
        pltpu.VMEM((T, D), F32),
        pltpu.VMEM((WIDTH, T), F32),
        pltpu.VMEM((WIDTH, T), BF16),
        pltpu.VMEM((WIDTH, D), BF16),
        pltpu.VMEM((2, 256, D), F32),
        pltpu.VMEM((T, D), BF16),
        pltpu.VMEM((4, 4, 2, 2, 16, A0), BF16),
        pltpu.VMEM((4, 4, 2, 2, 16, A1), BF16),
    )


def back(qt, ho, gheads, lt, cosine, sine, gains, nrm, xp, gnf, early, gl, fa, gh, outp):
    shape = jax.ShapeDtypeStruct
    return pl.pallas_call(
        back_kernel,
        out_shape=[
            *[shape((15, n), F32) for n in (960, 320, 320, 2560, 2560, 2560, 960)],
            shape((8, 128), F32),
            shape((WIDTH, T), F32),
            shape((WIDTH, T), BF16),
        ],
        in_specs=[VMEM] * 11 + [ANY] * 4,
        out_specs=[VMEM] * 8 + [ANY] * 2,
        scratch_shapes=[
            pltpu.VMEM((4, 4, 2, 2, 16, NA), BF16),
            pltpu.VMEM((T, NA), BF16),
            pltpu.VMEM((8, D), F32),
            pltpu.VMEM((D, 128), F32),
            pltpu.VMEM((16, L0 + L1), F32),
            pltpu.VMEM((16, A0), F32),
            pltpu.VMEM((16, A1), F32),
            pltpu.SemaphoreType.DMA((2,)),
            pltpu.SemaphoreType.DMA((2,)),
            *landing(L0),
            *local(L0),
            *landing(L1),
            *local(L1),
            *landing(A0),
            *landing(A1),
        ],
        compiler_params=pltpu.CompilerParams(collective_id=2, has_side_effects=True, vmem_limit_bytes=VLIM),
        name="back",
    )(qt, ho, gheads, lt, cosine, sine, gains, nrm, xp, gnf, early, gl, fa, gh, outp)


def settle_kernel(*refs):
    n = len(refs) // 2
    for src, dst in zip(refs[: n - 2], refs[n:]):

        @pl.when(pl.program_id(0) == 0)
        def _():
            dst[...] = src[...]

    for src, dst in zip(refs[n - 2 : n], refs[2 * n - 2 :]):
        dst[...] = src[...]


def settle(*results):
    whole = [pl.BlockSpec(r.shape, lambda i: (0, 0)) for r in results[:-2]]
    rows = [pl.BlockSpec((WIDTH // 4, T), lambda i: (i, 0))] * 2
    return pl.pallas_call(
        settle_kernel,
        grid=(4,),
        out_shape=[jax.ShapeDtypeStruct(r.shape, r.dtype) for r in results],
        in_specs=whole + rows,
        out_specs=whole + rows,
        name="settle",
    )(*results)


def shards(tokens, cotangent, wq, wk, wv, w_gate, w_up, wo, w_down, norm_attn, norm_ffn):
    cosine, sine = rope_tables()
    gain = jnp.stack([norm_attn, norm_ffn])
    ffn_raw = (w_gate, w_up, w_down.T)
    xp, cp, nrm, qt, ho, lt, gains, fa, e0, e1 = attend(tokens.T, cotangent.T, cosine, sine, gain, (wq, wk, wv, wo.T, *ffn_raw))
    gh, gheads, gnf, early, outp, gl, _, _ = ffn(xp, cp, gains, ho, e0, e1, ffn_raw)
    results = back(qt, ho, gheads, lt, cosine, sine, gains, nrm, xp, gnf, early, gl, fa, gh, outp)
    oq, ok, ov, og, ou, od, oo, on, grad_tokens, output = settle(*results)
    return output.T, grad_tokens.T, oq, ok, ov, og, ou, oo.T, od.T, on[0, :15], on[1, :15]


def solution(mesh):
    rows = P(("replica", "shard"), None)
    first, second, one = P("shard", None), P(None, "shard"), P("shard")
    in_specs = (rows, rows, first, first, first, first, first, second, second, one, one)
    out_specs = (rows, rows, first, first, first, first, first, second, second, one, one)
    return jax.shard_map(shards, mesh=mesh, in_specs=in_specs, out_specs=out_specs, check_vma=False)
```
